32 devices in a mesh: ctx: 8 (over y, x, core), fsdp: 4 (over z).
Axes of the slice: x: 2, y: 2, z: 4, core: 2. Of those that a mesh axis runs over, the one named last changes fastest.
Arguments:
- block_input: bfloat16 [4096, 768], P(('ctx', 'fsdp')), may hold values from -6 to 6
- positions: int32 [4096], replicated, may hold values from 0 to 4095, as said below
- norm1_gain: bfloat16 [768], P('fsdp'), may hold values from 0.5 to 1.5
- norm1_bias: bfloat16 [768], P('fsdp'), may hold values from -3 to 3
- qkv_weight: bfloat16 [768, 2304], P('fsdp'), may hold values from -0.21875 to 0.21875
- query_bias: bfloat16 [768], P('fsdp'), may hold values from -3 to 3
- value_bias: bfloat16 [768], P('fsdp'), may hold values from -3 to 3
- proj_weight: bfloat16 [768, 768], P('fsdp'), may hold values from -1.75 to 1.75
- proj_bias: bfloat16 [768], P('fsdp'), may hold values from -3 to 3
- norm2_gain: bfloat16 [768], P('fsdp'), may hold values from 0.5 to 1.5
- norm2_bias: bfloat16 [768], P('fsdp'), may hold values from -3 to 3
- fc_weight: bfloat16 [768, 3072], P('fsdp'), may hold values from -0.21875 to 0.21875
- fc_bias: bfloat16 [3072], P('fsdp'), may hold values from -3 to 3
- out_weight: bfloat16 [3072, 768], P('fsdp'), may hold values from -0.109375 to 0.109375
- out_bias: bfloat16 [768], P('fsdp'), may hold values from -3 to 3
- cotangent: bfloat16 [4096, 768], P(('ctx', 'fsdp')), may hold values from -6 to 6
Outputs:
- block_output: float32 [4096, 768], P(('ctx', 'fsdp'))
- input_grad: float32 [4096, 768], P(('ctx', 'fsdp'))
- norm1_gain_grad: float32 [768], P('fsdp')
- norm1_bias_grad: float32 [768], P('fsdp')
- qkv_weight_grad: float32 [768, 2304], P('fsdp')
- query_bias_grad: float32 [768], P('fsdp')
- value_bias_grad: float32 [768], P('fsdp')
- proj_weight_grad: float32 [768, 768], P('fsdp')
- proj_bias_grad: float32 [768], P('fsdp')
- norm2_gain_grad: float32 [768], P('fsdp')
- norm2_bias_grad: float32 [768], P('fsdp')
- fc_weight_grad: float32 [768, 3072], P('fsdp')
- fc_bias_grad: float32 [3072], P('fsdp')
- out_weight_grad: float32 [3072, 768], P('fsdp')
- out_bias_grad: float32 [768], P('fsdp')
The draws below stay inside these ranges and needn't reach their ends.
Inputs may be any that keep to these rules, and one draw needn't show every extreme that they name: positions is a permutation of 0 to 4095. For every g, the entries 2 * 256 * g to 2 * 256 * (g + 1) - 1 hold the 256 positions of a sequence block b_g in increasing order, then those of block 15 - b_g in increasing order; the b_g over all g are the numbers 0 to 7 in an order drawn from the seed.
All inputs are finite; a program needn't handle non-finite values.
Results may differ from the reference program's by a relative error of at most 0.03.
Values may be sent and summed in bfloat16 or wider, within the bound.
A program may use at most 128 MiB of HBM per device.

```python
import math
import jax
import jax.numpy as jnp
from jax import lax

D = 768
HEADS = 12
HEAD = 64
FF = 3072
BLOCK = 256
LENGTH = 4096


def draw_positions(key, part):
    group_count = LENGTH // (2 * BLOCK)
    lower_blocks = jax.random.permutation(jax.random.fold_in(key, 3), group_count).astype(jnp.int32)
    offsets = jnp.arange(BLOCK, dtype=jnp.int32)
    first_block = lower_blocks[:, None] * BLOCK + offsets[None, :]
    mirror_block = (2 * group_count - 1 - lower_blocks)[:, None] * BLOCK + offsets[None, :]
    ordered = jnp.concatenate([first_block, mirror_block], axis=1)
    return ordered.reshape(LENGTH).astype(jnp.int32)


def block_levels(key, extent, split, least, high):
    loudness = 1.0
    for position, shards_of in split:
        draws = jax.random.uniform(jax.random.fold_in(jax.random.fold_in(key, 6), position), (shards_of,), jnp.float32, least / len(split), high / len(split))
        loudness = loudness * jnp.repeat(jnp.exp(draws), extent[position] // shards_of).reshape((-1,) + (1,) * (len(extent) - 1 - position))
    return loudness


def normal_values(own_key, shape, scale, reach, cuts=(), kind=jnp.bfloat16):
    entries = jax.random.normal(own_key, shape, jnp.float32) * scale
    if len(cuts) > 0:
        entries = block_levels(own_key, shape, cuts, -0.22, 0.18) * entries
    return jnp.clip(entries, min=-reach, max=reach).astype(kind)


def setup_inputs(seed: int = 0) -> dict:
    splits = jax.random.split(jax.random.key(seed), 17)
    block_input = normal_values(splits[0], (LENGTH, D), 1.0, 6.0, ((0, 32),))
    positions = draw_positions(jax.random.fold_in(splits[16], 71), 0)
    norm1_gain = jnp.clip(1.0 + 0.1 * jax.random.normal(splits[2], (D,), jnp.float32), 0.5, 1.5).astype(jnp.bfloat16)
    norm1_bias = normal_values(splits[3], (D,), 0.5, 3.0, ((0, 4),))
    qkv_weight = normal_values(splits[4], (D, 3 * D), D ** -0.5, 0.21875, ((0, 4),))
    query_bias = normal_values(splits[5], (D,), 0.5, 3.0, ((0, 4),))
    value_bias = normal_values(splits[6], (D,), 0.5, 3.0, ((0, 4),))
    proj_weight = normal_values(splits[7], (D, D), (D // 64) ** -0.5, 1.75, ((0, 4),))
    proj_bias = normal_values(splits[8], (D,), 0.5, 3.0, ((0, 4),))
    norm2_gain = jnp.clip(1.0 + 0.1 * jax.random.normal(splits[9], (D,), jnp.float32), 0.5, 1.5).astype(jnp.bfloat16)
    norm2_bias = normal_values(splits[10], (D,), 0.5, 3.0, ((0, 4),))
    fc_weight = normal_values(splits[11], (D, FF), D ** -0.5, 0.21875, ((0, 4),))
    fc_bias = normal_values(splits[12], (FF,), 0.5, 3.0, ((0, 4),))
    out_weight = normal_values(splits[13], (FF, D), FF ** -0.5, 0.109375, ((0, 4),))
    out_bias = normal_values(splits[14], (D,), 0.5, 3.0, ((0, 4),))
    cotangent = normal_values(splits[15], (LENGTH, D), 1.0, 6.0, ((0, 32),))
    return {"block_input": block_input, "positions": positions, "norm1_gain": norm1_gain, "norm1_bias": norm1_bias, "qkv_weight": qkv_weight, "query_bias": query_bias, "value_bias": value_bias, "proj_weight": proj_weight, "proj_bias": proj_bias, "norm2_gain": norm2_gain, "norm2_bias": norm2_bias, "fc_weight": fc_weight, "fc_bias": fc_bias, "out_weight": out_weight, "out_bias": out_bias, "cotangent": cotangent}


EPSILON = 1e-05
NEG_FILL = -1e+30
GELU_C = 0.7978845608028654
GELU_K = 0.044715

def layer_norm(values_in, gain, shift):
    row_mean = lax.optimization_barrier(jnp.mean(values_in, axis=-1, keepdims=True))
    centered = values_in - row_mean
    variance = lax.optimization_barrier(jnp.mean(centered * centered, axis=-1, keepdims=True))
    inv_std = lax.rsqrt(variance + EPSILON)
    normed = centered * inv_std
    return (normed * gain.astype(jnp.float32) + shift.astype(jnp.float32), normed, inv_std)

def norm_backward(grad_norm, gain, normed, inv_std):
    scaled = grad_norm * gain.astype(jnp.float32)
    scaled_mean = lax.optimization_barrier(jnp.mean(scaled, axis=-1, keepdims=True))
    cross_mean = lax.optimization_barrier(jnp.mean(scaled * normed, axis=-1, keepdims=True))
    return inv_std * (scaled - scaled_mean - normed * cross_mean)

def gelu_forward(pre_act):
    cubed = pre_act * pre_act * pre_act
    return 0.5 * pre_act * (1.0 + jnp.tanh(GELU_C * (pre_act + GELU_K * cubed)))

def gelu_slope(pre_act):
    cubed = pre_act * pre_act * pre_act
    tanh_value = jnp.tanh(GELU_C * (pre_act + GELU_K * cubed))
    return 0.5 * (1.0 + tanh_value) + 0.5 * pre_act * (1.0 - tanh_value * tanh_value) * GELU_C * (1.0 + 3.0 * GELU_K * pre_act * pre_act)

def heads_of(matrix):
    return matrix.astype(jnp.float32).reshape(matrix.shape[0], HEADS, HEAD)

def tile_scores(query_block, query_pos, key_block, key_pos):
    scores = jnp.einsum('rhd,khd->hrk', heads_of(query_block), heads_of(key_block)) * HEAD ** (-0.5)
    allowed = (key_pos[None, :] <= query_pos[:, None])[None]
    return (jnp.where(allowed, scores, NEG_FILL), allowed)

def blocked(array_in, block_span):
    return array_in.reshape((array_in.shape[0] // block_span, block_span) + array_in.shape[1:])

def attention_forward(query, keys, values, positions):
    block_span = math.gcd(LENGTH, 2048)
    query_blocks = blocked(query, block_span)
    key_blocks = blocked(keys, block_span)
    value_blocks = blocked(values, block_span)
    pos_blocks = blocked(positions, block_span)

    def per_query(block_args):
        query_block, query_pos = block_args

        def max_step(carried, key_args):
            run_max, row_total = carried
            key_block, key_pos = key_args
            scores, allowed = tile_scores(query_block, query_pos, key_block, key_pos)
            new_max = jnp.maximum(run_max, lax.optimization_barrier(jnp.max(scores, axis=-1)))
            weights = jnp.where(allowed, jnp.exp(scores - new_max[..., None]), 0.0)
            row_total = row_total * jnp.exp(run_max - new_max) + lax.optimization_barrier(jnp.sum(weights, axis=-1))
            return ((new_max, row_total), None)
        initial = (jnp.full((HEADS, block_span), NEG_FILL, jnp.float32), jnp.zeros((HEADS, block_span), jnp.float32))
        stats, unused = lax.scan(max_step, initial, (key_blocks, pos_blocks))
        row_lse = stats[0] + jnp.log(stats[1])

        def out_step(weighted, key_args):
            key_block, value_block, key_pos = key_args
            scores, allowed = tile_scores(query_block, query_pos, key_block, key_pos)
            probs = jnp.where(allowed, jnp.exp(scores - row_lse[..., None]), 0.0)
            return (weighted + jnp.einsum('hrk,khd->rhd', probs, heads_of(value_block), precision=lax.Precision.HIGHEST), None)
        weighted, unused = lax.scan(out_step, jnp.zeros((block_span, HEADS, HEAD), jnp.float32), (key_blocks, value_blocks, pos_blocks))
        return (weighted.reshape(block_span, HEADS * HEAD).astype(jnp.bfloat16), row_lse)
    attn_blocks, lse_blocks = lax.map(per_query, (query_blocks, pos_blocks))
    return (attn_blocks.reshape(LENGTH, HEADS * HEAD), lse_blocks)

def attention_backward(query, keys, values, positions, grad_attn, attn, lse_blocks):
    block_span = math.gcd(LENGTH, 2048)
    block_count = LENGTH // block_span
    scale = HEAD ** (-0.5)
    delta = lax.optimization_barrier(jnp.sum(heads_of(grad_attn) * heads_of(attn), axis=-1))
    delta_blocks = jnp.transpose(blocked(delta, block_span), (0, 2, 1))
    query_blocks = blocked(query, block_span)
    grad_blocks = blocked(grad_attn, block_span)
    key_blocks = blocked(keys, block_span)
    value_blocks = blocked(values, block_span)
    pos_blocks = blocked(positions, block_span)

    def per_key(grad_query, key_args):
        key_block, value_block, key_pos = key_args
        key_heads = heads_of(key_block)
        value_heads = heads_of(value_block)

        def per_query(key_grads, query_args):
            query_block, grad_block, lse_block, delta_block, query_pos = query_args
            scores, allowed = tile_scores(query_block, query_pos, key_block, key_pos)
            probs = jnp.where(allowed, jnp.exp(scores - lse_block[..., None]), 0.0)
            grad_heads = heads_of(grad_block)
            grad_values = jnp.einsum('hrk,rhd->khd', probs.astype(jnp.bfloat16).astype(jnp.float32), grad_heads)
            grad_probs = jnp.einsum('rhd,khd->hrk', grad_heads, value_heads)
            grad_scores = (probs * (grad_probs - delta_block[..., None])).astype(jnp.bfloat16).astype(jnp.float32)
            grad_q = jnp.einsum('hrk,khd->rhd', grad_scores, key_heads) * scale
            grad_k = jnp.einsum('hrk,rhd->khd', grad_scores, heads_of(query_block)) * scale
            return ((key_grads[0] + grad_k, key_grads[1] + grad_values), grad_q)
        initial = (jnp.zeros((block_span, HEADS, HEAD), jnp.float32), jnp.zeros((block_span, HEADS, HEAD), jnp.float32))
        key_grads, query_parts = lax.scan(per_query, initial, (query_blocks, grad_blocks, lse_blocks, delta_blocks, pos_blocks))
        return (grad_query + query_parts, key_grads)
    grad_query, key_grads = lax.scan(per_key, jnp.zeros((block_count, block_span, HEADS, HEAD), jnp.float32), (key_blocks, value_blocks, pos_blocks))
    width = HEADS * HEAD
    return (grad_query.reshape(LENGTH, width), key_grads[0].reshape(LENGTH, width), key_grads[1].reshape(LENGTH, width))

def reference(block_input, positions, norm1_gain, norm1_bias, qkv_weight, query_bias, value_bias, proj_weight, proj_bias, norm2_gain, norm2_bias, fc_weight, fc_bias, out_weight, out_bias, cotangent):
    residual = block_input.astype(jnp.float32)
    normed1_out, normed1, inv_std1 = layer_norm(residual, norm1_gain, norm1_bias)
    norm1 = normed1_out.astype(jnp.bfloat16)
    qkv = jnp.dot(norm1, qkv_weight, preferred_element_type=jnp.float32)
    query = (qkv[:, :D] + query_bias.astype(jnp.float32)).astype(jnp.bfloat16)
    keys = qkv[:, D:2 * D].astype(jnp.bfloat16)
    values = (qkv[:, 2 * D:] + value_bias.astype(jnp.float32)).astype(jnp.bfloat16)
    attn, lse_blocks = attention_forward(query, keys, values, positions)
    middle = residual + jnp.dot(attn, proj_weight, preferred_element_type=jnp.float32) + proj_bias.astype(jnp.float32)
    normed2_out, normed2, inv_std2 = layer_norm(middle, norm2_gain, norm2_bias)
    norm2 = normed2_out.astype(jnp.bfloat16)
    pre_act = jnp.dot(norm2, fc_weight, preferred_element_type=jnp.float32) + fc_bias.astype(jnp.float32)
    act = gelu_forward(pre_act).astype(jnp.bfloat16)
    block_output = middle + jnp.dot(act, out_weight, preferred_element_type=jnp.float32) + out_bias.astype(jnp.float32)
    grad_out = cotangent.astype(jnp.float32)
    out_weight_grad = jnp.dot(act.T, cotangent, preferred_element_type=jnp.float32)
    out_bias_grad = lax.optimization_barrier(jnp.sum(grad_out, axis=0))
    grad_act = jnp.dot(cotangent, out_weight.T, preferred_element_type=jnp.float32)
    grad_pre = grad_act * gelu_slope(pre_act)
    fc_bias_grad = lax.optimization_barrier(jnp.sum(grad_pre, axis=0))
    grad_pre_half = grad_pre.astype(jnp.bfloat16)
    fc_weight_grad = jnp.dot(norm2.T, grad_pre_half, preferred_element_type=jnp.float32)
    grad_norm2 = jnp.dot(grad_pre_half, fc_weight.T, preferred_element_type=jnp.float32)
    norm2_gain_grad = lax.optimization_barrier(jnp.sum(grad_norm2 * normed2, axis=0))
    norm2_bias_grad = lax.optimization_barrier(jnp.sum(grad_norm2, axis=0))
    grad_middle = grad_out + norm_backward(grad_norm2, norm2_gain, normed2, inv_std2)
    proj_bias_grad = lax.optimization_barrier(jnp.sum(grad_middle, axis=0))
    grad_middle_half = grad_middle.astype(jnp.bfloat16)
    proj_weight_grad = jnp.dot(attn.T, grad_middle_half, preferred_element_type=jnp.float32)
    grad_attn = jnp.dot(grad_middle_half, proj_weight.T, preferred_element_type=jnp.float32).astype(jnp.bfloat16)
    grad_query, grad_keys, grad_values = attention_backward(query, keys, values, positions, grad_attn, attn, lse_blocks)
    query_bias_grad = lax.optimization_barrier(jnp.sum(grad_query, axis=0))
    value_bias_grad = lax.optimization_barrier(jnp.sum(grad_values, axis=0))
    grad_qkv = jnp.concatenate([grad_query, grad_keys, grad_values], axis=1).astype(jnp.bfloat16)
    qkv_weight_grad = jnp.dot(norm1.T, grad_qkv, preferred_element_type=jnp.float32)
    grad_norm1 = jnp.dot(grad_qkv, qkv_weight.T, preferred_element_type=jnp.float32)
    norm1_gain_grad = lax.optimization_barrier(jnp.sum(grad_norm1 * normed1, axis=0))
    norm1_bias_grad = lax.optimization_barrier(jnp.sum(grad_norm1, axis=0))
    input_grad = grad_middle + norm_backward(grad_norm1, norm1_gain, normed1, inv_std1)
    return (block_output, input_grad, norm1_gain_grad, norm1_bias_grad, qkv_weight_grad, query_bias_grad, value_bias_grad, proj_weight_grad, proj_bias_grad, norm2_gain_grad, norm2_bias_grad, fc_weight_grad, fc_bias_grad, out_weight_grad, out_bias_grad)
```

```python
import functools

import jax
import jax.numpy as jnp
from jax import lax
from jax.experimental import pallas as pl
from jax.experimental.pallas import tpu as pltpu
from jax.sharding import PartitionSpec as P

HEADS = 12
HEAD = 64


EPSILON = 1e-05
NEG_FILL = -1e30
GELU_C = 0.7978845608028654
GELU_K = 0.044715


def passed_along(block, axis, distance):
    devices = range(lax.axis_size(axis))
    route = [((i - distance) % len(devices), i) for i in devices]
    return lax.ppermute(block, axis, route)


def layer_norm(values_in, gain, shift):
    row_mean = jnp.mean(values_in, axis=-1, keepdims=True)
    centered = values_in - row_mean
    variance = jnp.mean(centered * centered, axis=-1, keepdims=True)
    inv_std = lax.rsqrt(variance + EPSILON)
    normed = centered * inv_std
    return (normed * gain.astype(jnp.float32) + shift.astype(jnp.float32), normed, inv_std)


def norm_backward(grad_norm, gain, normed, inv_std):
    scaled = grad_norm * gain.astype(jnp.float32)
    scaled_mean = jnp.mean(scaled, axis=-1, keepdims=True)
    cross_mean = jnp.mean(scaled * normed, axis=-1, keepdims=True)
    return inv_std * (scaled - scaled_mean - normed * cross_mean)


def gelu_forward(pre_act):
    cubed = pre_act * pre_act * pre_act
    return 0.5 * pre_act * (1.0 + jnp.tanh(GELU_C * (pre_act + GELU_K * cubed)))


def gelu_slope(pre_act):
    cubed = pre_act * pre_act * pre_act
    tanh_value = jnp.tanh(GELU_C * (pre_act + GELU_K * cubed))
    return 0.5 * (1.0 + tanh_value) + 0.5 * pre_act * (1.0 - tanh_value * tanh_value) * GELU_C * (
        1.0 + 3.0 * GELU_K * pre_act * pre_act
    )


def rows_product(left, right):
    return lax.dot_general(
        left, right, (((0,), (0,)), ((), ())), preferred_element_type=jnp.float32
    )


def transposed_product(left, right):
    return lax.dot_general(
        left, right, (((1,), (1,)), ((), ())), preferred_element_type=jnp.float32
    )


def split_heads(matrix):
    return matrix.reshape(matrix.shape[0], HEADS, HEAD)


def masked_scores(query, query_pos, keys, key_pos):
    scores = jnp.einsum(
        "rhd,khd->hrk", split_heads(query), split_heads(keys), preferred_element_type=jnp.float32
    ) * HEAD ** (-0.5)
    allowed = (key_pos[None, :] <= query_pos[:, None])[None]
    return (jnp.where(allowed, scores, NEG_FILL), allowed)


def attend_block(carried, query, query_pos, keys, values, key_pos):
    weighted, run_max, row_total = carried
    scores, allowed = masked_scores(query, query_pos, keys, key_pos)
    new_max = jnp.maximum(run_max, jnp.max(scores, axis=-1))
    weights = jnp.where(allowed, jnp.exp(scores - new_max[..., None]), 0.0)
    factor = jnp.exp(run_max - new_max)
    row_total = row_total * factor + jnp.sum(weights, axis=-1)
    update = jnp.einsum(
        "hrk,khd->rhd",
        weights,
        split_heads(values).astype(jnp.float32),
        precision=lax.Precision.HIGHEST,
        preferred_element_type=jnp.float32,
    )
    weighted = weighted * factor.T[:, :, None] + update
    return (weighted, new_max, row_total)


def attend_tile(carried, query, query_pos, keys, values, key_pos):
    half_rows = keys.shape[0] // 2
    latest = jnp.max(query_pos)
    for half_index in range(2):
        first_row = half_index * half_rows
        part_keys = keys[first_row : first_row + half_rows]
        part_values = values[first_row : first_row + half_rows]
        part_pos = key_pos[first_row : first_row + half_rows]

        def keep_state(state_in, block_keys, block_values, block_pos):
            return state_in

        def update_state(state_in, block_keys, block_values, block_pos):
            return attend_block(state_in, query, query_pos, block_keys, block_values, block_pos)

        carried = lax.cond(
            jnp.min(part_pos) > latest,
            keep_state,
            update_state,
            carried,
            part_keys,
            part_values,
            part_pos,
        )
    return carried


def block_grads(query, grad_attn, row_lse, row_delta, query_pos, keys, values, key_pos):
    scores, allowed = masked_scores(query, query_pos, keys, key_pos)
    probs = jnp.where(allowed, jnp.exp(scores - row_lse[..., None]), 0.0)
    grad_heads = split_heads(grad_attn)
    grad_values = jnp.einsum(
        "hrk,rhd->khd", probs.astype(jnp.bfloat16), grad_heads, preferred_element_type=jnp.float32
    )
    grad_probs = jnp.einsum(
        "rhd,khd->hrk", grad_heads, split_heads(values), preferred_element_type=jnp.float32
    )
    grad_scores = (probs * (grad_probs - row_delta[..., None])).astype(jnp.bfloat16)
    scale = HEAD ** (-0.5)
    grad_query = (
        jnp.einsum(
            "hrk,khd->rhd", grad_scores, split_heads(keys), preferred_element_type=jnp.float32
        )
        * scale
    )
    grad_keys = (
        jnp.einsum(
            "hrk,rhd->khd", grad_scores, split_heads(query), preferred_element_type=jnp.float32
        )
        * scale
    )
    key_rows = keys.shape[0]
    return (grad_query, grad_keys.reshape(key_rows, -1), grad_values.reshape(key_rows, -1))


def tile_grads(query, grad_attn, row_lse, row_delta, query_pos, keys, values, key_pos):
    half_rows = keys.shape[0] // 2
    key_width = keys.shape[1]
    latest = jnp.max(query_pos)
    query_total = jnp.zeros((query.shape[0], HEADS, HEAD), jnp.float32)
    key_parts = []
    value_parts = []
    for half_index in range(2):
        first_row = half_index * half_rows
        part_keys = keys[first_row : first_row + half_rows]
        part_values = values[first_row : first_row + half_rows]
        part_pos = key_pos[first_row : first_row + half_rows]

        def skipped(block_keys, block_values, block_pos):
            return (
                jnp.zeros((query.shape[0], HEADS, HEAD), jnp.float32),
                jnp.zeros((half_rows, key_width), jnp.float32),
                jnp.zeros((half_rows, key_width), jnp.float32),
            )

        def computed(block_keys, block_values, block_pos):
            return block_grads(
                query, grad_attn, row_lse, row_delta, query_pos, block_keys, block_values, block_pos
            )

        step_query, step_keys, step_values = lax.cond(
            jnp.min(part_pos) > latest, skipped, computed, part_keys, part_values, part_pos
        )
        query_total = query_total + step_query
        key_parts.append(step_keys)
        value_parts.append(step_values)
    return (query_total, jnp.concatenate(key_parts, axis=0), jnp.concatenate(value_parts, axis=0))


def shards(
    block_input,
    positions,
    norm1_gain,
    norm1_bias,
    qkv_weight,
    query_bias,
    value_bias,
    proj_weight,
    proj_bias,
    norm2_gain,
    norm2_bias,
    fc_weight,
    fc_bias,
    out_weight,
    out_bias,
    cotangent,
):
    rows = block_input.shape[0]
    width = block_input.shape[1]
    ctx_size = lax.axis_size("ctx")
    shard_count = lax.axis_size("fsdp")
    ctx_index = lax.axis_index("ctx")
    shard_index = lax.axis_index("fsdp")
    group_rows = rows * shard_count

    def key_positions(source):
        return lax.dynamic_slice_in_dim(positions, source * group_rows, group_rows)

    gain_one, shift_one, qkv_full, qbias_full, vbias_full, proj_full, pbias_full = (
        lax.all_gather(norm1_gain, "fsdp", axis=0, tiled=True),
        lax.all_gather(norm1_bias, "fsdp", axis=0, tiled=True),
        lax.all_gather(qkv_weight, "fsdp", axis=0, tiled=True),
        lax.all_gather(query_bias, "fsdp", axis=0, tiled=True),
        lax.all_gather(value_bias, "fsdp", axis=0, tiled=True),
        lax.all_gather(proj_weight, "fsdp", axis=0, tiled=True),
        lax.all_gather(proj_bias, "fsdp", axis=0, tiled=True),
    )
    gain_two, shift_two, fc_full, fbias_full, out_full, obias_full = (
        lax.all_gather(norm2_gain, "fsdp", axis=0, tiled=True),
        lax.all_gather(norm2_bias, "fsdp", axis=0, tiled=True),
        lax.all_gather(fc_weight, "fsdp", axis=0, tiled=True),
        lax.all_gather(fc_bias, "fsdp", axis=0, tiled=True),
        lax.all_gather(out_weight, "fsdp", axis=0, tiled=True),
        lax.all_gather(out_bias, "fsdp", axis=0, tiled=True),
    )
    residual = block_input.astype(jnp.float32)
    normed1_out, normed1, inv_std1 = layer_norm(residual, gain_one, shift_one)
    norm1 = normed1_out.astype(jnp.bfloat16)
    qkv = jnp.dot(norm1, qkv_full, preferred_element_type=jnp.float32)
    query = (qkv[:, :width] + qbias_full.astype(jnp.float32)).astype(jnp.bfloat16)
    keys = qkv[:, width : 2 * width].astype(jnp.bfloat16)
    values = (qkv[:, 2 * width :] + vbias_full.astype(jnp.float32)).astype(jnp.bfloat16)
    group_keys, group_values = (
        lax.all_gather(keys, "fsdp", axis=0, tiled=True),
        lax.all_gather(values, "fsdp", axis=0, tiled=True),
    )
    own_qpos = lax.dynamic_slice_in_dim(
        positions, (ctx_index * shard_count + shard_index) * rows, rows
    )
    own_kpos = key_positions(ctx_index)
    initial = (
        jnp.zeros((rows, HEADS, HEAD), jnp.float32),
        jnp.full((HEADS, rows), NEG_FILL, jnp.float32),
        jnp.zeros((HEADS, rows), jnp.float32),
    )
    carried = attend_tile(initial, query, own_qpos, group_keys, group_values, own_kpos)

    def forward_hop(hop_index, loop_carry):
        state_now, cycle_keys, cycle_values = loop_carry
        cycle_keys, cycle_values = passed_along((cycle_keys, cycle_values), "ctx", 1)
        source = (ctx_index - hop_index) % ctx_size
        state_now = attend_tile(
            state_now, query, own_qpos, cycle_keys, cycle_values, key_positions(source)
        )
        return (state_now, cycle_keys, cycle_values)

    result = lax.fori_loop(1, ctx_size, forward_hop, (carried, group_keys, group_values))
    carried = result[0]
    weighted, run_max, row_total = carried
    attn = (weighted / row_total.T[:, :, None]).reshape(rows, width).astype(jnp.bfloat16)
    row_lse = run_max + jnp.log(row_total)
    middle = (
        residual
        + jnp.dot(attn, proj_full, preferred_element_type=jnp.float32)
        + pbias_full.astype(jnp.float32)
    )
    normed2_out, normed2, inv_std2 = layer_norm(middle, gain_two, shift_two)
    norm2 = normed2_out.astype(jnp.bfloat16)
    pre_act = jnp.dot(norm2, fc_full, preferred_element_type=jnp.float32) + fbias_full.astype(
        jnp.float32
    )
    act = gelu_forward(pre_act).astype(jnp.bfloat16)
    block_output = (
        middle
        + jnp.dot(act, out_full, preferred_element_type=jnp.float32)
        + obias_full.astype(jnp.float32)
    )
    grad_out = cotangent.astype(jnp.float32)
    out_weight_grad = rows_product(act, cotangent)
    out_bias_grad = jnp.sum(grad_out, axis=0)
    grad_act = transposed_product(cotangent, out_full)
    grad_pre = grad_act * gelu_slope(pre_act)
    fc_bias_grad = jnp.sum(grad_pre, axis=0)
    grad_pre_half = grad_pre.astype(jnp.bfloat16)
    fc_weight_grad = rows_product(norm2, grad_pre_half)
    grad_norm2 = transposed_product(grad_pre_half, fc_full)
    norm2_gain_grad = jnp.sum(grad_norm2 * normed2, axis=0)
    norm2_bias_grad = jnp.sum(grad_norm2, axis=0)
    grad_middle = grad_out + norm_backward(grad_norm2, gain_two, normed2, inv_std2)
    mlp_shares = (
        lax.psum_scatter(norm2_gain_grad, "fsdp", scatter_dimension=0, tiled=True),
        lax.psum_scatter(norm2_bias_grad, "fsdp", scatter_dimension=0, tiled=True),
        lax.psum_scatter(fc_weight_grad, "fsdp", scatter_dimension=0, tiled=True),
        lax.psum_scatter(fc_bias_grad, "fsdp", scatter_dimension=0, tiled=True),
        lax.psum_scatter(out_weight_grad, "fsdp", scatter_dimension=0, tiled=True),
        lax.psum_scatter(out_bias_grad, "fsdp", scatter_dimension=0, tiled=True),
    )
    proj_bias_grad = jnp.sum(grad_middle, axis=0)
    grad_middle_half = grad_middle.astype(jnp.bfloat16)
    proj_weight_grad = rows_product(attn, grad_middle_half)
    grad_attn = transposed_product(grad_middle_half, proj_full).astype(jnp.bfloat16)
    row_delta = jnp.sum(
        split_heads(grad_attn).astype(jnp.float32) * split_heads(attn).astype(jnp.float32), axis=-1
    ).T
    grad_query, grad_keys, grad_values = tile_grads(
        query, grad_attn, row_lse, row_delta, own_qpos, group_keys, group_values, own_kpos
    )

    def pass_key_grads(key_grads):
        return passed_along((key_grads[0], key_grads[1]), "ctx", 1)

    def backward_hop(hop_index, loop_carry):
        query_sum, key_grads, cycle_keys, cycle_values = loop_carry
        cycle_keys, cycle_values = passed_along((cycle_keys, cycle_values), "ctx", 1)
        key_grads = pass_key_grads(key_grads)
        source = (ctx_index - hop_index) % ctx_size
        step_query, step_keys, step_values = tile_grads(
            query,
            grad_attn,
            row_lse,
            row_delta,
            own_qpos,
            cycle_keys,
            cycle_values,
            key_positions(source),
        )
        return (
            query_sum + step_query,
            (key_grads[0] + step_keys, key_grads[1] + step_values),
            cycle_keys,
            cycle_values,
        )

    result = lax.fori_loop(
        1, ctx_size, backward_hop, (grad_query, (grad_keys, grad_values), group_keys, group_values)
    )
    grad_query = result[0]
    key_grads = pass_key_grads(result[1])
    own_key_grad, own_value_grad = (
        lax.psum_scatter(key_grads[0], "fsdp", scatter_dimension=0, tiled=True),
        lax.psum_scatter(key_grads[1], "fsdp", scatter_dimension=0, tiled=True),
    )
    grad_query_rows = grad_query.reshape(rows, width)
    query_bias_grad = jnp.sum(grad_query_rows, axis=0)
    value_bias_grad = jnp.sum(own_value_grad, axis=0)
    grad_qkv = jnp.concatenate([grad_query_rows, own_key_grad, own_value_grad], axis=1).astype(
        jnp.bfloat16
    )
    qkv_weight_grad = rows_product(norm1, grad_qkv)
    grad_norm1 = transposed_product(grad_qkv, qkv_full)
    norm1_gain_grad = jnp.sum(grad_norm1 * normed1, axis=0)
    norm1_bias_grad = jnp.sum(grad_norm1, axis=0)
    input_grad = grad_middle + norm_backward(grad_norm1, gain_one, normed1, inv_std1)
    attn_shares = (
        lax.psum_scatter(norm1_gain_grad, "fsdp", scatter_dimension=0, tiled=True),
        lax.psum_scatter(norm1_bias_grad, "fsdp", scatter_dimension=0, tiled=True),
        lax.psum_scatter(qkv_weight_grad, "fsdp", scatter_dimension=0, tiled=True),
        lax.psum_scatter(query_bias_grad, "fsdp", scatter_dimension=0, tiled=True),
        lax.psum_scatter(value_bias_grad, "fsdp", scatter_dimension=0, tiled=True),
        lax.psum_scatter(proj_weight_grad, "fsdp", scatter_dimension=0, tiled=True),
        lax.psum_scatter(proj_bias_grad, "fsdp", scatter_dimension=0, tiled=True),
    )
    totals = lax.psum(
        (
            attn_shares[0],
            attn_shares[1],
            attn_shares[2],
            attn_shares[3],
            attn_shares[4],
            attn_shares[5],
            attn_shares[6],
            mlp_shares[0],
            mlp_shares[1],
            mlp_shares[2],
            mlp_shares[3],
            mlp_shares[4],
            mlp_shares[5],
        ),
        "ctx",
    )
    return (
        block_output,
        input_grad,
        totals[0],
        totals[1],
        totals[2],
        totals[3],
        totals[4],
        totals[5],
        totals[6],
        totals[7],
        totals[8],
        totals[9],
        totals[10],
        totals[11],
        totals[12],
    )


MESH = pl.DeviceIdType.MESH
SMEM = pltpu.SMEM
VMEM = pltpu.VMEM
F32 = jnp.float32
B16 = jnp.bfloat16


class Transfer:
    def __init__(self, links, src, dst, device):
        self.args = dict(
            src_ref=src,
            dst_ref=dst,
            send_sem=links.send_sem.at[links.count],
            recv_sem=links.recv_sem.at[links.count],
            device_id=device,
            device_id_type=MESH,
        )
        links.count += 1
        links.sent.append(self)

    def start(self):
        pltpu.make_async_remote_copy(**self.args).start()
        return self

    def arrived(self):
        pltpu.make_async_remote_copy(**self.args).wait_recv()

    def left(self):
        pltpu.make_async_remote_copy(**self.args).wait_send()


class Links:
    def __init__(self, send_sem, recv_sem):
        self.send_sem, self.recv_sem = send_sem, recv_sem
        self.count = 0
        self.sent = []
        ctx = lax.axis_index("ctx")
        self.ctx = ctx
        self.z = lax.axis_index("fsdp")
        self.core = lax.rem(ctx, 2)
        self.chip = lax.div(ctx, 2)
        x, y = lax.rem(self.chip, 2), lax.div(self.chip, 2)
        self.chip_x = self.chip + 1 - 2 * x
        self.chip_y = self.chip + 2 - 4 * y
        self.chip_d = 3 - self.chip
        self.other = 1 - self.core
        self.to_core = {"ctx": self.chip * 2 + self.other}
        self.to_x = {"ctx": self.chip_x * 2 + self.core}
        self.to_y = {"ctx": self.chip_y * 2 + self.core}

    def zed(self, step):
        return lax.rem(self.z + step, 4)

    def to_z(self, step):
        return {"fsdp": self.zed(step)}

    def peers(self):
        return [self.to_core, self.to_x, self.to_y, self.to_z(1), self.to_z(2), self.to_z(3)]

    def copy(self, src, dst, device):
        return Transfer(self, src, dst, device)

    def greet(self):
        barrier = pltpu.get_barrier_semaphore()
        for device in self.peers():
            pl.semaphore_signal(barrier, inc=1, device_id=device, device_id_type=MESH)

    def greeted(self):
        pl.semaphore_wait(pltpu.get_barrier_semaphore(), 6)

    def drain(self):
        for transfer in self.sent:
            transfer.left()


class RingGather:
    def __init__(self, links, buf):
        half = buf.shape[1] // 2
        own, left, right = links.z, links.zed(3), links.zed(1)

        def piece(member, part):
            return buf.at[member, part * half : (part + 1) * half]

        def move(member, part, step):
            return links.copy(piece(member, part), piece(member, part), links.to_z(step))

        self.first = [move(own, 0, 1), move(own, 1, 3), move(own, 1, 1), move(own, 0, 3)]
        self.second = [move(left, 0, 1), move(right, 1, 3)]

    def start(self):
        for transfer in self.first:
            transfer.start()

    def forward(self):
        for transfer, onward in zip(self.first[:2], self.second):
            transfer.arrived()
            onward.start()

    def near(self):
        for transfer in self.first[2:]:
            transfer.arrived()

    def far(self):
        for transfer in self.second:
            transfer.arrived()


class Shared:
    def __init__(self, links, source, target):
        half = target.shape[1] // 2
        rows = pl.ds(pl.multiple_of(links.core * half, half), half)
        self.cross = [
            links.copy(source(links.zed(step), rows), target.at[links.z, rows], links.to_z(step))
            for step in (1, 3, 2)
        ]
        self.hand = [
            links.copy(
                target.at[links.zed(4 - step), rows],
                target.at[links.zed(4 - step), rows],
                links.to_core,
            )
            for step in (1, 3, 2)
        ]

    def start(self):
        for transfer in self.cross:
            transfer.start()

    def forward(self):
        for transfer, onward in zip(self.cross, self.hand):
            transfer.arrived()
            onward.start()

    def finish(self):
        for transfer in self.hand:
            transfer.arrived()


class ContextGather:
    def __init__(self, links, buf):
        half = buf.shape[2] // 2

        def move(chip, part, device):
            rows = slice(None) if part is None else slice(part * half, (part + 1) * half)
            ref = buf.at[links.core, chip, rows]
            return links.copy(ref, ref, device)

        own, x, y, d = links.chip, links.chip_x, links.chip_y, links.chip_d
        self.own_core = move(own, None, links.to_core)
        self.x_parts = [move(own, 0, links.to_x), move(own, 1, links.to_x)]
        self.y_parts = [move(own, 1, links.to_y), move(own, 0, links.to_y)]
        self.onward = [move(x, 0, links.to_y), move(y, 1, links.to_x)]
        self.x_core = move(x, None, links.to_core)
        self.y_core = move(y, None, links.to_core)
        self.d_core = move(d, None, links.to_core)

    def start(self):
        for transfer in (
            self.x_parts[0],
            self.y_parts[0],
            self.own_core,
            self.x_parts[1],
            self.y_parts[1],
        ):
            transfer.start()

    def forward(self):
        self.x_parts[0].arrived()
        self.onward[0].start()
        self.y_parts[0].arrived()
        self.onward[1].start()

    def hand_near(self):
        self.x_parts[1].arrived()
        self.x_core.start()
        self.y_parts[1].arrived()
        self.y_core.start()

    def hand_far(self):
        self.onward[0].arrived()
        self.onward[1].arrived()
        self.d_core.start()


def chosen(flag, shape):
    return jnp.full(shape, flag, jnp.int32) == 1


def masked_heads(value, first, width):
    rows, span = value.shape
    pieces = []
    if first > 0:
        pieces.append(jnp.zeros((rows, first), value.dtype))
    pieces.append(value)
    if first + span < width:
        pieces.append(jnp.zeros((rows, width - first - span), value.dtype))
    wide = jnp.concatenate(pieces, axis=1) if len(pieces) > 1 else value
    head = (lax.broadcasted_iota(jnp.int32, (rows, width), 1) - first + HEAD) // HEAD - 1
    return [
        jnp.where(head == index, wide.astype(F32), 0.0).astype(value.dtype)
        for index in range(span // HEAD)
    ]


def soft_step(scores, old_max, old_sum):
    new_max = jnp.maximum(old_max, jnp.max(scores, axis=0, keepdims=True))
    weights = jnp.exp(scores - new_max)
    factor = jnp.exp(old_max - new_max)
    new_sum = old_sum * factor + jnp.sum(weights, axis=0, keepdims=True)
    return weights.astype(B16), factor, new_max, new_sum


def forward_phase(
    links, ids, x, cot, qkvw, fcw, projw, vec, qvbias,
    attn_t, lse, qm, kv, x_all, w_all, cot_all, fc_all, proj_all, vec_all, norm1,
    stage, fcs, max_h, sum_h, acc_h, max_x, sum_x, acc_x,
):
    rows = x.shape[0]
    span = qkvw.shape[0]
    block = 2 * rows
    heads = span // HEAD
    z = links.z
    links.greet()
    x_all[z] = x[...]
    cot_all[z] = cot[...]
    proj_all[z] = projw[...]
    vec_all[z] = vec[...]
    for member in range(4):
        stage[member, :, : 3 * span] = jnp.concatenate(
            [qkvw[:, t * 4 * span + member * span : t * 4 * span + (member + 1) * span] for t in range(3)],
            axis=1,
        )
        fcs[member] = fcw[:, member * 4 * span : (member + 1) * 4 * span]
    w_all[z] = stage[z]
    fc_all[z] = fcs[z]

    vectors = [
        links.copy(vec_all.at[z], vec_all.at[z], links.to_z(step)) for step in (1, 3, 2)
    ]
    inputs = RingGather(links, x_all)
    weights = Shared(links, lambda member, part: stage.at[member, part], w_all)
    cots = RingGather(links, cot_all)
    fcs_in = Shared(links, lambda member, part: fcs.at[member, part], fc_all)
    projs = Shared(links, lambda member, part: proj_all.at[z, part], proj_all)
    context = ContextGather(links, kv)

    links.greeted()
    for transfer in vectors:
        transfer.start()
    inputs.start()
    weights.start()
    for transfer in vectors:
        transfer.arrived()

    gain = jnp.concatenate([vec_all[m, 0:1, :span] for m in range(4)], axis=1).astype(F32)
    shift = jnp.concatenate([vec_all[m, 1:2, :span] for m in range(4)], axis=1).astype(F32)

    def normalise(member):
        normed = layer_norm(x_all[member].astype(F32), gain, shift)[0]
        first = pl.multiple_of(member * rows, rows)
        norm1[pl.ds(first, rows), :] = normed.astype(B16)

    normalise(z)
    inputs.forward()
    inputs.near()
    normalise(links.zed(1))
    normalise(links.zed(3))
    weights.forward()
    inputs.far()
    normalise(links.zed(2))
    weights.finish()
    cots.start()
    fcs_in.start()
    projs.start()

    matrix = w_all[...].reshape(4 * span, w_all.shape[2])[:, : 3 * span]
    for part in range(2):
        at = slice(part * block, (part + 1) * block)
        product = jnp.dot(norm1[at, :], matrix, preferred_element_type=F32)
        query = (product[:, :span] + qvbias[0:1, :].astype(F32)).astype(B16)
        query = query * jnp.asarray(HEAD**-0.5, B16)
        for head, lone in enumerate(masked_heads(query, 0, 4 * HEAD)):
            qm[head, at, :] = lone
        values = product[:, 2 * span :] + qvbias[1:2, :].astype(F32)
        kv[links.core, links.chip, at, :] = jnp.concatenate(
            [product[:, span : 2 * span], values], axis=1
        ).astype(B16)
    context.start()

    own_block = ids[2 * links.ctx]
    keep = lax.broadcasted_iota(jnp.int32, (block, block), 0) <= lax.broadcasted_iota(
        jnp.int32, (block, block), 1
    )
    none = jnp.full((1, block), NEG_FILL, F32)
    zero = jnp.zeros((1, block), F32)

    def halves(core, chip, part):
        at = slice(part * block, (part + 1) * block)
        return kv[core, chip, at, : 4 * HEAD], kv[core, chip, at, 2 * HEAD :].T

    def value_rows(head):
        return slice((1 + head) * HEAD, (2 + head) * HEAD)

    def head_rows(head):
        return slice(head * HEAD, (head + 1) * HEAD)

    k_low, vt_low = halves(links.core, links.chip, 0)
    k_high, vt_high = halves(links.core, links.chip, 1)
    for head in range(heads):
        q_low, q_high = qm[head, :block, :], qm[head, block:, :]
        scores = jnp.where(keep, transposed_product(k_low, q_low), NEG_FILL)
        w, _, top, total = soft_step(scores, none, zero)
        max_x[0, head : head + 1, :] = top
        sum_x[0, head : head + 1, :] = total
        acc_x[0, head_rows(head), :] = jnp.dot(
            vt_low[value_rows(head)], w, preferred_element_type=F32
        )
        scores = transposed_product(k_low, q_high)
        w, _, top, total = soft_step(scores, none, zero)
        acc = jnp.dot(vt_low[value_rows(head)], w, preferred_element_type=F32)
        scores = jnp.where(keep, transposed_product(k_high, q_high), NEG_FILL)
        w, factor, top, total = soft_step(scores, top, total)
        max_h[head : head + 1, :] = top
        sum_h[head : head + 1, :] = total
        acc_h[head_rows(head), :] = acc * factor + jnp.dot(
            vt_high[value_rows(head)], w, preferred_element_type=F32
        )
    max_x[1] = jnp.full_like(max_h, NEG_FILL)
    sum_x[1] = jnp.zeros_like(sum_h)
    acc_x[1] = jnp.zeros_like(acc_h)

    def hop(index, carry):
        near = index < 3
        far = index >= 5
        core = jnp.where((index == 1) | (index == 2) | (index == 5), links.core, links.other)
        chip = jnp.where(
            index == 0,
            links.chip,
            jnp.where(far, links.chip_d, jnp.where(lax.rem(index, 2) == 1, links.chip_x, links.chip_y)),
        )

        @pl.when(index == 0)
        def _():
            context.own_core.arrived()
            context.forward()

        @pl.when(index == 1)
        def _():
            context.hand_near()
            cots.forward()
            cots.near()

        @pl.when(index == 3)
        def _():
            context.x_core.arrived()
            context.hand_far()
            fcs_in.forward()

        @pl.when(index == 4)
        def _():
            context.y_core.arrived()
            cots.far()

        @pl.when(index == 6)
        def _():
            context.d_core.arrived()

        block_id = ids[2 * (2 * chip + core)]
        low = (block_id < own_block).astype(jnp.int32)
        in_low = chosen(low, (1, block))
        kv_low = kv[core, chip, :block, :]
        kv_high = kv[core, chip, block:, :]
        kv_pick = jnp.where(chosen(low, kv_low.shape), kv_low, kv_high)
        q_mask = chosen(low, (block, 4 * HEAD))
        work = []
        for head in range(heads):
            scores = transposed_product(kv_low[:, : 4 * HEAD], qm[head, block:, :])
            work.append((scores, max_h[head : head + 1, :], sum_h[head : head + 1, :]))
        for head in range(heads):
            q_pick = jnp.where(q_mask, qm[head, :block, :], qm[head, block:, :])
            scores = transposed_product(kv_pick[:, : 4 * HEAD], q_pick)
            at = slice(head, head + 1)
            work.append(
                (
                    scores,
                    jnp.where(in_low, max_x[0, at, :], max_x[1, at, :]),
                    jnp.where(in_low, sum_x[0, at, :], sum_x[1, at, :]),
                )
            )
        done = [soft_step(*entry) for entry in work]
        vt = kv_low[:, 2 * HEAD :].T
        for head in range(heads):
            w, factor, top, total = done[head]
            max_h[head : head + 1, :] = top
            sum_h[head : head + 1, :] = total
            acc_h[head_rows(head), :] = acc_h[head_rows(head), :] * factor + jnp.dot(
                vt[value_rows(head)], w, preferred_element_type=F32
            )
        vt = kv_pick[:, 2 * HEAD :].T
        for head in range(heads):
            w, factor, top, total = done[heads + head]
            acc = jnp.where(in_low, acc_x[0, head_rows(head), :], acc_x[1, head_rows(head), :])
            acc = acc * factor + jnp.dot(
                vt[value_rows(head)], w, preferred_element_type=F32
            )
            for part in range(2):
                own = in_low if part == 0 else ~in_low
                max_x[part, head : head + 1, :] = jnp.where(own, top, max_x[part, head : head + 1, :])
                sum_x[part, head : head + 1, :] = jnp.where(
                    own, total, sum_x[part, head : head + 1, :]
                )
                acc_x[part, head_rows(head), :] = jnp.where(own, acc, acc_x[part, head_rows(head), :])
        return carry

    lax.fori_loop(0, 7, hop, 0)
    projs.forward()
    for head in range(heads):
        at = slice(head, head + 1)
        total = sum_x[0, at, :]
        attn_t[head_rows(head), :block] = (acc_x[0, head_rows(head), :] / total).astype(B16)
        lse[at, :block] = max_x[0, at, :] + jnp.log(total)
        top = jnp.maximum(max_h[at, :], max_x[1, at, :])
        left, right = jnp.exp(max_h[at, :] - top), jnp.exp(max_x[1, at, :] - top)
        total = sum_h[at, :] * left + sum_x[1, at, :] * right
        acc = acc_h[head_rows(head), :] * left + acc_x[1, head_rows(head), :] * right
        attn_t[head_rows(head), block:] = (acc / total).astype(B16)
        lse[at, block:] = top + jnp.log(total)
    fcs_in.finish()
    projs.finish()


def forward_kernel(*refs):
    send_sem, recv_sem = refs[-2:]
    links = Links(send_sem, recv_sem)
    forward_phase(links, *refs[:-2])
    links.drain()


def forward_call(ids, x, cot, qkvw, fcw, projw, vec, qvbias):
    rows, width = x.shape
    span = qkvw.shape[0]
    hidden = fcw.shape[1] // 4
    group = 4 * rows

    def shape(dims, dtype=B16):
        return jax.ShapeDtypeStruct(dims, dtype)

    outs = (
        shape((span, group)),
        shape((8, group), F32),
        shape((span // HEAD, group, 4 * HEAD)),
        shape((2, 4, group, 2 * span)),
        shape((4, rows, width)),
        shape((4, span, 640)),
        shape((4, rows, width)),
        shape((4, span, hidden)),
        shape((4, span, width)),
        shape((4,) + vec.shape),
        shape((group, width)),
    )
    return pl.pallas_call(
        forward_kernel,
        out_shape=outs,
        in_specs=[pl.BlockSpec(memory_space=SMEM)] + [pl.BlockSpec(memory_space=VMEM)] * 7,
        out_specs=(pl.BlockSpec(memory_space=VMEM),) * len(outs),
        scratch_shapes=[
            VMEM((4, span, 640), B16),
            VMEM((4, span, hidden), B16),
            VMEM((8, group // 2), F32),
            VMEM((8, group // 2), F32),
            VMEM((span, group // 2), F32),
            VMEM((2, 8, group // 2), F32),
            VMEM((2, 8, group // 2), F32),
            VMEM((2, span, group // 2), F32),
            pltpu.SemaphoreType.DMA((48,)),
            pltpu.SemaphoreType.DMA((48,)),
        ],
        compiler_params=pltpu.CompilerParams(
            collective_id=0, has_side_effects=True, vmem_limit_bytes=56 << 20
        ),
        name="forward",
    )(ids, x, cot, qkvw, fcw, projw, vec, qvbias)


def head_cols(head, offset=0):
    return slice(offset + head * HEAD, offset + (head + 1) * HEAD)


def tile_keep(block, key_block, query_block):
    key_row = lax.broadcasted_iota(jnp.int32, (block, block), 0)
    query_col = lax.broadcasted_iota(jnp.int32, (block, block), 1)
    return key_row <= query_col + jnp.where(key_block == query_block, 0, block)


def old_forward_kernel(
    heads, block, ids_ref, own_ref, q_ref, kv_ref, out_ref, lse_ref, max_ref, sum_ref, acc_ref
):
    span = heads * HEAD
    max_ref[...] = jnp.full_like(max_ref, NEG_FILL)
    sum_ref[...] = jnp.zeros_like(sum_ref)
    acc_ref[...] = jnp.zeros_like(acc_ref)

    def step(index, carry):
        first = pl.multiple_of(index * block, block)
        key_block = ids_ref[index]
        for part in range(2):
            cols = slice(part * block, (part + 1) * block)
            query_block = own_ref[part]

            @pl.when(key_block <= query_block)
            def _():
                keep = tile_keep(block, key_block, query_block)
                for head in range(heads):
                    k = kv_ref[pl.ds(first, block), head_cols(head)]
                    v = kv_ref[pl.ds(first, block), head_cols(head, span)]
                    q = q_ref[cols, head_cols(head)]
                    scores = jnp.where(keep, transposed_product(k, q), NEG_FILL)
                    old_max = max_ref[head : head + 1, cols]
                    new_max = jnp.maximum(old_max, jnp.max(scores, axis=0, keepdims=True))
                    weights = jnp.exp(scores - new_max)
                    factor = jnp.exp(old_max - new_max)
                    max_ref[head : head + 1, cols] = new_max
                    sum_ref[head : head + 1, cols] = sum_ref[
                        head : head + 1, cols
                    ] * factor + jnp.sum(weights, axis=0, keepdims=True)
                    acc_ref[head_cols(head), cols] = acc_ref[
                        head_cols(head), cols
                    ] * factor + rows_product(v, weights.astype(jnp.bfloat16))

        return carry

    lax.fori_loop(0, kv_ref.shape[0] // block, step, 0)
    for head in range(heads):
        total = sum_ref[head : head + 1, :]
        out_ref[head_cols(head), :] = (acc_ref[head_cols(head), :] / total).astype(out_ref.dtype)
        lse_ref[head : head + 1, :] = max_ref[head : head + 1, :] + jnp.log(total)


def backward_kernel(
    heads, block, ids_ref, own_ref, q_ref, kv_ref, do_ref, lse_ref, delta_ref, dq_ref, dkv_ref, acc_ref
):
    span = heads * HEAD
    dq_ref[...] = jnp.zeros_like(dq_ref)

    def step(index, carry):
        first = pl.multiple_of(index * block, block)
        key_block = ids_ref[index]
        acc_ref[...] = jnp.zeros_like(acc_ref)
        for part in range(2):
            cols = slice(part * block, (part + 1) * block)
            query_block = own_ref[part]

            @pl.when(key_block <= query_block)
            def _():
                keep = tile_keep(block, key_block, query_block)
                key_parts = []
                value_parts = []
                for head in range(heads):
                    k = kv_ref[pl.ds(first, block), head_cols(head)]
                    v = kv_ref[pl.ds(first, block), head_cols(head, span)]
                    q = q_ref[cols, head_cols(head)]
                    do = do_ref[cols, head_cols(head)]
                    scores = jnp.where(keep, transposed_product(k, q), NEG_FILL)
                    probs = jnp.exp(scores - lse_ref[head : head + 1, cols])
                    value_parts.append(
                        jnp.dot(
                            probs.astype(jnp.bfloat16), do, preferred_element_type=jnp.float32
                        )
                    )
                    grad_probs = transposed_product(v, do)
                    grad_scores = (
                        probs * (grad_probs - delta_ref[head : head + 1, cols])
                    ).astype(jnp.bfloat16)
                    key_parts.append(
                        jnp.dot(grad_scores, q, preferred_element_type=jnp.float32)
                    )
                    dq_ref[head_cols(head), cols] += rows_product(k, grad_scores)
                acc_ref[...] += jnp.concatenate(key_parts + value_parts, axis=1)

        dkv_ref[pl.ds(first, block), :] = acc_ref[...].astype(dkv_ref.dtype)
        return carry

    lax.fori_loop(0, kv_ref.shape[0] // block, step, 0)


def attention_forward(heads, block, ids, own, q, kv):
    group_rows, span = q.shape
    return pl.pallas_call(
        functools.partial(old_forward_kernel, heads, block),
        out_shape=(
            jax.ShapeDtypeStruct((span, group_rows), jnp.bfloat16),
            jax.ShapeDtypeStruct((heads, group_rows), jnp.float32),
        ),
        in_specs=[pl.BlockSpec(memory_space=SMEM)] * 2 + [pl.BlockSpec(memory_space=VMEM)] * 2,
        out_specs=(pl.BlockSpec(memory_space=VMEM),) * 2,
        scratch_shapes=[
            VMEM((heads, group_rows), jnp.float32),
            VMEM((heads, group_rows), jnp.float32),
            VMEM((span, group_rows), jnp.float32),
        ],
        cost_estimate=pl.CostEstimate(
            flops=2 * group_rows * kv.shape[0] * span,
            bytes_accessed=2 * kv.size,
            transcendentals=group_rows * kv.shape[0] * heads // 2,
        ),
        name="attention_forward",
    )(ids, own, q, kv)


def attention_backward(heads, block, ids, own, q, kv, do, lse, delta):
    group_rows, span = q.shape
    return pl.pallas_call(
        functools.partial(backward_kernel, heads, block),
        out_shape=(
            jax.ShapeDtypeStruct((span, group_rows), jnp.float32),
            jax.ShapeDtypeStruct(kv.shape, jnp.bfloat16),
        ),
        in_specs=[pl.BlockSpec(memory_space=SMEM)] * 2 + [pl.BlockSpec(memory_space=VMEM)] * 5,
        out_specs=(pl.BlockSpec(memory_space=VMEM),) * 2,
        scratch_shapes=[VMEM((block, 2 * span), jnp.float32)],
        cost_estimate=pl.CostEstimate(
            flops=5 * group_rows * kv.shape[0] * span,
            bytes_accessed=4 * kv.size,
            transcendentals=group_rows * kv.shape[0] * heads // 2,
        ),
        name="attention_backward",
    )(ids, own, q, kv, do, lse, delta)


def head_shards(
    block_input,
    positions,
    norm1_gain,
    norm1_bias,
    qkv_weight,
    query_bias,
    value_bias,
    proj_weight,
    proj_bias,
    norm2_gain,
    norm2_bias,
    fc_weight,
    fc_bias,
    out_weight,
    out_bias,
    cotangent,
):
    rows, width = block_input.shape
    ctx_size = lax.axis_size("ctx")
    members = lax.axis_size("fsdp")
    ctx_index = lax.axis_index("ctx")
    member = lax.axis_index("fsdp")
    group_rows = rows * members
    block = group_rows // 2
    span = width // members
    heads = HEADS // members
    hidden = fc_weight.shape[1] // members
    piece = span // ctx_size
    f32, b16 = jnp.float32, jnp.bfloat16

    def gathered(value, axis=0):
        return lax.all_gather(value, "fsdp", axis=axis, tiled=True)

    def scattered(value):
        return lax.psum_scatter(value, "fsdp", scatter_dimension=0, tiled=True)

    def exchanged(value):
        return lax.all_to_all(value, "fsdp", 0, 0, tiled=True)

    def own_rows(value):
        return lax.dynamic_slice_in_dim(value, member * rows, rows)

    vec = jnp.stack([norm1_gain, norm1_bias, proj_bias, norm2_gain, norm2_bias, out_bias])
    vec = jnp.pad(vec, ((0, 10), (0, 256 - span)))
    ids = positions.reshape(2 * ctx_size, block)[:, 0] // block
    own_ids = lax.dynamic_slice_in_dim(ids, 2 * ctx_index, 2)
    attn_t, lse, qm, kv_all, x_all, w_all, cot_all, fc_all, proj_all, vec_all, norm1 = forward_call(
        ids, block_input, cotangent, qkv_weight, fc_weight, proj_weight, vec, jnp.stack([query_bias, value_bias])
    )
    lse = lse[:heads]
    query = qm[0, :, :span] + qm[1, :, :span] + qm[2, :, :span]
    all_kv = kv_all.transpose(1, 0, 2, 3).reshape(-1, 2 * span)
    residual = x_all.reshape(group_rows, width).astype(f32)
    qkv_cols = w_all[:, :, : 3 * span].reshape(width, 3 * span)
    cotangent_all = cot_all.reshape(group_rows, width)
    fc_cols = fc_all.reshape(width, hidden)
    proj_full = proj_all.reshape(width, width)
    vectors = vec_all[:, :6, :span].transpose(1, 0, 2).reshape(6, width)
    gain_one, shift_one, pbias, gain_two, shift_two, obias = (vectors[i] for i in range(6))
    attn_all_t = gathered(attn_t)
    middle_all = residual + rows_product(attn_all_t, proj_full) + pbias.astype(f32)
    norm2 = layer_norm(middle_all, gain_two, shift_two)[0].astype(b16)
    pre_act = jnp.dot(norm2, fc_cols, preferred_element_type=f32) + fc_bias.astype(f32)
    act = gelu_forward(pre_act).astype(b16)
    grad_act = transposed_product(cotangent_all, out_weight)
    grad_pre = grad_act * gelu_slope(pre_act)
    fc_bias_grad = jnp.sum(grad_pre, axis=0)
    grad_pre_half = grad_pre.astype(b16)
    grad_norm2 = scattered(transposed_product(grad_pre_half, fc_cols).astype(b16)).astype(f32)
    middle = own_rows(middle_all)
    _, normed2, inv_std2 = layer_norm(middle, gain_two, shift_two)
    grad_out = cotangent.astype(f32)
    grad_middle = grad_out + norm_backward(grad_norm2, gain_two, normed2, inv_std2)
    grad_middle_all = gathered(grad_middle.astype(b16))

    mlp_out = scattered(jnp.dot(act, out_weight, preferred_element_type=f32).astype(b16))
    block_output = middle + mlp_out.astype(f32) + obias.astype(f32)

    grad_attn = transposed_product(grad_middle_all, proj_weight).astype(b16)
    delta = jnp.sum(
        (grad_attn.T.astype(f32) * attn_t.astype(f32)).reshape(heads, HEAD, group_rows), axis=1
    )
    grad_query_t, grad_kv = attention_backward(
        heads, block, ids, own_ids, query, all_kv, grad_attn, lse, delta
    )
    own_kv = lax.psum_scatter(grad_kv, "ctx", scatter_dimension=0, tiled=True)

    out_weight_grad = rows_product(act, cotangent_all).astype(b16)
    fc_weight_grad = rows_product(norm2, grad_pre_half).astype(b16)
    proj_weight_grad = jnp.dot(attn_t, grad_middle_all, preferred_element_type=f32).astype(b16)
    shares = jnp.concatenate(
        [
            out_weight_grad.reshape(ctx_size, -1, width),
            proj_weight_grad.reshape(ctx_size, piece, width),
            fc_weight_grad.reshape(members, ctx_size, piece, hidden)
            .transpose(1, 0, 2, 3)
            .reshape(ctx_size, members * piece, hidden),
        ],
        axis=1,
    )
    shares = lax.psum_scatter(shares, "ctx", scatter_dimension=0, tiled=True)[0]
    kept = shares.shape[0] - members * piece
    shares = jnp.concatenate([shares[:kept], exchanged(shares[kept:])], axis=0)
    shares = lax.all_gather(shares, "ctx", axis=0, tiled=False)
    out_rows = out_weight.shape[0] // ctx_size
    out_weight_grad = shares[:, :out_rows].reshape(out_weight.shape).astype(f32)
    proj_weight_grad = shares[:, out_rows:kept].reshape(proj_weight.shape).astype(f32)
    fc_weight_grad = (
        shares[:, kept:]
        .reshape(ctx_size, members, piece, hidden)
        .transpose(0, 2, 1, 3)
        .reshape(fc_weight.shape)
        .astype(f32)
    )

    grad_query = grad_query_t.T * HEAD**-0.5
    grad_qkv = jnp.concatenate([grad_query.astype(b16), own_kv], axis=1)
    grad_norm1 = scattered(transposed_product(grad_qkv, qkv_cols).astype(b16)).astype(f32)
    qkv_share = rows_product(norm1, grad_qkv).astype(b16)
    qkv_share = (
        qkv_share.reshape(members, ctx_size, piece, 3 * span)
        .transpose(1, 0, 2, 3)
        .reshape(ctx_size, members * piece, 3 * span)
    )
    qkv_share = lax.psum_scatter(qkv_share, "ctx", scatter_dimension=0, tiled=True)[0]
    qkv_share = lax.all_gather(exchanged(qkv_share), "ctx", axis=0, tiled=False)
    qkv_weight_grad = (
        qkv_share.reshape(ctx_size, members, piece, 3, span)
        .transpose(0, 2, 3, 1, 4)
        .reshape(qkv_weight.shape)
        .astype(f32)
    )
    _, normed1, inv_std1 = layer_norm(block_input.astype(f32), gain_one, shift_one)
    input_grad = grad_middle + norm_backward(grad_norm1, gain_one, normed1, inv_std1)

    split_sums = jnp.concatenate(
        [
            jnp.sum(grad_query, axis=0),
            jnp.sum(own_kv[:, span:].astype(f32), axis=0),
            fc_bias_grad,
        ]
    )
    row_sums = jnp.stack(
        [
            jnp.sum(grad_norm1 * normed1, axis=0),
            jnp.sum(grad_norm1, axis=0),
            jnp.sum(grad_middle, axis=0),
            jnp.sum(grad_norm2 * normed2, axis=0),
            jnp.sum(grad_norm2, axis=0),
            jnp.sum(grad_out, axis=0),
        ]
    ).reshape(6, members, span)
    own_slot = (jnp.arange(members) == member)[:, None]
    sums = jnp.concatenate(
        [
            row_sums.transpose(1, 0, 2).reshape(members, 6 * span),
            jnp.where(own_slot, split_sums[None], 0.0),
        ],
        axis=1,
    )
    sums = lax.dynamic_index_in_dim(lax.psum(sums, ("ctx", "fsdp")), member, keepdims=False)
    parts = sums[: 8 * span].reshape(8, span)
    return (
        block_output,
        input_grad,
        parts[0],
        parts[1],
        qkv_weight_grad,
        parts[6],
        parts[7],
        proj_weight_grad,
        parts[2],
        parts[3],
        parts[4],
        fc_weight_grad,
        sums[8 * span :],
        out_weight_grad,
        parts[5],
    )


def solution(mesh):
    in_specs = (
        P(("ctx", "fsdp"), None),
        P(),
        P("fsdp"),
        P("fsdp"),
        P("fsdp", None),
        P("fsdp"),
        P("fsdp"),
        P("fsdp", None),
        P("fsdp"),
        P("fsdp"),
        P("fsdp"),
        P("fsdp", None),
        P("fsdp"),
        P("fsdp", None),
        P("fsdp"),
        P(("ctx", "fsdp"), None),
    )
    out_specs = (
        P(("ctx", "fsdp"), None),
        P(("ctx", "fsdp"), None),
        P("fsdp"),
        P("fsdp"),
        P("fsdp", None),
        P("fsdp"),
        P("fsdp"),
        P("fsdp", None),
        P("fsdp"),
        P("fsdp"),
        P("fsdp"),
        P("fsdp", None),
        P("fsdp"),
        P("fsdp", None),
        P("fsdp"),
    )
    members = mesh.shape["fsdp"]
    by_heads = HEADS % members == 0 and (HEADS // members * HEAD) % mesh.shape["ctx"] == 0
    body = head_shards if by_heads else shards
    return jax.shard_map(body, mesh=mesh, in_specs=in_specs, out_specs=out_specs, check_vma=False)
```

```python
import functools

import jax
import jax.numpy as jnp
from jax import lax
from jax.experimental import pallas as pl
from jax.experimental.pallas import tpu as pltpu
from jax.sharding import PartitionSpec as P

HEADS = 12
HEAD = 64


EPSILON = 1e-05
NEG_FILL = -1e30
GELU_C = 0.7978845608028654
GELU_K = 0.044715


def passed_along(block, axis, distance):
    devices = range(lax.axis_size(axis))
    route = [((i - distance) % len(devices), i) for i in devices]
    return lax.ppermute(block, axis, route)


def layer_norm(values_in, gain, shift):
    row_mean = jnp.mean(values_in, axis=-1, keepdims=True)
    centered = values_in - row_mean
    variance = jnp.mean(centered * centered, axis=-1, keepdims=True)
    inv_std = lax.rsqrt(variance + EPSILON)
    normed = centered * inv_std
    return (normed * gain.astype(jnp.float32) + shift.astype(jnp.float32), normed, inv_std)


def norm_backward(grad_norm, gain, normed, inv_std):
    scaled = grad_norm * gain.astype(jnp.float32)
    scaled_mean = jnp.mean(scaled, axis=-1, keepdims=True)
    cross_mean = jnp.mean(scaled * normed, axis=-1, keepdims=True)
    return inv_std * (scaled - scaled_mean - normed * cross_mean)


def gelu_forward(pre_act):
    cubed = pre_act * pre_act * pre_act
    return 0.5 * pre_act * (1.0 + jnp.tanh(GELU_C * (pre_act + GELU_K * cubed)))


def gelu_slope(pre_act):
    cubed = pre_act * pre_act * pre_act
    tanh_value = jnp.tanh(GELU_C * (pre_act + GELU_K * cubed))
    return 0.5 * (1.0 + tanh_value) + 0.5 * pre_act * (1.0 - tanh_value * tanh_value) * GELU_C * (
        1.0 + 3.0 * GELU_K * pre_act * pre_act
    )


def rows_product(left, right):
    return lax.dot_general(
        left, right, (((0,), (0,)), ((), ())), preferred_element_type=jnp.float32
    )


def transposed_product(left, right):
    return lax.dot_general(
        left, right, (((1,), (1,)), ((), ())), preferred_element_type=jnp.float32
    )


def split_heads(matrix):
    return matrix.reshape(matrix.shape[0], HEADS, HEAD)


def masked_scores(query, query_pos, keys, key_pos):
    scores = jnp.einsum(
        "rhd,khd->hrk", split_heads(query), split_heads(keys), preferred_element_type=jnp.float32
    ) * HEAD ** (-0.5)
    allowed = (key_pos[None, :] <= query_pos[:, None])[None]
    return (jnp.where(allowed, scores, NEG_FILL), allowed)


def attend_block(carried, query, query_pos, keys, values, key_pos):
    weighted, run_max, row_total = carried
    scores, allowed = masked_scores(query, query_pos, keys, key_pos)
    new_max = jnp.maximum(run_max, jnp.max(scores, axis=-1))
    weights = jnp.where(allowed, jnp.exp(scores - new_max[..., None]), 0.0)
    factor = jnp.exp(run_max - new_max)
    row_total = row_total * factor + jnp.sum(weights, axis=-1)
    update = jnp.einsum(
        "hrk,khd->rhd",
        weights,
        split_heads(values).astype(jnp.float32),
        precision=lax.Precision.HIGHEST,
        preferred_element_type=jnp.float32,
    )
    weighted = weighted * factor.T[:, :, None] + update
    return (weighted, new_max, row_total)


def attend_tile(carried, query, query_pos, keys, values, key_pos):
    half_rows = keys.shape[0] // 2
    latest = jnp.max(query_pos)
    for half_index in range(2):
        first_row = half_index * half_rows
        part_keys = keys[first_row : first_row + half_rows]
        part_values = values[first_row : first_row + half_rows]
        part_pos = key_pos[first_row : first_row + half_rows]

        def keep_state(state_in, block_keys, block_values, block_pos):
            return state_in

        def update_state(state_in, block_keys, block_values, block_pos):
            return attend_block(state_in, query, query_pos, block_keys, block_values, block_pos)

        carried = lax.cond(
            jnp.min(part_pos) > latest,
            keep_state,
            update_state,
            carried,
            part_keys,
            part_values,
            part_pos,
        )
    return carried


def block_grads(query, grad_attn, row_lse, row_delta, query_pos, keys, values, key_pos):
    scores, allowed = masked_scores(query, query_pos, keys, key_pos)
    probs = jnp.where(allowed, jnp.exp(scores - row_lse[..., None]), 0.0)
    grad_heads = split_heads(grad_attn)
    grad_values = jnp.einsum(
        "hrk,rhd->khd", probs.astype(jnp.bfloat16), grad_heads, preferred_element_type=jnp.float32
    )
    grad_probs = jnp.einsum(
        "rhd,khd->hrk", grad_heads, split_heads(values), preferred_element_type=jnp.float32
    )
    grad_scores = (probs * (grad_probs - row_delta[..., None])).astype(jnp.bfloat16)
    scale = HEAD ** (-0.5)
    grad_query = (
        jnp.einsum(
            "hrk,khd->rhd", grad_scores, split_heads(keys), preferred_element_type=jnp.float32
        )
        * scale
    )
    grad_keys = (
        jnp.einsum(
            "hrk,rhd->khd", grad_scores, split_heads(query), preferred_element_type=jnp.float32
        )
        * scale
    )
    key_rows = keys.shape[0]
    return (grad_query, grad_keys.reshape(key_rows, -1), grad_values.reshape(key_rows, -1))


def tile_grads(query, grad_attn, row_lse, row_delta, query_pos, keys, values, key_pos):
    half_rows = keys.shape[0] // 2
    key_width = keys.shape[1]
    latest = jnp.max(query_pos)
    query_total = jnp.zeros((query.shape[0], HEADS, HEAD), jnp.float32)
    key_parts = []
    value_parts = []
    for half_index in range(2):
        first_row = half_index * half_rows
        part_keys = keys[first_row : first_row + half_rows]
        part_values = values[first_row : first_row + half_rows]
        part_pos = key_pos[first_row : first_row + half_rows]

        def skipped(block_keys, block_values, block_pos):
            return (
                jnp.zeros((query.shape[0], HEADS, HEAD), jnp.float32),
                jnp.zeros((half_rows, key_width), jnp.float32),
                jnp.zeros((half_rows, key_width), jnp.float32),
            )

        def computed(block_keys, block_values, block_pos):
            return block_grads(
                query, grad_attn, row_lse, row_delta, query_pos, block_keys, block_values, block_pos
            )

        step_query, step_keys, step_values = lax.cond(
            jnp.min(part_pos) > latest, skipped, computed, part_keys, part_values, part_pos
        )
        query_total = query_total + step_query
        key_parts.append(step_keys)
        value_parts.append(step_values)
    return (query_total, jnp.concatenate(key_parts, axis=0), jnp.concatenate(value_parts, axis=0))


def shards(
    block_input,
    positions,
    norm1_gain,
    norm1_bias,
    qkv_weight,
    query_bias,
    value_bias,
    proj_weight,
    proj_bias,
    norm2_gain,
    norm2_bias,
    fc_weight,
    fc_bias,
    out_weight,
    out_bias,
    cotangent,
):
    rows = block_input.shape[0]
    width = block_input.shape[1]
    ctx_size = lax.axis_size("ctx")
    shard_count = lax.axis_size("fsdp")
    ctx_index = lax.axis_index("ctx")
    shard_index = lax.axis_index("fsdp")
    group_rows = rows * shard_count

    def key_positions(source):
        return lax.dynamic_slice_in_dim(positions, source * group_rows, group_rows)

    gain_one, shift_one, qkv_full, qbias_full, vbias_full, proj_full, pbias_full = (
        lax.all_gather(norm1_gain, "fsdp", axis=0, tiled=True),
        lax.all_gather(norm1_bias, "fsdp", axis=0, tiled=True),
        lax.all_gather(qkv_weight, "fsdp", axis=0, tiled=True),
        lax.all_gather(query_bias, "fsdp", axis=0, tiled=True),
        lax.all_gather(value_bias, "fsdp", axis=0, tiled=True),
        lax.all_gather(proj_weight, "fsdp", axis=0, tiled=True),
        lax.all_gather(proj_bias, "fsdp", axis=0, tiled=True),
    )
    gain_two, shift_two, fc_full, fbias_full, out_full, obias_full = (
        lax.all_gather(norm2_gain, "fsdp", axis=0, tiled=True),
        lax.all_gather(norm2_bias, "fsdp", axis=0, tiled=True),
        lax.all_gather(fc_weight, "fsdp", axis=0, tiled=True),
        lax.all_gather(fc_bias, "fsdp", axis=0, tiled=True),
        lax.all_gather(out_weight, "fsdp", axis=0, tiled=True),
        lax.all_gather(out_bias, "fsdp", axis=0, tiled=True),
    )
    residual = block_input.astype(jnp.float32)
    normed1_out, normed1, inv_std1 = layer_norm(residual, gain_one, shift_one)
    norm1 = normed1_out.astype(jnp.bfloat16)
    qkv = jnp.dot(norm1, qkv_full, preferred_element_type=jnp.float32)
    query = (qkv[:, :width] + qbias_full.astype(jnp.float32)).astype(jnp.bfloat16)
    keys = qkv[:, width : 2 * width].astype(jnp.bfloat16)
    values = (qkv[:, 2 * width :] + vbias_full.astype(jnp.float32)).astype(jnp.bfloat16)
    group_keys, group_values = (
        lax.all_gather(keys, "fsdp", axis=0, tiled=True),
        lax.all_gather(values, "fsdp", axis=0, tiled=True),
    )
    own_qpos = lax.dynamic_slice_in_dim(
        positions, (ctx_index * shard_count + shard_index) * rows, rows
    )
    own_kpos = key_positions(ctx_index)
    initial = (
        jnp.zeros((rows, HEADS, HEAD), jnp.float32),
        jnp.full((HEADS, rows), NEG_FILL, jnp.float32),
        jnp.zeros((HEADS, rows), jnp.float32),
    )
    carried = attend_tile(initial, query, own_qpos, group_keys, group_values, own_kpos)

    def forward_hop(hop_index, loop_carry):
        state_now, cycle_keys, cycle_values = loop_carry
        cycle_keys, cycle_values = passed_along((cycle_keys, cycle_values), "ctx", 1)
        source = (ctx_index - hop_index) % ctx_size
        state_now = attend_tile(
            state_now, query, own_qpos, cycle_keys, cycle_values, key_positions(source)
        )
        return (state_now, cycle_keys, cycle_values)

    result = lax.fori_loop(1, ctx_size, forward_hop, (carried, group_keys, group_values))
    carried = result[0]
    weighted, run_max, row_total = carried
    attn = (weighted / row_total.T[:, :, None]).reshape(rows, width).astype(jnp.bfloat16)
    row_lse = run_max + jnp.log(row_total)
    middle = (
        residual
        + jnp.dot(attn, proj_full, preferred_element_type=jnp.float32)
        + pbias_full.astype(jnp.float32)
    )
    normed2_out, normed2, inv_std2 = layer_norm(middle, gain_two, shift_two)
    norm2 = normed2_out.astype(jnp.bfloat16)
    pre_act = jnp.dot(norm2, fc_full, preferred_element_type=jnp.float32) + fbias_full.astype(
        jnp.float32
    )
    act = gelu_forward(pre_act).astype(jnp.bfloat16)
    block_output = (
        middle
        + jnp.dot(act, out_full, preferred_element_type=jnp.float32)
        + obias_full.astype(jnp.float32)
    )
    grad_out = cotangent.astype(jnp.float32)
    out_weight_grad = rows_product(act, cotangent)
    out_bias_grad = jnp.sum(grad_out, axis=0)
    grad_act = transposed_product(cotangent, out_full)
    grad_pre = grad_act * gelu_slope(pre_act)
    fc_bias_grad = jnp.sum(grad_pre, axis=0)
    grad_pre_half = grad_pre.astype(jnp.bfloat16)
    fc_weight_grad = rows_product(norm2, grad_pre_half)
    grad_norm2 = transposed_product(grad_pre_half, fc_full)
    norm2_gain_grad = jnp.sum(grad_norm2 * normed2, axis=0)
    norm2_bias_grad = jnp.sum(grad_norm2, axis=0)
    grad_middle = grad_out + norm_backward(grad_norm2, gain_two, normed2, inv_std2)
    mlp_shares = (
        lax.psum_scatter(norm2_gain_grad, "fsdp", scatter_dimension=0, tiled=True),
        lax.psum_scatter(norm2_bias_grad, "fsdp", scatter_dimension=0, tiled=True),
        lax.psum_scatter(fc_weight_grad, "fsdp", scatter_dimension=0, tiled=True),
        lax.psum_scatter(fc_bias_grad, "fsdp", scatter_dimension=0, tiled=True),
        lax.psum_scatter(out_weight_grad, "fsdp", scatter_dimension=0, tiled=True),
        lax.psum_scatter(out_bias_grad, "fsdp", scatter_dimension=0, tiled=True),
    )
    proj_bias_grad = jnp.sum(grad_middle, axis=0)
    grad_middle_half = grad_middle.astype(jnp.bfloat16)
    proj_weight_grad = rows_product(attn, grad_middle_half)
    grad_attn = transposed_product(grad_middle_half, proj_full).astype(jnp.bfloat16)
    row_delta = jnp.sum(
        split_heads(grad_attn).astype(jnp.float32) * split_heads(attn).astype(jnp.float32), axis=-1
    ).T
    grad_query, grad_keys, grad_values = tile_grads(
        query, grad_attn, row_lse, row_delta, own_qpos, group_keys, group_values, own_kpos
    )

    def pass_key_grads(key_grads):
        return passed_along((key_grads[0], key_grads[1]), "ctx", 1)

    def backward_hop(hop_index, loop_carry):
        query_sum, key_grads, cycle_keys, cycle_values = loop_carry
        cycle_keys, cycle_values = passed_along((cycle_keys, cycle_values), "ctx", 1)
        key_grads = pass_key_grads(key_grads)
        source = (ctx_index - hop_index) % ctx_size
        step_query, step_keys, step_values = tile_grads(
            query,
            grad_attn,
            row_lse,
            row_delta,
            own_qpos,
            cycle_keys,
            cycle_values,
            key_positions(source),
        )
        return (
            query_sum + step_query,
            (key_grads[0] + step_keys, key_grads[1] + step_values),
            cycle_keys,
            cycle_values,
        )

    result = lax.fori_loop(
        1, ctx_size, backward_hop, (grad_query, (grad_keys, grad_values), group_keys, group_values)
    )
    grad_query = result[0]
    key_grads = pass_key_grads(result[1])
    own_key_grad, own_value_grad = (
        lax.psum_scatter(key_grads[0], "fsdp", scatter_dimension=0, tiled=True),
        lax.psum_scatter(key_grads[1], "fsdp", scatter_dimension=0, tiled=True),
    )
    grad_query_rows = grad_query.reshape(rows, width)
    query_bias_grad = jnp.sum(grad_query_rows, axis=0)
    value_bias_grad = jnp.sum(own_value_grad, axis=0)
    grad_qkv = jnp.concatenate([grad_query_rows, own_key_grad, own_value_grad], axis=1).astype(
        jnp.bfloat16
    )
    qkv_weight_grad = rows_product(norm1, grad_qkv)
    grad_norm1 = transposed_product(grad_qkv, qkv_full)
    norm1_gain_grad = jnp.sum(grad_norm1 * normed1, axis=0)
    norm1_bias_grad = jnp.sum(grad_norm1, axis=0)
    input_grad = grad_middle + norm_backward(grad_norm1, gain_one, normed1, inv_std1)
    attn_shares = (
        lax.psum_scatter(norm1_gain_grad, "fsdp", scatter_dimension=0, tiled=True),
        lax.psum_scatter(norm1_bias_grad, "fsdp", scatter_dimension=0, tiled=True),
        lax.psum_scatter(qkv_weight_grad, "fsdp", scatter_dimension=0, tiled=True),
        lax.psum_scatter(query_bias_grad, "fsdp", scatter_dimension=0, tiled=True),
        lax.psum_scatter(value_bias_grad, "fsdp", scatter_dimension=0, tiled=True),
        lax.psum_scatter(proj_weight_grad, "fsdp", scatter_dimension=0, tiled=True),
        lax.psum_scatter(proj_bias_grad, "fsdp", scatter_dimension=0, tiled=True),
    )
    totals = lax.psum(
        (
            attn_shares[0],
            attn_shares[1],
            attn_shares[2],
            attn_shares[3],
            attn_shares[4],
            attn_shares[5],
            attn_shares[6],
            mlp_shares[0],
            mlp_shares[1],
            mlp_shares[2],
            mlp_shares[3],
            mlp_shares[4],
            mlp_shares[5],
        ),
        "ctx",
    )
    return (
        block_output,
        input_grad,
        totals[0],
        totals[1],
        totals[2],
        totals[3],
        totals[4],
        totals[5],
        totals[6],
        totals[7],
        totals[8],
        totals[9],
        totals[10],
        totals[11],
        totals[12],
    )


MESH = pl.DeviceIdType.MESH
SMEM = pltpu.SMEM
VMEM = pltpu.VMEM
F32 = jnp.float32
B16 = jnp.bfloat16


class Transfer:
    def __init__(self, links, src, dst, device):
        self.args = dict(
            src_ref=src,
            dst_ref=dst,
            send_sem=links.send_sem.at[links.count],
            recv_sem=links.recv_sem.at[links.count],
            device_id=device,
            device_id_type=MESH,
        )
        links.count += 1
        links.sent.append(self)

    def start(self):
        pltpu.make_async_remote_copy(**self.args).start()
        return self

    def arrived(self):
        pltpu.make_async_remote_copy(**self.args).wait_recv()

    def left(self):
        pltpu.make_async_remote_copy(**self.args).wait_send()


class Links:
    def __init__(self, send_sem, recv_sem):
        self.send_sem, self.recv_sem = send_sem, recv_sem
        self.count = 0
        self.sent = []
        ctx = lax.axis_index("ctx")
        self.ctx = ctx
        self.z = lax.axis_index("fsdp")
        self.core = lax.rem(ctx, 2)
        self.chip = lax.div(ctx, 2)
        x, y = lax.rem(self.chip, 2), lax.div(self.chip, 2)
        self.chip_x = self.chip + 1 - 2 * x
        self.chip_y = self.chip + 2 - 4 * y
        self.chip_d = 3 - self.chip
        self.other = 1 - self.core
        self.to_core = {"ctx": self.chip * 2 + self.other}
        self.to_x = {"ctx": self.chip_x * 2 + self.core}
        self.to_y = {"ctx": self.chip_y * 2 + self.core}

    def zed(self, step):
        return lax.rem(self.z + step, 4)

    def to_z(self, step):
        return {"fsdp": self.zed(step)}

    def peers(self):
        return [self.to_core, self.to_x, self.to_y, self.to_z(1), self.to_z(2), self.to_z(3)]

    def copy(self, src, dst, device):
        return Transfer(self, src, dst, device)

    def greet(self):
        barrier = pltpu.get_barrier_semaphore()
        for device in self.peers():
            pl.semaphore_signal(barrier, inc=1, device_id=device, device_id_type=MESH)

    def greeted(self):
        pl.semaphore_wait(pltpu.get_barrier_semaphore(), 6)

    def drain(self):
        for transfer in self.sent:
            transfer.left()


class RingGather:
    def __init__(self, links, buf):
        half = buf.shape[1] // 2
        own, left, right = links.z, links.zed(3), links.zed(1)

        def piece(member, part):
            return buf.at[member, part * half : (part + 1) * half]

        def move(member, part, step):
            return links.copy(piece(member, part), piece(member, part), links.to_z(step))

        self.first = [move(own, 0, 1), move(own, 1, 3), move(own, 1, 1), move(own, 0, 3)]
        self.second = [move(left, 0, 1), move(right, 1, 3)]

    def start(self):
        for transfer in self.first:
            transfer.start()

    def forward(self):
        for transfer, onward in zip(self.first[:2], self.second):
            transfer.arrived()
            onward.start()

    def near(self):
        for transfer in self.first[2:]:
            transfer.arrived()

    def far(self):
        for transfer in self.second:
            transfer.arrived()


class Shared:
    def __init__(self, links, source, target):
        half = target.shape[1] // 2
        rows = pl.ds(pl.multiple_of(links.core * half, half), half)
        self.cross = [
            links.copy(source(links.zed(step), rows), target.at[links.z, rows], links.to_z(step))
            for step in (1, 3, 2)
        ]
        self.hand = [
            links.copy(
                target.at[links.zed(4 - step), rows],
                target.at[links.zed(4 - step), rows],
                links.to_core,
            )
            for step in (1, 3, 2)
        ]

    def start(self):
        for transfer in self.cross:
            transfer.start()

    def forward(self):
        for transfer, onward in zip(self.cross, self.hand):
            transfer.arrived()
            onward.start()

    def finish(self):
        for transfer in self.hand:
            transfer.arrived()


class ContextGather:
    def __init__(self, links, buf):
        half = buf.shape[2] // 2

        def move(chip, part, device):
            rows = slice(None) if part is None else slice(part * half, (part + 1) * half)
            ref = buf.at[links.core, chip, rows]
            return links.copy(ref, ref, device)

        own, x, y, d = links.chip, links.chip_x, links.chip_y, links.chip_d
        self.own_core = move(own, None, links.to_core)
        self.x_parts = [move(own, 0, links.to_x), move(own, 1, links.to_x)]
        self.y_parts = [move(own, 1, links.to_y), move(own, 0, links.to_y)]
        self.onward = [move(x, 0, links.to_y), move(y, 1, links.to_x)]
        self.x_core = move(x, None, links.to_core)
        self.y_core = move(y, None, links.to_core)
        self.d_core = move(d, None, links.to_core)

    def start(self):
        for transfer in (
            self.x_parts[0],
            self.y_parts[0],
            self.own_core,
            self.x_parts[1],
            self.y_parts[1],
        ):
            transfer.start()

    def forward(self):
        self.x_parts[0].arrived()
        self.onward[0].start()
        self.y_parts[0].arrived()
        self.onward[1].start()

    def hand_near(self):
        self.x_parts[1].arrived()
        self.x_core.start()
        self.y_parts[1].arrived()
        self.y_core.start()

    def hand_far(self):
        self.onward[0].arrived()
        self.onward[1].arrived()
        self.d_core.start()


def chosen(flag, shape):
    return jnp.full(shape, flag, jnp.int32) == 1


def masked_heads(value, first, width):
    rows, span = value.shape
    pieces = []
    if first > 0:
        pieces.append(jnp.zeros((rows, first), value.dtype))
    pieces.append(value)
    if first + span < width:
        pieces.append(jnp.zeros((rows, width - first - span), value.dtype))
    wide = jnp.concatenate(pieces, axis=1) if len(pieces) > 1 else value
    head = (lax.broadcasted_iota(jnp.int32, (rows, width), 1) - first + HEAD) // HEAD - 1
    return [
        jnp.where(head == index, wide.astype(F32), 0.0).astype(value.dtype)
        for index in range(span // HEAD)
    ]


def soft_step(scores, old_max, old_sum):
    new_max = jnp.maximum(old_max, jnp.max(scores, axis=0, keepdims=True))
    weights = jnp.exp(scores - new_max)
    factor = jnp.exp(old_max - new_max)
    new_sum = old_sum * factor + jnp.sum(weights, axis=0, keepdims=True)
    return weights.astype(B16), factor, new_max, new_sum


def forward_phase(
    links, ids, x, cot, qkvw, fcw, projw, vec, qvbias,
    attn_t, lse, qm, kv, x_all, w_all, cot_all, fc_all, proj_all, vec_all, norm1,
    stage, fcs, max_h, sum_h, acc_h, max_x, sum_x, acc_x,
):
    rows = x.shape[0]
    span = qkvw.shape[0]
    block = 2 * rows
    heads = span // HEAD
    z = links.z
    links.greet()
    x_all[z] = x[...]
    cot_all[z] = cot[...]
    proj_all[z] = projw[...]
    vec_all[z] = vec[...]
    for member in range(4):
        stage[member, :, : 3 * span] = jnp.concatenate(
            [qkvw[:, t * 4 * span + member * span : t * 4 * span + (member + 1) * span] for t in range(3)],
            axis=1,
        )
        fcs[member] = fcw[:, member * 4 * span : (member + 1) * 4 * span]
    w_all[z] = stage[z]
    fc_all[z] = fcs[z]

    vectors = [
        links.copy(vec_all.at[z], vec_all.at[z], links.to_z(step)) for step in (1, 3, 2)
    ]
    inputs = RingGather(links, x_all)
    weights = Shared(links, lambda member, part: stage.at[member, part], w_all)
    cots = RingGather(links, cot_all)
    fcs_in = Shared(links, lambda member, part: fcs.at[member, part], fc_all)
    projs = Shared(links, lambda member, part: proj_all.at[z, part], proj_all)
    context = ContextGather(links, kv)

    links.greeted()
    for transfer in vectors:
        transfer.start()
    inputs.start()
    weights.start()
    for transfer in vectors:
        transfer.arrived()

    gain = jnp.concatenate([vec_all[m, 0:1, :span] for m in range(4)], axis=1).astype(F32)
    shift = jnp.concatenate([vec_all[m, 1:2, :span] for m in range(4)], axis=1).astype(F32)

    def normalise(member):
        normed = layer_norm(x_all[member].astype(F32), gain, shift)[0]
        first = pl.multiple_of(member * rows, rows)
        norm1[pl.ds(first, rows), :] = normed.astype(B16)

    normalise(z)
    inputs.forward()
    inputs.near()
    normalise(links.zed(1))
    normalise(links.zed(3))
    weights.forward()
    inputs.far()
    normalise(links.zed(2))
    weights.finish()
    cots.start()
    fcs_in.start()
    projs.start()

    matrix = w_all[...].reshape(4 * span, w_all.shape[2])[:, : 3 * span]
    for part in range(2):
        at = slice(part * block, (part + 1) * block)
        product = jnp.dot(norm1[at, :], matrix, preferred_element_type=F32)
        query = (product[:, :span] + qvbias[0:1, :].astype(F32)).astype(B16)
        query = query * jnp.asarray(HEAD**-0.5, B16)
        for head, lone in enumerate(masked_heads(query, 0, 4 * HEAD)):
            qm[head, at, :] = lone
        values = product[:, 2 * span :] + qvbias[1:2, :].astype(F32)
        kv[links.core, links.chip, at, :] = jnp.concatenate(
            [product[:, span : 2 * span], values], axis=1
        ).astype(B16)
    context.start()

    own_block = ids[2 * links.ctx]
    keep = lax.broadcasted_iota(jnp.int32, (block, block), 0) <= lax.broadcasted_iota(
        jnp.int32, (block, block), 1
    )
    none = jnp.full((1, block), NEG_FILL, F32)
    zero = jnp.zeros((1, block), F32)

    def halves(core, chip, part):
        at = slice(part * block, (part + 1) * block)
        return kv[core, chip, at, : 4 * HEAD], kv[core, chip, at, 2 * HEAD :].T

    def value_rows(head):
        return slice((1 + head) * HEAD, (2 + head) * HEAD)

    def head_rows(head):
        return slice(head * HEAD, (head + 1) * HEAD)

    k_low, vt_low = halves(links.core, links.chip, 0)
    k_high, vt_high = halves(links.core, links.chip, 1)
    for head in range(heads):
        q_low, q_high = qm[head, :block, :], qm[head, block:, :]
        scores = jnp.where(keep, transposed_product(k_low, q_low), NEG_FILL)
        w, _, top, total = soft_step(scores, none, zero)
        max_x[0, head : head + 1, :] = top
        sum_x[0, head : head + 1, :] = total
        acc_x[0, head_rows(head), :] = jnp.dot(
            vt_low[value_rows(head)], w, preferred_element_type=F32
        )
        scores = transposed_product(k_low, q_high)
        w, _, top, total = soft_step(scores, none, zero)
        acc = jnp.dot(vt_low[value_rows(head)], w, preferred_element_type=F32)
        scores = jnp.where(keep, transposed_product(k_high, q_high), NEG_FILL)
        w, factor, top, total = soft_step(scores, top, total)
        max_h[head : head + 1, :] = top
        sum_h[head : head + 1, :] = total
        acc_h[head_rows(head), :] = acc * factor + jnp.dot(
            vt_high[value_rows(head)], w, preferred_element_type=F32
        )
    max_x[1] = jnp.full_like(max_h, NEG_FILL)
    sum_x[1] = jnp.zeros_like(sum_h)
    acc_x[1] = jnp.zeros_like(acc_h)

    def hop(index, carry):
        near = index < 3
        far = index >= 5
        core = jnp.where((index == 1) | (index == 2) | (index == 5), links.core, links.other)
        chip = jnp.where(
            index == 0,
            links.chip,
            jnp.where(far, links.chip_d, jnp.where(lax.rem(index, 2) == 1, links.chip_x, links.chip_y)),
        )

        @pl.when(index == 0)
        def _():
            context.own_core.arrived()
            context.forward()

        @pl.when(index == 1)
        def _():
            context.hand_near()
            cots.forward()
            cots.near()

        @pl.when(index == 3)
        def _():
            context.x_core.arrived()
            context.hand_far()
            fcs_in.forward()

        @pl.when(index == 4)
        def _():
            context.y_core.arrived()
            cots.far()

        @pl.when(index == 6)
        def _():
            context.d_core.arrived()

        block_id = ids[2 * (2 * chip + core)]
        low = (block_id < own_block).astype(jnp.int32)
        in_low = chosen(low, (1, block))
        kv_low = kv[core, chip, :block, :]
        kv_high = kv[core, chip, block:, :]
        kv_pick = jnp.where(chosen(low, kv_low.shape), kv_low, kv_high)
        q_mask = chosen(low, (block, 4 * HEAD))
        work = []
        for head in range(heads):
            scores = transposed_product(kv_low[:, : 4 * HEAD], qm[head, block:, :])
            work.append((scores, max_h[head : head + 1, :], sum_h[head : head + 1, :]))
        for head in range(heads):
            q_pick = jnp.where(q_mask, qm[head, :block, :], qm[head, block:, :])
            scores = transposed_product(kv_pick[:, : 4 * HEAD], q_pick)
            at = slice(head, head + 1)
            work.append(
                (
                    scores,
                    jnp.where(in_low, max_x[0, at, :], max_x[1, at, :]),
                    jnp.where(in_low, sum_x[0, at, :], sum_x[1, at, :]),
                )
            )
        done = [soft_step(*entry) for entry in work]
        vt = kv_low[:, 2 * HEAD :].T
        for head in range(heads):
            w, factor, top, total = done[head]
            max_h[head : head + 1, :] = top
            sum_h[head : head + 1, :] = total
            acc_h[head_rows(head), :] = acc_h[head_rows(head), :] * factor + jnp.dot(
                vt[value_rows(head)], w, preferred_element_type=F32
            )
        vt = kv_pick[:, 2 * HEAD :].T
        for head in range(heads):
            w, factor, top, total = done[heads + head]
            acc = jnp.where(in_low, acc_x[0, head_rows(head), :], acc_x[1, head_rows(head), :])
            acc = acc * factor + jnp.dot(
                vt[value_rows(head)], w, preferred_element_type=F32
            )
            for part in range(2):
                own = in_low if part == 0 else ~in_low
                max_x[part, head : head + 1, :] = jnp.where(own, top, max_x[part, head : head + 1, :])
                sum_x[part, head : head + 1, :] = jnp.where(
                    own, total, sum_x[part, head : head + 1, :]
                )
                acc_x[part, head_rows(head), :] = jnp.where(own, acc, acc_x[part, head_rows(head), :])
        return carry

    lax.fori_loop(0, 7, hop, 0)
    projs.forward()
    for head in range(heads):
        at = slice(head, head + 1)
        total = sum_x[0, at, :]
        attn_t[head_rows(head), :block] = (acc_x[0, head_rows(head), :] / total).astype(B16)
        lse[at, :block] = max_x[0, at, :] + jnp.log(total)
        top = jnp.maximum(max_h[at, :], max_x[1, at, :])
        left, right = jnp.exp(max_h[at, :] - top), jnp.exp(max_x[1, at, :] - top)
        total = sum_h[at, :] * left + sum_x[1, at, :] * right
        acc = acc_h[head_rows(head), :] * left + acc_x[1, head_rows(head), :] * right
        attn_t[head_rows(head), block:] = (acc / total).astype(B16)
        lse[at, block:] = top + jnp.log(total)
    fcs_in.finish()
    projs.finish()


def forward_kernel(*refs):
    send_sem, recv_sem = refs[-2:]
    links = Links(send_sem, recv_sem)
    forward_phase(links, *refs[:-2])
    links.drain()


def parts_of(rows):
    first = (rows // 2 + 15) // 16 * 16
    return [slice(0, first), slice(first, rows)]


class FourSum:
    def __init__(self, links, parts, early, late, far, own, near):
        self.parts, self.early, self.late, self.own, self.near = parts, early, late, own, near
        self.cuts = parts_of(early.shape[0])
        self.far = [
            links.copy(parts.at[far, self.cuts[k]], early.at[self.cuts[k]], near[k][0]) for k in range(2)
        ]
        self.ready, self.summed = [], []
        for k, (device, part, added) in enumerate(near):
            for half, group in ((1 - added, self.ready), (added, self.summed)):
                cut = self.cuts[half]
                group.append(links.copy(parts.at[part, cut], late.at[k, cut], device))

    def send_far(self):
        for transfer in self.far:
            transfer.start()

    def send_ready(self):
        for transfer in self.ready:
            transfer.start()

    def send_summed(self):
        for k, (_, part, added) in enumerate(self.near):
            cut = self.cuts[added]
            self.far[added].arrived()
            both = self.parts[part, cut].astype(F32) + self.early[cut].astype(F32)
            self.parts[part, cut] = both.astype(B16)
            self.summed[k].start()

    def total(self):
        for transfer in self.ready + self.summed:
            transfer.arrived()
        return (
            self.parts[self.own].astype(F32)
            + self.late[0].astype(F32)
            + self.late[1].astype(F32)
        )


def ring_sum(links, parts, early, late):
    right, left = links.zed(1), links.zed(3)
    near = [(links.to_z(1), right, 0), (links.to_z(3), left, 1)]
    return FourSum(links, parts, early, late, links.zed(2), links.z, near)


class ContextSum:
    def __init__(self, links, grads, handed, early, late):
        self.links, self.grads, self.handed = links, grads, handed
        order = (links.chip_d, links.chip_x, links.chip_y, links.chip)
        self.order = order
        self.hands = [
            links.copy(grads.at[links.other, chip], handed.at[k], links.to_core)
            for k, chip in enumerate(order)
        ]
        near = [(links.to_x, links.chip_x, 1), (links.to_y, links.chip_y, 0)]
        self.four = FourSum(
            links, grads.at[links.core], early, late, links.chip_d, links.chip, near
        )

    def hand(self, k):
        self.hands[k].start()

    def merge(self, k):
        self.hands[k].arrived()
        core, chip = self.links.core, self.order[k]
        both = self.grads[core, chip].astype(F32) + self.handed[k].astype(F32)
        self.grads[core, chip] = both.astype(B16)


def backward_phase(
    links, ids, attn_t, lse, qm, kv, x_all, w_all, cot_all, fc_all, proj_all, vec_all, norm1, projw, outw, fcb,
    block_out, input_grad, h_mlp, h_attn, sums,
    a_all, grad_act, norm2, act, grad_pre, gn2, gn2_e, gn2_l, mlp, mlp_e, mlp_l, gn1, gn1_e, gn1_l,
    gm_all, gm_own, mid_own, normed1, dkv, dkv_h, dkv_e, dkv_l, g_mlp, gmlp_h, gmlp_e, gmlp_l,
    g_attn, gattn_h, gattn_e, gattn_l, fc_piece, qkv_piece, dom, delta, dq, gqkv, zsum, bsum, ssum, rowsum,
):
    members, rows, width = x_all.shape
    span = attn_t.shape[0]
    group = members * rows
    block = group // 2
    heads = span // HEAD
    half = width // 2
    small = span // 4
    z = links.z
    right, left, opposite = links.zed(1), links.zed(3), links.zed(2)

    def row(index):
        return jnp.concatenate(
            [vec_all[m, index : index + 1, :span] for m in range(members)], axis=1
        ).astype(F32)

    def head_rows(head):
        return slice(head * HEAD, (head + 1) * HEAD)

    def member_rows(member):
        return pl.ds(pl.multiple_of(member * rows, rows), rows)

    def in_order(index):
        return jnp.where(
            index == 0, opposite, jnp.where(index == 1, right, jnp.where(index == 2, left, z))
        )

    attns = RingGather(links, a_all)
    gms = RingGather(links, gm_all)
    ring_gn2 = ring_sum(links, gn2, gn2_e, gn2_l)
    ring_mlp = ring_sum(links, mlp, mlp_e, mlp_l)
    ring_gn1 = ring_sum(links, gn1, gn1_e, gn1_l)
    sum_mlp = ContextSum(links, g_mlp, gmlp_h, gmlp_e, gmlp_l)
    sum_attn = ContextSum(links, g_attn, gattn_h, gattn_e, gattn_l)
    sum_kv = ContextSum(links, dkv, dkv_h, dkv_e, dkv_l)
    gather_mlp = ContextGather(links, h_mlp)
    gather_attn = ContextGather(links, h_attn)

    def spread(piece, gathered, first):
        at = pl.ds(pl.multiple_of(first + small * z, 16), small)
        place = gathered.at[links.core, links.chip, at]
        return [links.copy(piece.at[links.zed(s)], place, links.to_z(s)) for s in (1, 3, 2)]

    spread_fc = spread(fc_piece, h_mlp, span)
    spread_qkv = spread(qkv_piece, h_attn, 0)

    links.greet()
    a_all[z] = attn_t[...]
    gain_one = row(0)
    gain_two, shift_two = row(3), row(4)
    proj_bias, out_bias = row(2), row(5)
    links.greeted()
    attns.start()
    one, zero_shift = jnp.ones((1, width), F32), jnp.zeros((1, width), F32)

    def before(index, carry):
        grad_act[member_rows(index), :] = transposed_product(cot_all[index], outw[...])
        normed1[member_rows(index), :] = layer_norm(x_all[index].astype(F32), one, zero_shift)[1]
        return carry

    lax.fori_loop(0, 2, before, 0)
    attns.forward()
    lax.fori_loop(2, 4, before, 0)
    attns.near()
    attns.far()
    rowsum[...] = jnp.zeros_like(rowsum)
    fc_matrix = fc_all.shape

    def mlp_block(index, carry):
        member = in_order(index)
        at = member_rows(member)

        @pl.when(index == 3)
        def _():
            ring_gn2.send_ready()
            ring_gn2.send_summed()

        attn_cols = a_all[:, :, at].reshape(width, rows)
        middle = (
            x_all[member].astype(F32)
            + rows_product(attn_cols, proj_all[...].reshape(width, width))
            + proj_bias
        )
        shifted, normed, _ = layer_norm(middle, gain_two, shift_two)
        half_norm = shifted.astype(B16)
        norm2[at, :] = half_norm
        fc = fc_all[...].reshape(width, fc_matrix[2])
        pre_act = jnp.dot(half_norm, fc, preferred_element_type=F32) + fcb[...].astype(F32)
        squared = pre_act * pre_act
        tanh_value = jnp.tanh(GELU_C * pre_act * (1.0 + GELU_K * squared))
        act[at, :] = (0.5 * pre_act * (1.0 + tanh_value)).astype(B16)
        slope = 0.5 * (1.0 + tanh_value) + (0.5 * GELU_C) * pre_act * (
            1.0 - tanh_value * tanh_value
        ) * (1.0 + 3.0 * GELU_K * squared)
        grad = grad_act[at, :] * slope
        rowsum[7:8, :] += jnp.sum(grad, axis=0, keepdims=True)
        grad_half = grad.astype(B16)
        grad_pre[at, :] = grad_half
        back = transposed_product(grad_half, fc)
        gn2[member] = back.astype(B16)
        rowsum[3:4, :] += jnp.sum(back * normed, axis=0, keepdims=True)
        rowsum[4:5, :] += jnp.sum(back, axis=0, keepdims=True)

        @pl.when(index == 0)
        def _():
            ring_gn2.send_far()

        @pl.when(index == 3)
        def _():
            mid_own[...] = middle

        return carry

    lax.fori_loop(0, 4, mlp_block, 0)

    def mlp_weights(core):
        cols = pl.ds(pl.multiple_of(core * half, half), half)
        cots = cot_all[:, :, cols].reshape(group, half)
        product = rows_product(act[...], cots).astype(B16)
        g_mlp[core, :, :span, :] = product.reshape(4, span, half)
        product = rows_product(norm2[...], grad_pre[:, cols]).astype(B16)
        product = product.reshape(members, 4, small, half)
        for member in range(members):
            at = span + member * small
            g_mlp[core, :, at : at + small, :] = product[member]

    mlp_weights(links.other)
    for k in range(4):
        sum_mlp.hand(k)

    grad_norm2 = ring_gn2.total()
    _, normed, inv_std = layer_norm(mid_own[...], gain_two, shift_two)
    cot_own = cot_all[z].astype(F32)
    grad_middle = cot_own + norm_backward(grad_norm2, gain_two, normed, inv_std)
    gm_own[...] = grad_middle
    gm_all[z] = grad_middle.astype(B16)
    gms.start()
    rowsum[2:3, :] = jnp.sum(grad_middle, axis=0, keepdims=True)
    rowsum[5:6, :] = jnp.sum(cot_own, axis=0, keepdims=True)

    mlp_weights(links.core)
    sum_mlp.merge(0)
    sum_mlp.four.send_far()
    sum_mlp.merge(1)
    sum_mlp.merge(2)
    sum_mlp.four.send_ready()
    gms.forward()

    def mlp_product(index, carry):
        at = member_rows(index)
        mlp[index] = jnp.dot(act[at, :], outw[...], preferred_element_type=F32).astype(B16)
        return carry

    lax.fori_loop(0, 4, mlp_product, 0)
    sum_mlp.four.send_summed()
    sum_mlp.merge(3)
    gms.near()
    gms.far()
    ring_mlp.send_far()
    ring_mlp.send_ready()

    grad_mid = gm_all[...].reshape(group, width)
    grad_attn_t = transposed_product(projw[...], grad_mid).astype(B16).astype(F32)
    delta_rows = grad_attn_t * attn_t[...].astype(F32)
    for head in range(heads):
        delta[head : head + 1, :] = jnp.sum(delta_rows[head_rows(head), :], axis=0, keepdims=True)
    grad_attn = transposed_product(grad_mid, projw[...]).astype(B16)
    for head, lone in enumerate(masked_heads(grad_attn, HEAD, 4 * HEAD)):
        dom[head] = lone
    product = jnp.dot(attn_t[...], grad_mid, preferred_element_type=F32).astype(B16)
    for core in range(2):
        g_attn[core, :, span:, :] = product[:, core * half : (core + 1) * half].reshape(4, small, half)
    dq[...] = jnp.zeros_like(dq)

    own_block = ids[2 * links.ctx]
    keep = lax.broadcasted_iota(jnp.int32, (block, block), 0) <= lax.broadcasted_iota(
        jnp.int32, (block, block), 1
    )
    low_rows, high_rows = slice(0, block), slice(block, group)

    def tile(keys, queries, grads, lse_of, delta_of, masked=False):
        probs, scores_grad = [], []
        for head in range(heads):
            scores = transposed_product(keys[:, : 4 * HEAD], queries[head])
            if masked:
                scores = jnp.where(keep, scores, NEG_FILL)
            weights = jnp.exp(scores - lse_of(head))
            grad_probs = transposed_product(keys[:, 2 * HEAD :], grads[head])
            probs.append(weights.astype(B16))
            scores_grad.append((weights * (grad_probs - delta_of(head))).astype(B16))
        keys_t = keys[:, : 4 * HEAD].T
        query_grad = [
            jnp.dot(keys_t[head_rows(head)], scores_grad[head], preferred_element_type=F32)
            for head in range(heads)
        ]
        value_grad = jnp.dot(
            jnp.concatenate(probs, axis=1),
            jnp.concatenate(grads, axis=0),
            preferred_element_type=F32,
        )
        key_grad = jnp.dot(
            jnp.concatenate(scores_grad, axis=1),
            jnp.concatenate(queries, axis=0),
            preferred_element_type=F32,
        )
        both = jnp.concatenate(
            [
                key_grad[:, : 2 * HEAD],
                key_grad[:, 2 * HEAD :] + value_grad[:, : 2 * HEAD],
                value_grad[:, 2 * HEAD :],
            ],
            axis=1,
        )
        return query_grad, both

    def stacked(ref, at):
        return [ref[head, at, :] for head in range(heads)]

    def rows_at(ref, at):
        return lambda head: ref[head : head + 1, at]

    def hop(index, carry):
        chip = jnp.where(
            index < 2,
            links.chip_d,
            jnp.where(index < 4, links.chip_x, jnp.where(index < 6, links.chip_y, links.chip)),
        )
        core = jnp.where(lax.rem(index, 2) == 0, links.other, links.core)

        @pl.when(index == 1)
        def _():
            sum_kv.hand(0)
            ring_mlp.send_summed()

        @pl.when(index == 2)
        def _():
            sum_kv.merge(0)
            sum_kv.four.send_far()
            total = sum_mlp.four.total().astype(B16)
            h_mlp[links.core, links.chip, :span, :] = total[:span]
            fc_piece[...] = total[span:].reshape(members, small, half)
            own = pl.ds(pl.multiple_of(span + small * z, 16), small)
            h_mlp[links.core, links.chip, own, :] = fc_piece[z]
            for transfer in spread_fc:
                transfer.start()

        @pl.when(index == 3)
        def _():
            sum_kv.hand(1)
            block_out[...] = ring_mlp.total() + mid_own[...] + out_bias
            for transfer in spread_fc:
                transfer.arrived()
            gather_mlp.start()

        @pl.when(index == 4)
        def _():
            sum_kv.merge(1)
            gather_mlp.forward()

        @pl.when(index == 5)
        def _():
            sum_kv.hand(2)
            gather_mlp.hand_near()

        @pl.when(index == 6)
        def _():
            sum_kv.merge(2)
            sum_kv.four.send_ready()
            sum_kv.four.send_summed()
            gather_mlp.hand_far()

        block_id = ids[2 * (2 * chip + core)]
        low = (block_id < own_block).astype(jnp.int32)
        in_low = chosen(low, (1, block))
        kv_low = kv[core, chip, low_rows, :]
        kv_pick = jnp.where(chosen(low, kv_low.shape), kv_low, kv[core, chip, high_rows, :])
        q_mask = chosen(low, (block, 4 * HEAD))

        def pick(ref):
            return [
                jnp.where(q_mask, ref[head, low_rows, :], ref[head, high_rows, :])
                for head in range(heads)
            ]

        def pick_row(ref):
            return lambda head: jnp.where(
                in_low, ref[head : head + 1, low_rows], ref[head : head + 1, high_rows]
            )

        query_grad, first = tile(
            kv_low,
            stacked(qm, high_rows),
            stacked(dom, high_rows),
            rows_at(lse, high_rows),
            rows_at(delta, high_rows),
        )
        for head in range(heads):
            dq[1, head_rows(head), :] += query_grad[head]
        query_grad, second = tile(kv_pick, pick(qm), pick(dom), pick_row(lse), pick_row(delta))
        for head in range(heads):
            at = head_rows(head)
            dq[0, at, :] += jnp.where(in_low, query_grad[head], 0.0)
            dq[1, at, :] += jnp.where(in_low, 0.0, query_grad[head])
        mask = chosen(low, second.shape)
        dkv[core, chip, low_rows, :] = (first + jnp.where(mask, second, 0.0)).astype(B16)
        dkv[core, chip, high_rows, :] = jnp.where(mask, 0.0, second).astype(B16)
        return carry

    lax.fori_loop(0, 7, hop, 0)
    sum_kv.hand(3)
    for keys_at, queries_at, masked in (
        (low_rows, high_rows, False),
        (low_rows, low_rows, True),
        (high_rows, high_rows, True),
    ):
        query_grad, both = tile(
            kv[links.core, links.chip, keys_at, :],
            stacked(qm, queries_at),
            stacked(dom, queries_at),
            rows_at(lse, queries_at),
            rows_at(delta, queries_at),
            masked,
        )
        part = 0 if queries_at is low_rows else 1
        for head in range(heads):
            dq[part, head_rows(head), :] += query_grad[head]
        if keys_at is low_rows and not masked:
            held = both
        elif keys_at is low_rows:
            dkv[links.core, links.chip, keys_at, :] = (held + both).astype(B16)
        else:
            dkv[links.core, links.chip, keys_at, :] = both.astype(B16)

    grad_query = jnp.concatenate([dq[0].T, dq[1].T], axis=0) * HEAD**-0.5
    sum_kv.merge(3)
    own_kv = sum_kv.four.total().astype(B16)
    split = jnp.concatenate(
        [
            jnp.sum(grad_query, axis=0, keepdims=True),
            jnp.sum(own_kv[:, span:].astype(F32), axis=0, keepdims=True),
            jnp.zeros((1, width - 2 * span), F32),
        ],
        axis=1,
    )
    rowsum[6:7, :] = split
    gqkv[...] = jnp.concatenate(
        [grad_query.astype(B16), own_kv, jnp.zeros((group, 640 - 3 * span), B16)], axis=1
    )

    def attn_weights(core):
        cols = pl.ds(pl.multiple_of(core * 256, 256), half)
        product = rows_product(norm1[...], gqkv[:, cols]).astype(B16)
        product = product.reshape(members, 4, small, half)
        for member in range(members):
            g_attn[core, :, member * small : (member + 1) * small, :] = product[member]

    attn_weights(links.other)
    for k in range(4):
        sum_attn.hand(k)

    def norm1_block(index, carry):
        member = in_order(index)
        at = member_rows(member)

        @pl.when(index == 3)
        def _():
            ring_gn1.send_ready()

        back = transposed_product(
            gqkv[at, : 3 * span], w_all[...].reshape(width, 640)[:, : 3 * span]
        )
        gn1[member] = back.astype(B16)
        rowsum[0:1, :] += jnp.sum(back * normed1[at, :], axis=0, keepdims=True)
        rowsum[1:2, :] += jnp.sum(back, axis=0, keepdims=True)

        @pl.when(index == 0)
        def _():
            ring_gn1.send_far()

        return carry

    lax.fori_loop(0, 4, norm1_block, 0)
    ring_gn1.send_summed()
    zsum[z] = rowsum[...]
    z_sums = [links.copy(zsum.at[z], zsum.at[z], links.to_z(s)) for s in (1, 3, 2)]
    for transfer in z_sums:
        transfer.start()
    attn_weights(links.core)
    sum_attn.merge(0)
    sum_attn.four.send_far()
    sum_attn.merge(1)
    sum_attn.merge(2)
    sum_attn.four.send_ready()
    gather_mlp.x_core.arrived()
    gather_mlp.y_core.arrived()
    gather_mlp.d_core.arrived()
    sum_attn.merge(3)
    sum_attn.four.send_summed()
    for transfer in z_sums:
        transfer.arrived()
    index = lax.broadcasted_iota(jnp.int32, rowsum.shape, 0)
    value = zsum[0] + zsum[1] + zsum[2] + zsum[3]
    value = jnp.where(index < 6, value, zsum[z])
    ssum[0] = value
    steps = [
        links.copy(ssum.at[k], bsum.at[k], device)
        for k, device in enumerate((links.to_core, links.to_x, links.to_y))
    ]
    steps[0].start()

    grad_norm1 = ring_gn1.total()
    _, normed, inv_std = layer_norm(x_all[z].astype(F32), one, zero_shift)
    input_grad[...] = gm_own[...] + norm_backward(grad_norm1, gain_one, normed, inv_std)

    steps[0].arrived()
    ssum[1] = ssum[0] + bsum[0]
    steps[1].start()
    total = sum_attn.four.total().astype(B16)
    h_attn[links.core, links.chip, span:, :] = total[span:]
    qkv_piece[...] = total[:span].reshape(members, small, half)
    own = pl.ds(pl.multiple_of(small * z, 16), small)
    h_attn[links.core, links.chip, own, :] = qkv_piece[z]
    for transfer in spread_qkv:
        transfer.start()
    steps[1].arrived()
    ssum[2] = ssum[1] + bsum[1]
    steps[2].start()
    for transfer in spread_qkv:
        transfer.arrived()
    gather_attn.start()
    steps[2].arrived()
    sums[...] = ssum[2] + bsum[2]
    gather_attn.forward()
    gather_attn.own_core.arrived()
    gather_mlp.own_core.arrived()
    gather_attn.hand_near()
    gather_attn.hand_far()
    gather_attn.x_core.arrived()
    gather_attn.y_core.arrived()
    gather_attn.d_core.arrived()


def backward_kernel(*refs):
    send_sem, recv_sem = refs[-2:]
    links = Links(send_sem, recv_sem)
    backward_phase(links, *refs[:-2])
    links.drain()


def forward_call(ids, x, cot, qkvw, fcw, projw, vec, qvbias):
    rows, width = x.shape
    span = qkvw.shape[0]
    hidden = fcw.shape[1] // 4
    group = 4 * rows

    def shape(dims, dtype=B16):
        return jax.ShapeDtypeStruct(dims, dtype)

    outs = (
        shape((span, group)),
        shape((8, group), F32),
        shape((span // HEAD, group, 4 * HEAD)),
        shape((2, 4, group, 2 * span)),
        shape((4, rows, width)),
        shape((4, span, 640)),
        shape((4, rows, width)),
        shape((4, span, hidden)),
        shape((4, span, width)),
        shape((4,) + vec.shape),
        shape((group, width)),
    )
    return pl.pallas_call(
        forward_kernel,
        out_shape=outs,
        in_specs=[pl.BlockSpec(memory_space=SMEM)] + [pl.BlockSpec(memory_space=VMEM)] * 7,
        out_specs=(pl.BlockSpec(memory_space=VMEM),) * len(outs),
        scratch_shapes=[
            VMEM((4, span, 640), B16),
            VMEM((4, span, hidden), B16),
            VMEM((8, group // 2), F32),
            VMEM((8, group // 2), F32),
            VMEM((span, group // 2), F32),
            VMEM((2, 8, group // 2), F32),
            VMEM((2, 8, group // 2), F32),
            VMEM((2, span, group // 2), F32),
            pltpu.SemaphoreType.DMA((48,)),
            pltpu.SemaphoreType.DMA((48,)),
        ],
        compiler_params=pltpu.CompilerParams(
            collective_id=0, has_side_effects=True, vmem_limit_bytes=56 << 20
        ),
        name="forward",
    )(ids, x, cot, qkvw, fcw, projw, vec, qvbias)


def backward_call(*args):
    ids, attn_t, lse, qm, kv, x_all, w_all, cot_all, fc_all, proj_all, vec_all, norm1, projw, outw, fcb = args
    members, rows, width = x_all.shape
    span = attn_t.shape[0]
    group = members * rows
    block = group // 2
    heads = span // HEAD
    half = width // 2
    small = span // 4
    mlp_rows, attn_rows = 2 * span, span + small

    def shape(dims, dtype=B16):
        return jax.ShapeDtypeStruct(dims, dtype)

    def summed(rows_of, cols):
        return [
            VMEM((4, rows_of, cols), B16),
            VMEM((rows_of, cols), B16),
            VMEM((2, rows_of, cols), B16),
        ]

    def ring():
        return [
            VMEM((members, rows, width), B16),
            VMEM((rows, width), B16),
            VMEM((2, rows, width), B16),
        ]

    outs = (
        shape((rows, width), F32),
        shape((rows, width), F32),
        shape((2, 4, mlp_rows, half)),
        shape((2, 4, attn_rows, half)),
        shape((8, width), F32),
    )
    scratch = (
        [
            VMEM((members, span, group), B16),
            VMEM((group, width), F32),
            VMEM((group, width), B16),
            VMEM((group, width), B16),
            VMEM((group, width), B16),
        ]
        + ring()
        + ring()
        + ring()
        + [
            VMEM((members, rows, width), B16),
            VMEM((rows, width), F32),
            VMEM((rows, width), F32),
            VMEM((group, width), F32),
            VMEM((2, 4, group, 2 * span), B16),
        ]
        + summed(group, 2 * span)
        + [VMEM((2, 4, mlp_rows, half), B16)]
        + summed(mlp_rows, half)
        + [VMEM((2, 4, attn_rows, half), B16)]
        + summed(attn_rows, half)
        + [
            VMEM((members, small, half), B16),
            VMEM((members, small, half), B16),
            VMEM((heads, group, 4 * HEAD), B16),
            VMEM((8, group), F32),
            VMEM((2, span, block), F32),
            VMEM((group, 640), B16),
            VMEM((members, 8, width), F32),
            VMEM((3, 8, width), F32),
            VMEM((3, 8, width), F32),
            VMEM((8, width), F32),
            pltpu.SemaphoreType.DMA((128,)),
            pltpu.SemaphoreType.DMA((128,)),
        ]
    )
    return pl.pallas_call(
        backward_kernel,
        out_shape=outs,
        in_specs=[pl.BlockSpec(memory_space=SMEM)] + [pl.BlockSpec(memory_space=VMEM)] * (len(args) - 1),
        out_specs=(pl.BlockSpec(memory_space=VMEM),) * len(outs),
        scratch_shapes=scratch,
        compiler_params=pltpu.CompilerParams(
            collective_id=1, has_side_effects=True, vmem_limit_bytes=60 << 20
        ),
        name="backward",
    )(*args)


def head_shards(
    block_input,
    positions,
    norm1_gain,
    norm1_bias,
    qkv_weight,
    query_bias,
    value_bias,
    proj_weight,
    proj_bias,
    norm2_gain,
    norm2_bias,
    fc_weight,
    fc_bias,
    out_weight,
    out_bias,
    cotangent,
):
    rows, width = block_input.shape
    span = width // 4
    half = width // 2
    small = span // 4
    member = lax.axis_index("fsdp")
    vec = jnp.stack([norm1_gain, norm1_bias, proj_bias, norm2_gain, norm2_bias, out_bias])
    vec = jnp.pad(vec, ((0, 10), (0, 256 - span)))
    ids = positions.reshape(-1, 2 * rows)[:, 0] // (2 * rows)
    attn_t, lse, qm, kv_all, x_all, w_all, cot_all, fc_all, proj_all, vec_all, norm1 = forward_call(
        ids,
        block_input,
        cotangent,
        qkv_weight,
        fc_weight,
        proj_weight,
        vec,
        jnp.stack([query_bias, value_bias]),
    )
    block_output, input_grad, h_mlp, h_attn, sums = backward_call(
        ids, attn_t, lse, qm, kv_all, x_all, w_all, cot_all, fc_all, proj_all, vec_all, norm1,
        proj_weight, out_weight, fc_bias[None],
    )
    out_grad = h_mlp[:, :, :span].transpose(1, 2, 0, 3).reshape(width, width).astype(F32)
    fc_grad = (
        h_mlp[:, :, span:]
        .reshape(2, 4, 4, small, half)
        .transpose(1, 3, 2, 0, 4)
        .reshape(span, 4 * width)
        .astype(F32)
    )
    proj_grad = h_attn[:, :, span:].transpose(1, 2, 0, 3).reshape(span, width).astype(F32)
    pieces = h_attn[:, :, :span].reshape(2, 4, 4, small, half)
    pieces = jnp.concatenate([pieces[0], pieces[1][..., 128:320]], axis=-1)
    qkv_grad = (
        pieces.reshape(4, 4, small, 3, span)
        .transpose(0, 2, 3, 1, 4)
        .reshape(span, 3 * width)
        .astype(F32)
    )
    own = lax.dynamic_slice_in_dim(sums[:6], member * span, span, axis=1)
    return (
        block_output,
        input_grad,
        own[0],
        own[1],
        qkv_grad,
        sums[6, :span],
        sums[6, span : 2 * span],
        proj_grad,
        own[2],
        own[3],
        own[4],
        fc_grad,
        sums[7],
        out_grad,
        own[5],
    )


def solution(mesh):
    sharded = P(("ctx", "fsdp"), None)
    rows, vector = P("fsdp", None), P("fsdp")
    in_specs = (
        sharded, P(), vector, vector, rows, vector, vector, rows, vector, vector, vector, rows, vector, rows,
        vector, sharded,
    )
    out_specs = (
        sharded, sharded, vector, vector, rows, vector, vector, rows, vector, vector, vector, rows, vector, rows,
        vector,
    )
    body = head_shards if dict(mesh.shape) == {"ctx": 8, "fsdp": 4} else shards
    return jax.shard_map(body, mesh=mesh, in_specs=in_specs, out_specs=out_specs, check_vma=False)
```

```python
import functools

import jax
import jax.numpy as jnp
from jax import lax
from jax.experimental import pallas as pl
from jax.experimental.pallas import tpu as pltpu
from jax.sharding import PartitionSpec as P

HEADS = 12
HEAD = 64


EPSILON = 1e-05
NEG_FILL = -1e30
GELU_C = 0.7978845608028654
GELU_K = 0.044715


def passed_along(block, axis, distance):
    devices = range(lax.axis_size(axis))
    route = [((i - distance) % len(devices), i) for i in devices]
    return lax.ppermute(block, axis, route)


def layer_norm(values_in, gain, shift):
    row_mean = jnp.mean(values_in, axis=-1, keepdims=True)
    centered = values_in - row_mean
    variance = jnp.mean(centered * centered, axis=-1, keepdims=True)
    inv_std = lax.rsqrt(variance + EPSILON)
    normed = centered * inv_std
    return (normed * gain.astype(jnp.float32) + shift.astype(jnp.float32), normed, inv_std)


def norm_backward(grad_norm, gain, normed, inv_std):
    scaled = grad_norm * gain.astype(jnp.float32)
    scaled_mean = jnp.mean(scaled, axis=-1, keepdims=True)
    cross_mean = jnp.mean(scaled * normed, axis=-1, keepdims=True)
    return inv_std * (scaled - scaled_mean - normed * cross_mean)


def gelu_forward(pre_act):
    cubed = pre_act * pre_act * pre_act
    return 0.5 * pre_act * (1.0 + jnp.tanh(GELU_C * (pre_act + GELU_K * cubed)))


def gelu_slope(pre_act):
    cubed = pre_act * pre_act * pre_act
    tanh_value = jnp.tanh(GELU_C * (pre_act + GELU_K * cubed))
    return 0.5 * (1.0 + tanh_value) + 0.5 * pre_act * (1.0 - tanh_value * tanh_value) * GELU_C * (
        1.0 + 3.0 * GELU_K * pre_act * pre_act
    )


def rows_product(left, right):
    return lax.dot_general(
        left, right, (((0,), (0,)), ((), ())), preferred_element_type=jnp.float32
    )


def transposed_product(left, right):
    return lax.dot_general(
        left, right, (((1,), (1,)), ((), ())), preferred_element_type=jnp.float32
    )


def split_heads(matrix):
    return matrix.reshape(matrix.shape[0], HEADS, HEAD)


def masked_scores(query, query_pos, keys, key_pos):
    scores = jnp.einsum(
        "rhd,khd->hrk", split_heads(query), split_heads(keys), preferred_element_type=jnp.float32
    ) * HEAD ** (-0.5)
    allowed = (key_pos[None, :] <= query_pos[:, None])[None]
    return (jnp.where(allowed, scores, NEG_FILL), allowed)


def attend_block(carried, query, query_pos, keys, values, key_pos):
    weighted, run_max, row_total = carried
    scores, allowed = masked_scores(query, query_pos, keys, key_pos)
    new_max = jnp.maximum(run_max, jnp.max(scores, axis=-1))
    weights = jnp.where(allowed, jnp.exp(scores - new_max[..., None]), 0.0)
    factor = jnp.exp(run_max - new_max)
    row_total = row_total * factor + jnp.sum(weights, axis=-1)
    update = jnp.einsum(
        "hrk,khd->rhd",
        weights,
        split_heads(values).astype(jnp.float32),
        precision=lax.Precision.HIGHEST,
        preferred_element_type=jnp.float32,
    )
    weighted = weighted * factor.T[:, :, None] + update
    return (weighted, new_max, row_total)


def attend_tile(carried, query, query_pos, keys, values, key_pos):
    half_rows = keys.shape[0] // 2
    latest = jnp.max(query_pos)
    for half_index in range(2):
        first_row = half_index * half_rows
        part_keys = keys[first_row : first_row + half_rows]
        part_values = values[first_row : first_row + half_rows]
        part_pos = key_pos[first_row : first_row + half_rows]

        def keep_state(state_in, block_keys, block_values, block_pos):
            return state_in

        def update_state(state_in, block_keys, block_values, block_pos):
            return attend_block(state_in, query, query_pos, block_keys, block_values, block_pos)

        carried = lax.cond(
            jnp.min(part_pos) > latest,
            keep_state,
            update_state,
            carried,
            part_keys,
            part_values,
            part_pos,
        )
    return carried


def block_grads(query, grad_attn, row_lse, row_delta, query_pos, keys, values, key_pos):
    scores, allowed = masked_scores(query, query_pos, keys, key_pos)
    probs = jnp.where(allowed, jnp.exp(scores - row_lse[..., None]), 0.0)
    grad_heads = split_heads(grad_attn)
    grad_values = jnp.einsum(
        "hrk,rhd->khd", probs.astype(jnp.bfloat16), grad_heads, preferred_element_type=jnp.float32
    )
    grad_probs = jnp.einsum(
        "rhd,khd->hrk", grad_heads, split_heads(values), preferred_element_type=jnp.float32
    )
    grad_scores = (probs * (grad_probs - row_delta[..., None])).astype(jnp.bfloat16)
    scale = HEAD ** (-0.5)
    grad_query = (
        jnp.einsum(
            "hrk,khd->rhd", grad_scores, split_heads(keys), preferred_element_type=jnp.float32
        )
        * scale
    )
    grad_keys = (
        jnp.einsum(
            "hrk,rhd->khd", grad_scores, split_heads(query), preferred_element_type=jnp.float32
        )
        * scale
    )
    key_rows = keys.shape[0]
    return (grad_query, grad_keys.reshape(key_rows, -1), grad_values.reshape(key_rows, -1))


def tile_grads(query, grad_attn, row_lse, row_delta, query_pos, keys, values, key_pos):
    half_rows = keys.shape[0] // 2
    key_width = keys.shape[1]
    latest = jnp.max(query_pos)
    query_total = jnp.zeros((query.shape[0], HEADS, HEAD), jnp.float32)
    key_parts = []
    value_parts = []
    for half_index in range(2):
        first_row = half_index * half_rows
        part_keys = keys[first_row : first_row + half_rows]
        part_values = values[first_row : first_row + half_rows]
        part_pos = key_pos[first_row : first_row + half_rows]

        def skipped(block_keys, block_values, block_pos):
            return (
                jnp.zeros((query.shape[0], HEADS, HEAD), jnp.float32),
                jnp.zeros((half_rows, key_width), jnp.float32),
                jnp.zeros((half_rows, key_width), jnp.float32),
            )

        def computed(block_keys, block_values, block_pos):
            return block_grads(
                query, grad_attn, row_lse, row_delta, query_pos, block_keys, block_values, block_pos
            )

        step_query, step_keys, step_values = lax.cond(
            jnp.min(part_pos) > latest, skipped, computed, part_keys, part_values, part_pos
        )
        query_total = query_total + step_query
        key_parts.append(step_keys)
        value_parts.append(step_values)
    return (query_total, jnp.concatenate(key_parts, axis=0), jnp.concatenate(value_parts, axis=0))


def shards(
    block_input,
    positions,
    norm1_gain,
    norm1_bias,
    qkv_weight,
    query_bias,
    value_bias,
    proj_weight,
    proj_bias,
    norm2_gain,
    norm2_bias,
    fc_weight,
    fc_bias,
    out_weight,
    out_bias,
    cotangent,
):
    rows = block_input.shape[0]
    width = block_input.shape[1]
    ctx_size = lax.axis_size("ctx")
    shard_count = lax.axis_size("fsdp")
    ctx_index = lax.axis_index("ctx")
    shard_index = lax.axis_index("fsdp")
    group_rows = rows * shard_count

    def key_positions(source):
        return lax.dynamic_slice_in_dim(positions, source * group_rows, group_rows)

    gain_one, shift_one, qkv_full, qbias_full, vbias_full, proj_full, pbias_full = (
        lax.all_gather(norm1_gain, "fsdp", axis=0, tiled=True),
        lax.all_gather(norm1_bias, "fsdp", axis=0, tiled=True),
        lax.all_gather(qkv_weight, "fsdp", axis=0, tiled=True),
        lax.all_gather(query_bias, "fsdp", axis=0, tiled=True),
        lax.all_gather(value_bias, "fsdp", axis=0, tiled=True),
        lax.all_gather(proj_weight, "fsdp", axis=0, tiled=True),
        lax.all_gather(proj_bias, "fsdp", axis=0, tiled=True),
    )
    gain_two, shift_two, fc_full, fbias_full, out_full, obias_full = (
        lax.all_gather(norm2_gain, "fsdp", axis=0, tiled=True),
        lax.all_gather(norm2_bias, "fsdp", axis=0, tiled=True),
        lax.all_gather(fc_weight, "fsdp", axis=0, tiled=True),
        lax.all_gather(fc_bias, "fsdp", axis=0, tiled=True),
        lax.all_gather(out_weight, "fsdp", axis=0, tiled=True),
        lax.all_gather(out_bias, "fsdp", axis=0, tiled=True),
    )
    residual = block_input.astype(jnp.float32)
    normed1_out, normed1, inv_std1 = layer_norm(residual, gain_one, shift_one)
    norm1 = normed1_out.astype(jnp.bfloat16)
    qkv = jnp.dot(norm1, qkv_full, preferred_element_type=jnp.float32)
    query = (qkv[:, :width] + qbias_full.astype(jnp.float32)).astype(jnp.bfloat16)
    keys = qkv[:, width : 2 * width].astype(jnp.bfloat16)
    values = (qkv[:, 2 * width :] + vbias_full.astype(jnp.float32)).astype(jnp.bfloat16)
    group_keys, group_values = (
        lax.all_gather(keys, "fsdp", axis=0, tiled=True),
        lax.all_gather(values, "fsdp", axis=0, tiled=True),
    )
    own_qpos = lax.dynamic_slice_in_dim(
        positions, (ctx_index * shard_count + shard_index) * rows, rows
    )
    own_kpos = key_positions(ctx_index)
    initial = (
        jnp.zeros((rows, HEADS, HEAD), jnp.float32),
        jnp.full((HEADS, rows), NEG_FILL, jnp.float32),
        jnp.zeros((HEADS, rows), jnp.float32),
    )
    carried = attend_tile(initial, query, own_qpos, group_keys, group_values, own_kpos)

    def forward_hop(hop_index, loop_carry):
        state_now, cycle_keys, cycle_values = loop_carry
        cycle_keys, cycle_values = passed_along((cycle_keys, cycle_values), "ctx", 1)
        source = (ctx_index - hop_index) % ctx_size
        state_now = attend_tile(
            state_now, query, own_qpos, cycle_keys, cycle_values, key_positions(source)
        )
        return (state_now, cycle_keys, cycle_values)

    result = lax.fori_loop(1, ctx_size, forward_hop, (carried, group_keys, group_values))
    carried = result[0]
    weighted, run_max, row_total = carried
    attn = (weighted / row_total.T[:, :, None]).reshape(rows, width).astype(jnp.bfloat16)
    row_lse = run_max + jnp.log(row_total)
    middle = (
        residual
        + jnp.dot(attn, proj_full, preferred_element_type=jnp.float32)
        + pbias_full.astype(jnp.float32)
    )
    normed2_out, normed2, inv_std2 = layer_norm(middle, gain_two, shift_two)
    norm2 = normed2_out.astype(jnp.bfloat16)
    pre_act = jnp.dot(norm2, fc_full, preferred_element_type=jnp.float32) + fbias_full.astype(
        jnp.float32
    )
    act = gelu_forward(pre_act).astype(jnp.bfloat16)
    block_output = (
        middle
        + jnp.dot(act, out_full, preferred_element_type=jnp.float32)
        + obias_full.astype(jnp.float32)
    )
    grad_out = cotangent.astype(jnp.float32)
    out_weight_grad = rows_product(act, cotangent)
    out_bias_grad = jnp.sum(grad_out, axis=0)
    grad_act = transposed_product(cotangent, out_full)
    grad_pre = grad_act * gelu_slope(pre_act)
    fc_bias_grad = jnp.sum(grad_pre, axis=0)
    grad_pre_half = grad_pre.astype(jnp.bfloat16)
    fc_weight_grad = rows_product(norm2, grad_pre_half)
    grad_norm2 = transposed_product(grad_pre_half, fc_full)
    norm2_gain_grad = jnp.sum(grad_norm2 * normed2, axis=0)
    norm2_bias_grad = jnp.sum(grad_norm2, axis=0)
    grad_middle = grad_out + norm_backward(grad_norm2, gain_two, normed2, inv_std2)
    mlp_shares = (
        lax.psum_scatter(norm2_gain_grad, "fsdp", scatter_dimension=0, tiled=True),
        lax.psum_scatter(norm2_bias_grad, "fsdp", scatter_dimension=0, tiled=True),
        lax.psum_scatter(fc_weight_grad, "fsdp", scatter_dimension=0, tiled=True),
        lax.psum_scatter(fc_bias_grad, "fsdp", scatter_dimension=0, tiled=True),
        lax.psum_scatter(out_weight_grad, "fsdp", scatter_dimension=0, tiled=True),
        lax.psum_scatter(out_bias_grad, "fsdp", scatter_dimension=0, tiled=True),
    )
    proj_bias_grad = jnp.sum(grad_middle, axis=0)
    grad_middle_half = grad_middle.astype(jnp.bfloat16)
    proj_weight_grad = rows_product(attn, grad_middle_half)
    grad_attn = transposed_product(grad_middle_half, proj_full).astype(jnp.bfloat16)
    row_delta = jnp.sum(
        split_heads(grad_attn).astype(jnp.float32) * split_heads(attn).astype(jnp.float32), axis=-1
    ).T
    grad_query, grad_keys, grad_values = tile_grads(
        query, grad_attn, row_lse, row_delta, own_qpos, group_keys, group_values, own_kpos
    )

    def pass_key_grads(key_grads):
        return passed_along((key_grads[0], key_grads[1]), "ctx", 1)

    def backward_hop(hop_index, loop_carry):
        query_sum, key_grads, cycle_keys, cycle_values = loop_carry
        cycle_keys, cycle_values = passed_along((cycle_keys, cycle_values), "ctx", 1)
        key_grads = pass_key_grads(key_grads)
        source = (ctx_index - hop_index) % ctx_size
        step_query, step_keys, step_values = tile_grads(
            query,
            grad_attn,
            row_lse,
            row_delta,
            own_qpos,
            cycle_keys,
            cycle_values,
            key_positions(source),
        )
        return (
            query_sum + step_query,
            (key_grads[0] + step_keys, key_grads[1] + step_values),
            cycle_keys,
            cycle_values,
        )

    result = lax.fori_loop(
        1, ctx_size, backward_hop, (grad_query, (grad_keys, grad_values), group_keys, group_values)
    )
    grad_query = result[0]
    key_grads = pass_key_grads(result[1])
    own_key_grad, own_value_grad = (
        lax.psum_scatter(key_grads[0], "fsdp", scatter_dimension=0, tiled=True),
        lax.psum_scatter(key_grads[1], "fsdp", scatter_dimension=0, tiled=True),
    )
    grad_query_rows = grad_query.reshape(rows, width)
    query_bias_grad = jnp.sum(grad_query_rows, axis=0)
    value_bias_grad = jnp.sum(own_value_grad, axis=0)
    grad_qkv = jnp.concatenate([grad_query_rows, own_key_grad, own_value_grad], axis=1).astype(
        jnp.bfloat16
    )
    qkv_weight_grad = rows_product(norm1, grad_qkv)
    grad_norm1 = transposed_product(grad_qkv, qkv_full)
    norm1_gain_grad = jnp.sum(grad_norm1 * normed1, axis=0)
    norm1_bias_grad = jnp.sum(grad_norm1, axis=0)
    input_grad = grad_middle + norm_backward(grad_norm1, gain_one, normed1, inv_std1)
    attn_shares = (
        lax.psum_scatter(norm1_gain_grad, "fsdp", scatter_dimension=0, tiled=True),
        lax.psum_scatter(norm1_bias_grad, "fsdp", scatter_dimension=0, tiled=True),
        lax.psum_scatter(qkv_weight_grad, "fsdp", scatter_dimension=0, tiled=True),
        lax.psum_scatter(query_bias_grad, "fsdp", scatter_dimension=0, tiled=True),
        lax.psum_scatter(value_bias_grad, "fsdp", scatter_dimension=0, tiled=True),
        lax.psum_scatter(proj_weight_grad, "fsdp", scatter_dimension=0, tiled=True),
        lax.psum_scatter(proj_bias_grad, "fsdp", scatter_dimension=0, tiled=True),
    )
    totals = lax.psum(
        (
            attn_shares[0],
            attn_shares[1],
            attn_shares[2],
            attn_shares[3],
            attn_shares[4],
            attn_shares[5],
            attn_shares[6],
            mlp_shares[0],
            mlp_shares[1],
            mlp_shares[2],
            mlp_shares[3],
            mlp_shares[4],
            mlp_shares[5],
        ),
        "ctx",
    )
    return (
        block_output,
        input_grad,
        totals[0],
        totals[1],
        totals[2],
        totals[3],
        totals[4],
        totals[5],
        totals[6],
        totals[7],
        totals[8],
        totals[9],
        totals[10],
        totals[11],
        totals[12],
    )


MESH = pl.DeviceIdType.MESH
SMEM = pltpu.SMEM
VMEM = pltpu.VMEM
F32 = jnp.float32
B16 = jnp.bfloat16


class Transfer:
    def __init__(self, links, src, dst, device):
        self.args = dict(
            src_ref=src,
            dst_ref=dst,
            send_sem=links.send_sem.at[links.count],
            recv_sem=links.recv_sem.at[links.count],
            device_id=device,
            device_id_type=MESH,
        )
        links.count += 1
        links.sent.append(self)

    def start(self):
        pltpu.make_async_remote_copy(**self.args).start()
        return self

    def arrived(self):
        pltpu.make_async_remote_copy(**self.args).wait_recv()

    def left(self):
        pltpu.make_async_remote_copy(**self.args).wait_send()


class Links:
    def __init__(self, send_sem, recv_sem):
        self.send_sem, self.recv_sem = send_sem, recv_sem
        self.count = 0
        self.sent = []
        ctx = lax.axis_index("ctx")
        self.ctx = ctx
        self.z = lax.axis_index("fsdp")
        self.core = lax.rem(ctx, 2)
        self.chip = lax.div(ctx, 2)
        x, y = lax.rem(self.chip, 2), lax.div(self.chip, 2)
        self.chip_x = self.chip + 1 - 2 * x
        self.chip_y = self.chip + 2 - 4 * y
        self.chip_d = 3 - self.chip
        self.other = 1 - self.core
        self.to_core = {"ctx": self.chip * 2 + self.other}
        self.to_x = {"ctx": self.chip_x * 2 + self.core}
        self.to_y = {"ctx": self.chip_y * 2 + self.core}

    def zed(self, step):
        return lax.rem(self.z + step, 4)

    def to_z(self, step):
        return {"fsdp": self.zed(step)}

    def peers(self):
        return [self.to_core, self.to_x, self.to_y, self.to_z(1), self.to_z(2), self.to_z(3)]

    def copy(self, src, dst, device):
        return Transfer(self, src, dst, device)

    def greet(self):
        barrier = pltpu.get_barrier_semaphore()
        for device in self.peers():
            pl.semaphore_signal(barrier, inc=1, device_id=device, device_id_type=MESH)

    def greeted(self):
        pl.semaphore_wait(pltpu.get_barrier_semaphore(), 6)

    def drain(self):
        for transfer in self.sent:
            transfer.left()


class RingGather:
    def __init__(self, links, buf):
        half = buf.shape[1] // 2
        own, left, right = links.z, links.zed(3), links.zed(1)

        def piece(member, part):
            return buf.at[member, part * half : (part + 1) * half]

        def move(member, part, step):
            return links.copy(piece(member, part), piece(member, part), links.to_z(step))

        self.first = [move(own, 0, 1), move(own, 1, 3), move(own, 1, 1), move(own, 0, 3)]
        self.second = [move(left, 0, 1), move(right, 1, 3)]

    def start(self):
        for transfer in self.first:
            transfer.start()

    def forward(self):
        for transfer, onward in zip(self.first[:2], self.second):
            transfer.arrived()
            onward.start()

    def near(self):
        for transfer in self.first[2:]:
            transfer.arrived()

    def far(self):
        for transfer in self.second:
            transfer.arrived()


class Shared:
    def __init__(self, links, source, target):
        small, half = target.shape[1] // 4, target.shape[2] // 2
        cols = pl.ds(pl.multiple_of(links.core * half, 128), half)

        def rows(chip):
            return pl.ds(pl.multiple_of(chip * small, 16), small)

        def move(chip, part, device):
            ref = target.at[2 * part : 2 * part + 2, rows(chip), cols]
            return links.copy(ref, ref, device)

        own = rows(links.chip)
        place = target.at[links.z, own, cols]
        place[...] = source(links.z, own)[...]
        self.cross = [
            links.copy(source(links.zed(step), own), place, links.to_z(step)) for step in (2, 1, 3)
        ]
        own, x, y = links.chip, links.chip_x, links.chip_y
        self.near = [
            move(own, 0, links.to_x),
            move(own, 1, links.to_y),
            move(own, 1, links.to_x),
            move(own, 0, links.to_y),
        ]
        self.onward = [move(x, 0, links.to_y), move(y, 1, links.to_x)]
        ref = target.at[:, :, cols]
        self.hand = links.copy(ref, ref, links.to_core)

    def start(self):
        for transfer in self.cross:
            transfer.start()

    def gather(self):
        for transfer in self.cross:
            transfer.arrived()
        for transfer in self.near:
            transfer.start()

    def forward(self):
        for transfer, onward in zip(self.near[:2], self.onward):
            transfer.arrived()
            onward.start()

    def give(self):
        for transfer in self.near[2:] + self.onward:
            transfer.arrived()
        self.hand.start()

    def finish(self):
        self.hand.arrived()


class ContextGather:
    def __init__(self, links, buf):
        half = buf.shape[2] // 2

        def move(chip, part, device):
            rows = slice(None) if part is None else slice(part * half, (part + 1) * half)
            ref = buf.at[links.core, chip, rows]
            return links.copy(ref, ref, device)

        own, x, y, d = links.chip, links.chip_x, links.chip_y, links.chip_d
        self.own_core = move(own, None, links.to_core)
        self.x_parts = [move(own, 0, links.to_x), move(own, 1, links.to_x)]
        self.y_parts = [move(own, 1, links.to_y), move(own, 0, links.to_y)]
        self.onward = [move(x, 0, links.to_y), move(y, 1, links.to_x)]
        self.x_core = move(x, None, links.to_core)
        self.y_core = move(y, None, links.to_core)
        self.d_core = move(d, None, links.to_core)

    def start(self):
        for transfer in (
            self.x_parts[0],
            self.y_parts[0],
            self.own_core,
            self.x_parts[1],
            self.y_parts[1],
        ):
            transfer.start()

    def forward(self):
        self.x_parts[0].arrived()
        self.onward[0].start()
        self.y_parts[0].arrived()
        self.onward[1].start()

    def hand_near(self):
        self.x_parts[1].arrived()
        self.x_core.start()
        self.y_parts[1].arrived()
        self.y_core.start()

    def hand_far(self):
        self.onward[0].arrived()
        self.onward[1].arrived()
        self.d_core.start()


def chosen(flag, shape):
    return jnp.full(shape, flag, jnp.int32) == 1


def masked_heads(value, first, width):
    rows, span = value.shape
    pieces = []
    if first > 0:
        pieces.append(jnp.zeros((rows, first), value.dtype))
    pieces.append(value)
    if first + span < width:
        pieces.append(jnp.zeros((rows, width - first - span), value.dtype))
    wide = jnp.concatenate(pieces, axis=1) if len(pieces) > 1 else value
    head = (lax.broadcasted_iota(jnp.int32, (rows, width), 1) - first + HEAD) // HEAD - 1
    return [
        jnp.where(head == index, wide.astype(F32), 0.0).astype(value.dtype)
        for index in range(span // HEAD)
    ]


def soft_step(scores, old_max, old_sum):
    new_max = jnp.maximum(old_max, jnp.max(scores, axis=0, keepdims=True))
    weights = jnp.exp(scores - new_max)
    factor = jnp.exp(old_max - new_max)
    new_sum = old_sum * factor + jnp.sum(weights, axis=0, keepdims=True)
    return weights.astype(B16), factor, new_max, new_sum


def forward_phase(
    links, ids, x, cot, qkvw, fcw, projw, v0, v1, v2, v3, v4, v5, qbias, vbias,
    attn_t, lse, qm, kv, x_all, w_all, cot_all, fc_all, proj_all, vec_all, norm1, normed1,
    stage, max_h, sum_h, acc_h, max_x, sum_x, acc_x,
):
    rows = x.shape[0]
    span = qkvw.shape[0]
    block = 2 * rows
    heads = span // HEAD
    z = links.z
    links.greet()
    x_all[z] = x[...]
    cot_all[z] = cot[...]
    own_vectors = jnp.concatenate(
        [v[...].astype(F32).reshape(1, span) for v in (v0, v1, v2, v3, v4, v5)]
        + [jnp.zeros((10, span), F32)],
        axis=0,
    )
    vec_all[z, :, :span] = own_vectors.astype(B16)
    for member in range(4):
        stage[member, :, : 3 * span] = jnp.concatenate(
            [qkvw[:, t * 4 * span + member * span : t * 4 * span + (member + 1) * span] for t in range(3)],
            axis=1,
        )

    vectors = [
        links.copy(vec_all.at[z], vec_all.at[z], links.to_z(step)) for step in (1, 3, 2)
    ]
    inputs = RingGather(links, x_all)
    half = cot.shape[1] // 2

    def own_cols(first):
        return pl.ds(pl.multiple_of(first + links.core * half, 128), half)

    weights = Shared(links, lambda member, at: stage.at[member, at, own_cols(0)], w_all)
    cots = RingGather(links, cot_all)
    fcs_in = Shared(links, lambda member, at: fcw.at[at, own_cols(member * 2 * half)], fc_all)
    projs = Shared(links, lambda member, at: projw.at[at, own_cols(0)], proj_all)
    context = ContextGather(links, kv)

    links.greeted()
    for transfer in vectors:
        transfer.start()
    weights.start()
    inputs.start()
    for transfer in vectors:
        transfer.arrived()

    gain = jnp.concatenate([vec_all[m, 0:1, :span] for m in range(4)], axis=1).astype(F32)
    shift = jnp.concatenate([vec_all[m, 1:2, :span] for m in range(4)], axis=1).astype(F32)

    def normalise(member):
        shifted, normed, _ = layer_norm(x_all[member].astype(F32), gain, shift)
        at = pl.ds(pl.multiple_of(member * rows, rows), rows)
        norm1[at, :] = shifted.astype(B16)
        normed1[at, :] = normed

    normalise(z)
    inputs.forward()
    weights.gather()
    fcs_in.start()
    projs.start()
    inputs.near()
    normalise(links.zed(1))
    normalise(links.zed(3))
    weights.forward()
    inputs.far()
    cots.start()
    normalise(links.zed(2))
    weights.give()
    weights.finish()

    matrix = w_all[...].reshape(4 * span, w_all.shape[2])[:, : 3 * span]
    for part in range(2):
        at = slice(part * block, (part + 1) * block)
        product = jnp.dot(norm1[at, :], matrix, preferred_element_type=F32)
        query = (product[:, :span] + qbias[...].astype(F32).reshape(1, span)).astype(B16)
        query = query * jnp.asarray(HEAD**-0.5, B16)
        for head, lone in enumerate(masked_heads(query, 0, 4 * HEAD)):
            qm[head, at, :] = lone
        values = product[:, 2 * span :] + vbias[...].astype(F32).reshape(1, span)
        kv[links.core, links.chip, at, :] = jnp.concatenate(
            [product[:, span : 2 * span], values], axis=1
        ).astype(B16)
    context.start()

    own_block = ids[2 * links.ctx]
    keep = lax.broadcasted_iota(jnp.int32, (block, block), 0) <= lax.broadcasted_iota(
        jnp.int32, (block, block), 1
    )
    none = jnp.full((1, block), NEG_FILL, F32)
    zero = jnp.zeros((1, block), F32)

    def halves(core, chip, part):
        at = slice(part * block, (part + 1) * block)
        return kv[core, chip, at, : 4 * HEAD], kv[core, chip, at, 2 * HEAD :].T

    def value_rows(head):
        return slice((1 + head) * HEAD, (2 + head) * HEAD)

    def head_rows(head):
        return slice(head * HEAD, (head + 1) * HEAD)

    k_low, vt_low = halves(links.core, links.chip, 0)
    k_high, vt_high = halves(links.core, links.chip, 1)
    for head in range(heads):
        q_low, q_high = qm[head, :block, :], qm[head, block:, :]
        scores = jnp.where(keep, transposed_product(k_low, q_low), NEG_FILL)
        w, _, top, total = soft_step(scores, none, zero)
        max_x[0, head : head + 1, :] = top
        sum_x[0, head : head + 1, :] = total
        acc_x[0, head_rows(head), :] = jnp.dot(
            vt_low[value_rows(head)], w, preferred_element_type=F32
        )
        scores = transposed_product(k_low, q_high)
        w, _, top, total = soft_step(scores, none, zero)
        acc = jnp.dot(vt_low[value_rows(head)], w, preferred_element_type=F32)
        scores = jnp.where(keep, transposed_product(k_high, q_high), NEG_FILL)
        w, factor, top, total = soft_step(scores, top, total)
        max_h[head : head + 1, :] = top
        sum_h[head : head + 1, :] = total
        acc_h[head_rows(head), :] = acc * factor + jnp.dot(
            vt_high[value_rows(head)], w, preferred_element_type=F32
        )
    max_x[1] = jnp.full_like(max_h, NEG_FILL)
    sum_x[1] = jnp.zeros_like(sum_h)
    acc_x[1] = jnp.zeros_like(acc_h)

    def hop(index, carry):
        near = index < 3
        far = index >= 5
        core = jnp.where((index == 1) | (index == 2) | (index == 5), links.core, links.other)
        chip = jnp.where(
            index == 0,
            links.chip,
            jnp.where(far, links.chip_d, jnp.where(lax.rem(index, 2) == 1, links.chip_x, links.chip_y)),
        )

        @pl.when(index == 0)
        def _():
            context.own_core.arrived()
            context.forward()

        @pl.when(index == 1)
        def _():
            context.hand_near()
            cots.forward()

        @pl.when(index == 2)
        def _():
            fcs_in.gather()
            projs.gather()

        @pl.when(index == 3)
        def _():
            context.x_core.arrived()
            context.hand_far()

        @pl.when(index == 4)
        def _():
            context.y_core.arrived()
            cots.near()

        @pl.when(index == 5)
        def _():
            fcs_in.forward()
            projs.forward()

        @pl.when(index == 6)
        def _():
            context.d_core.arrived()

        block_id = ids[2 * (2 * chip + core)]
        low = (block_id < own_block).astype(jnp.int32)
        in_low = chosen(low, (1, block))
        kv_low = kv[core, chip, :block, :]
        kv_high = kv[core, chip, block:, :]
        kv_pick = jnp.where(chosen(low, kv_low.shape), kv_low, kv_high)
        q_mask = chosen(low, (block, 4 * HEAD))
        work = []
        for head in range(heads):
            scores = transposed_product(kv_low[:, : 4 * HEAD], qm[head, block:, :])
            work.append((scores, max_h[head : head + 1, :], sum_h[head : head + 1, :]))
        for head in range(heads):
            q_pick = jnp.where(q_mask, qm[head, :block, :], qm[head, block:, :])
            scores = transposed_product(kv_pick[:, : 4 * HEAD], q_pick)
            at = slice(head, head + 1)
            work.append(
                (
                    scores,
                    jnp.where(in_low, max_x[0, at, :], max_x[1, at, :]),
                    jnp.where(in_low, sum_x[0, at, :], sum_x[1, at, :]),
                )
            )
        done = [soft_step(*entry) for entry in work]
        vt = kv_low[:, 2 * HEAD :].T
        for head in range(heads):
            w, factor, top, total = done[head]
            max_h[head : head + 1, :] = top
            sum_h[head : head + 1, :] = total
            acc_h[head_rows(head), :] = acc_h[head_rows(head), :] * factor + jnp.dot(
                vt[value_rows(head)], w, preferred_element_type=F32
            )
        vt = kv_pick[:, 2 * HEAD :].T
        for head in range(heads):
            w, factor, top, total = done[heads + head]
            acc = jnp.where(in_low, acc_x[0, head_rows(head), :], acc_x[1, head_rows(head), :])
            acc = acc * factor + jnp.dot(
                vt[value_rows(head)], w, preferred_element_type=F32
            )
            for part in range(2):
                own = in_low if part == 0 else ~in_low
                max_x[part, head : head + 1, :] = jnp.where(own, top, max_x[part, head : head + 1, :])
                sum_x[part, head : head + 1, :] = jnp.where(
                    own, total, sum_x[part, head : head + 1, :]
                )
                acc_x[part, head_rows(head), :] = jnp.where(own, acc, acc_x[part, head_rows(head), :])
        return carry

    lax.fori_loop(0, 7, hop, 0)
    for head in range(heads):
        at = slice(head, head + 1)
        total = sum_x[0, at, :]
        attn_t[head_rows(head), :block] = (acc_x[0, head_rows(head), :] / total).astype(B16)
        lse[at, :block] = max_x[0, at, :] + jnp.log(total)
        top = jnp.maximum(max_h[at, :], max_x[1, at, :])
        left, right = jnp.exp(max_h[at, :] - top), jnp.exp(max_x[1, at, :] - top)
        total = sum_h[at, :] * left + sum_x[1, at, :] * right
        acc = acc_h[head_rows(head), :] * left + acc_x[1, head_rows(head), :] * right
        attn_t[head_rows(head), block:] = (acc / total).astype(B16)
        lse[at, block:] = top + jnp.log(total)
    return cots, fcs_in, projs


def parts_of(rows):
    first = (rows // 2 + 15) // 16 * 16
    return [slice(0, first), slice(first, rows)]


class FourSum:
    def __init__(self, links, parts, early, late, far, own, near):
        self.parts, self.early, self.late, self.own, self.near = parts, early, late, own, near
        self.cuts = parts_of(early.shape[0])
        self.far = [
            links.copy(parts.at[far, self.cuts[k]], early.at[self.cuts[k]], near[k][0]) for k in range(2)
        ]
        self.ready, self.summed = [], []
        for k, (device, part, added) in enumerate(near):
            for half, group in ((1 - added, self.ready), (added, self.summed)):
                cut = self.cuts[half]
                group.append(links.copy(parts.at[part, cut], late.at[k, cut], device))

    def send_far(self):
        for transfer in self.far:
            transfer.start()

    def send_ready(self):
        for transfer in self.ready:
            transfer.start()

    def send_summed(self):
        for k, (_, part, added) in enumerate(self.near):
            cut = self.cuts[added]
            self.far[added].arrived()
            both = self.parts[part, cut].astype(F32) + self.early[cut].astype(F32)
            self.parts[part, cut] = both.astype(B16)
            self.summed[k].start()

    def total(self):
        for transfer in self.ready + self.summed:
            transfer.arrived()
        return (
            self.parts[self.own].astype(F32)
            + self.late[0].astype(F32)
            + self.late[1].astype(F32)
        )


def ring_sum(links, parts, early, late):
    right, left = links.zed(1), links.zed(3)
    near = [(links.to_z(1), right, 0), (links.to_z(3), left, 1)]
    return FourSum(links, parts, early, late, links.zed(2), links.z, near)


class ContextSum:
    def __init__(self, links, grads, handed, early, late):
        self.links, self.grads, self.handed = links, grads, handed
        order = (links.chip_d, links.chip_x, links.chip_y, links.chip)
        self.order = order
        self.hands = [
            links.copy(grads.at[links.other, chip], handed.at[k], links.to_core)
            for k, chip in enumerate(order)
        ]
        near = [(links.to_x, links.chip_x, 1), (links.to_y, links.chip_y, 0)]
        self.four = FourSum(
            links, grads.at[links.core], early, late, links.chip_d, links.chip, near
        )

    def hand(self, k):
        self.hands[k].start()

    def merge(self, k):
        self.hands[k].arrived()
        core, chip = self.links.core, self.order[k]
        both = self.grads[core, chip].astype(F32) + self.handed[k].astype(F32)
        self.grads[core, chip] = both.astype(B16)


def backward_phase(
    links, arriving, ids, attn_t, lse, qm, kv, x_all, w_all, cot_all, fc_all, proj_all, vec_all, norm1, projw, outw, fcb,
    block_out, input_grad, h_mlp, h_attn, sums, normed1,
    a_all, grad_act, norm2, act, grad_pre, gn2, gn2_e, gn2_l, mlp, mlp_e, mlp_l, gn1, gn1_e, gn1_l,
    gm_all, gm_own, mid_own, dkv, dkv_h, dkv_e, dkv_l, g_mlp, gmlp_h, gmlp_e, gmlp_l,
    g_attn, gattn_h, gattn_e, gattn_l, fc_piece, qkv_piece, dom, delta, dq, gqkv, zsum, bsum, ssum, rowsum,
):
    members, rows, width = x_all.shape
    span = attn_t.shape[0]
    group = members * rows
    block = group // 2
    heads = span // HEAD
    half = width // 2
    small = span // 4
    z = links.z
    right, left, opposite = links.zed(1), links.zed(3), links.zed(2)

    def row(index):
        return jnp.concatenate(
            [vec_all[m, index : index + 1, :span] for m in range(members)], axis=1
        ).astype(F32)

    def head_rows(head):
        return slice(head * HEAD, (head + 1) * HEAD)

    def member_rows(member):
        return pl.ds(pl.multiple_of(member * rows, rows), rows)

    def in_order(index):
        return jnp.where(
            index == 0, opposite, jnp.where(index == 1, right, jnp.where(index == 2, left, z))
        )

    attns = RingGather(links, a_all)
    gms = RingGather(links, gm_all)
    ring_gn2 = ring_sum(links, gn2, gn2_e, gn2_l)
    ring_mlp = ring_sum(links, mlp, mlp_e, mlp_l)
    ring_gn1 = ring_sum(links, gn1, gn1_e, gn1_l)
    sum_mlp = ContextSum(links, g_mlp, gmlp_h, gmlp_e, gmlp_l)
    sum_attn = ContextSum(links, g_attn, gattn_h, gattn_e, gattn_l)
    sum_kv = ContextSum(links, dkv, dkv_h, dkv_e, dkv_l)
    gather_mlp = ContextGather(links, h_mlp)
    gather_attn = ContextGather(links, h_attn)

    def spread(piece, gathered, first):
        at = pl.ds(pl.multiple_of(first + small * z, 16), small)
        place = gathered.at[links.core, links.chip, at]
        return [links.copy(piece.at[links.zed(s)], place, links.to_z(s)) for s in (1, 3, 2)]

    spread_fc = spread(fc_piece, h_mlp, span)
    spread_qkv = spread(qkv_piece, h_attn, 0)

    cots, fcs_in, projs = arriving
    gain_one = row(0)
    gain_two, shift_two = row(3), row(4)
    proj_bias, out_bias = row(2), row(5)
    fc_bias = fcb[...].astype(F32).reshape(1, fcb.shape[0])
    attns.start()
    fcs_in.give()
    projs.give()
    cots.far()
    one, zero_shift = jnp.ones((1, width), F32), jnp.zeros((1, width), F32)

    def before(index, carry):
        grad_act[member_rows(index), :] = transposed_product(cot_all[index], outw[...])
        return carry

    lax.fori_loop(0, 2, before, 0)
    attns.forward()
    lax.fori_loop(2, 4, before, 0)
    attns.near()
    attns.far()
    fcs_in.finish()
    projs.finish()
    rowsum[...] = jnp.zeros_like(rowsum)
    fc_matrix = fc_all.shape

    def mlp_block(index, carry):
        member = in_order(index)
        at = member_rows(member)

        @pl.when(index == 3)
        def _():
            ring_gn2.send_ready()
            ring_gn2.send_summed()

        attn_cols = a_all[:, :, at].reshape(width, rows)
        middle = (
            x_all[member].astype(F32)
            + rows_product(attn_cols, proj_all[...].reshape(width, width))
            + proj_bias
        )
        shifted, normed, _ = layer_norm(middle, gain_two, shift_two)
        half_norm = shifted.astype(B16)
        norm2[at, :] = half_norm
        fc = fc_all[...].reshape(width, fc_matrix[2])
        pre_act = jnp.dot(half_norm, fc, preferred_element_type=F32) + fc_bias
        squared = pre_act * pre_act
        tanh_value = jnp.tanh(GELU_C * pre_act * (1.0 + GELU_K * squared))
        act[at, :] = (0.5 * pre_act * (1.0 + tanh_value)).astype(B16)
        slope = 0.5 * (1.0 + tanh_value) + (0.5 * GELU_C) * pre_act * (
            1.0 - tanh_value * tanh_value
        ) * (1.0 + 3.0 * GELU_K * squared)
        grad = grad_act[at, :] * slope
        rowsum[7:8, :] += jnp.sum(grad, axis=0, keepdims=True)
        grad_half = grad.astype(B16)
        grad_pre[at, :] = grad_half
        back = transposed_product(grad_half, fc)
        gn2[member] = back.astype(B16)
        rowsum[3:4, :] += jnp.sum(back * normed, axis=0, keepdims=True)
        rowsum[4:5, :] += jnp.sum(back, axis=0, keepdims=True)

        @pl.when(index == 0)
        def _():
            ring_gn2.send_far()

        @pl.when(index == 3)
        def _():
            mid_own[...] = middle

        return carry

    lax.fori_loop(0, 4, mlp_block, 0)

    def mlp_weights(core):
        cols = pl.ds(pl.multiple_of(core * half, half), half)
        cots = cot_all[:, :, cols].reshape(group, half)
        product = rows_product(act[...], cots).astype(B16)
        g_mlp[core, :, :span, :] = product.reshape(4, span, half)
        product = rows_product(norm2[...], grad_pre[:, cols]).astype(B16)
        product = product.reshape(members, 4, small, half)
        for member in range(members):
            at = span + member * small
            g_mlp[core, :, at : at + small, :] = product[member]

    mlp_weights(links.other)
    for k in range(4):
        sum_mlp.hand(k)
    mlp_weights(links.core)
    sum_mlp.merge(0)
    sum_mlp.four.send_far()
    sum_mlp.merge(1)
    sum_mlp.merge(2)
    sum_mlp.four.send_ready()

    grad_norm2 = ring_gn2.total()
    _, normed, inv_std = layer_norm(mid_own[...], gain_two, shift_two)
    cot_own = cot_all[z].astype(F32)
    grad_middle = cot_own + norm_backward(grad_norm2, gain_two, normed, inv_std)
    gm_own[...] = grad_middle
    gm_all[z] = grad_middle.astype(B16)
    gms.start()
    rowsum[2:3, :] = jnp.sum(grad_middle, axis=0, keepdims=True)
    rowsum[5:6, :] = jnp.sum(cot_own, axis=0, keepdims=True)

    sum_mlp.four.send_summed()
    sum_mlp.merge(3)
    gms.forward()

    def mlp_product(index, carry):
        at = member_rows(index)
        mlp[index] = jnp.dot(act[at, :], outw[...], preferred_element_type=F32).astype(B16)
        return carry

    lax.fori_loop(0, 4, mlp_product, 0)
    gms.near()
    gms.far()
    ring_mlp.send_far()
    ring_mlp.send_ready()
    total = sum_mlp.four.total().astype(B16)
    h_mlp[links.core, links.chip, :span, :] = total[:span]
    fc_piece[...] = total[span:].reshape(members, small, half)
    own = pl.ds(pl.multiple_of(span + small * z, 16), small)
    h_mlp[links.core, links.chip, own, :] = fc_piece[z]
    for transfer in spread_fc:
        transfer.start()

    grad_mid = gm_all[...].reshape(group, width)
    grad_attn_t = transposed_product(projw[...], grad_mid).astype(B16).astype(F32)
    delta_rows = grad_attn_t * attn_t[...].astype(F32)
    for head in range(heads):
        delta[head : head + 1, :] = jnp.sum(delta_rows[head_rows(head), :], axis=0, keepdims=True)
    grad_attn = transposed_product(grad_mid, projw[...]).astype(B16)
    for head, lone in enumerate(masked_heads(grad_attn, HEAD, 4 * HEAD)):
        dom[head] = lone
    product = jnp.dot(attn_t[...], grad_mid, preferred_element_type=F32).astype(B16)
    for core in range(2):
        g_attn[core, :, span:, :] = product[:, core * half : (core + 1) * half].reshape(4, small, half)
    dq[...] = jnp.zeros_like(dq)

    own_block = ids[2 * links.ctx]
    keep = lax.broadcasted_iota(jnp.int32, (block, block), 0) <= lax.broadcasted_iota(
        jnp.int32, (block, block), 1
    )
    low_rows, high_rows = slice(0, block), slice(block, group)

    def tile(keys, queries, grads, lse_of, delta_of, masked=False):
        probs, scores_grad = [], []
        for head in range(heads):
            scores = transposed_product(keys[:, : 4 * HEAD], queries[head])
            if masked:
                scores = jnp.where(keep, scores, NEG_FILL)
            weights = jnp.exp(scores - lse_of(head))
            grad_probs = transposed_product(keys[:, 2 * HEAD :], grads[head])
            probs.append(weights.astype(B16))
            scores_grad.append((weights * (grad_probs - delta_of(head))).astype(B16))
        keys_t = keys[:, : 4 * HEAD].T
        query_grad = [
            jnp.dot(keys_t[head_rows(head)], scores_grad[head], preferred_element_type=F32)
            for head in range(heads)
        ]
        value_grad = jnp.dot(
            jnp.concatenate(probs, axis=1),
            jnp.concatenate(grads, axis=0),
            preferred_element_type=F32,
        )
        key_grad = jnp.dot(
            jnp.concatenate(scores_grad, axis=1),
            jnp.concatenate(queries, axis=0),
            preferred_element_type=F32,
        )
        both = jnp.concatenate(
            [
                key_grad[:, : 2 * HEAD],
                key_grad[:, 2 * HEAD :] + value_grad[:, : 2 * HEAD],
                value_grad[:, 2 * HEAD :],
            ],
            axis=1,
        )
        return query_grad, both

    def stacked(ref, at):
        return [ref[head, at, :] for head in range(heads)]

    def rows_at(ref, at):
        return lambda head: ref[head : head + 1, at]

    def hop(index, carry):
        chip = jnp.where(
            index < 2,
            links.chip_d,
            jnp.where(index < 4, links.chip_x, jnp.where(index < 6, links.chip_y, links.chip)),
        )
        core = jnp.where(lax.rem(index, 2) == 0, links.other, links.core)

        @pl.when(index == 0)
        def _():
            for transfer in spread_fc:
                transfer.arrived()
            gather_mlp.start()

        @pl.when(index == 1)
        def _():
            sum_kv.hand(0)
            ring_mlp.send_summed()

        @pl.when(index == 2)
        def _():
            sum_kv.merge(0)
            sum_kv.four.send_far()

        @pl.when(index == 3)
        def _():
            sum_kv.hand(1)
            gather_mlp.forward()

        @pl.when(index == 4)
        def _():
            sum_kv.merge(1)
            sum_kv.four.ready[0].start()

        @pl.when(index == 5)
        def _():
            sum_kv.hand(2)
            gather_mlp.hand_near()

        @pl.when(index == 6)
        def _():
            sum_kv.merge(2)
            sum_kv.four.ready[1].start()
            sum_kv.four.send_summed()

        block_id = ids[2 * (2 * chip + core)]
        low = (block_id < own_block).astype(jnp.int32)
        in_low = chosen(low, (1, block))
        kv_low = kv[core, chip, low_rows, :]
        kv_pick = jnp.where(chosen(low, kv_low.shape), kv_low, kv[core, chip, high_rows, :])
        q_mask = chosen(low, (block, 4 * HEAD))

        def pick(ref):
            return [
                jnp.where(q_mask, ref[head, low_rows, :], ref[head, high_rows, :])
                for head in range(heads)
            ]

        def pick_row(ref):
            return lambda head: jnp.where(
                in_low, ref[head : head + 1, low_rows], ref[head : head + 1, high_rows]
            )

        query_grad, first = tile(
            kv_low,
            stacked(qm, high_rows),
            stacked(dom, high_rows),
            rows_at(lse, high_rows),
            rows_at(delta, high_rows),
        )
        for head in range(heads):
            dq[1, head_rows(head), :] += query_grad[head]
        query_grad, second = tile(kv_pick, pick(qm), pick(dom), pick_row(lse), pick_row(delta))
        for head in range(heads):
            at = head_rows(head)
            dq[0, at, :] += jnp.where(in_low, query_grad[head], 0.0)
            dq[1, at, :] += jnp.where(in_low, 0.0, query_grad[head])
        mask = chosen(low, second.shape)
        dkv[core, chip, low_rows, :] = (first + jnp.where(mask, second, 0.0)).astype(B16)
        dkv[core, chip, high_rows, :] = jnp.where(mask, 0.0, second).astype(B16)
        return carry

    lax.fori_loop(0, 7, hop, 0)
    sum_kv.hand(3)
    gather_mlp.hand_far()
    block_out[...] = ring_mlp.total() + mid_own[...] + out_bias
    for keys_at, queries_at, masked in (
        (low_rows, high_rows, False),
        (low_rows, low_rows, True),
        (high_rows, high_rows, True),
    ):
        query_grad, both = tile(
            kv[links.core, links.chip, keys_at, :],
            stacked(qm, queries_at),
            stacked(dom, queries_at),
            rows_at(lse, queries_at),
            rows_at(delta, queries_at),
            masked,
        )
        part = 0 if queries_at is low_rows else 1
        for head in range(heads):
            dq[part, head_rows(head), :] += query_grad[head]
        if keys_at is low_rows and not masked:
            held = both
        elif keys_at is low_rows:
            dkv[links.core, links.chip, keys_at, :] = (held + both).astype(B16)
        else:
            dkv[links.core, links.chip, keys_at, :] = both.astype(B16)

    grad_query = jnp.concatenate([dq[0].T, dq[1].T], axis=0) * HEAD**-0.5
    sum_kv.merge(3)
    own_kv = sum_kv.four.total().astype(B16)
    split = jnp.concatenate(
        [
            jnp.sum(grad_query, axis=0, keepdims=True),
            jnp.sum(own_kv[:, span:].astype(F32), axis=0, keepdims=True),
            jnp.zeros((1, width - 2 * span), F32),
        ],
        axis=1,
    )
    rowsum[6:7, :] = split
    gqkv[...] = jnp.concatenate(
        [grad_query.astype(B16), own_kv, jnp.zeros((group, 640 - 3 * span), B16)], axis=1
    )

    def attn_weights(core):
        cols = pl.ds(pl.multiple_of(core * 256, 256), half)
        product = rows_product(norm1[...], gqkv[:, cols]).astype(B16)
        product = product.reshape(members, 4, small, half)
        for member in range(members):
            g_attn[core, :, member * small : (member + 1) * small, :] = product[member]

    attn_weights(links.other)
    for k in range(4):
        sum_attn.hand(k)
    attn_weights(links.core)
    sum_attn.merge(0)
    sum_attn.four.send_far()
    sum_attn.merge(1)
    sum_attn.merge(2)
    sum_attn.four.send_ready()

    def norm1_block(index, carry):
        member = in_order(index)
        at = member_rows(member)

        @pl.when(index == 3)
        def _():
            ring_gn1.send_ready()

        back = transposed_product(
            gqkv[at, : 3 * span], w_all[...].reshape(width, width)[:, : 3 * span]
        )
        gn1[member] = back.astype(B16)
        rowsum[0:1, :] += jnp.sum(back * normed1[at, :], axis=0, keepdims=True)
        rowsum[1:2, :] += jnp.sum(back, axis=0, keepdims=True)

        @pl.when(index == 0)
        def _():
            ring_gn1.send_far()

        return carry

    lax.fori_loop(0, 4, norm1_block, 0)
    ring_gn1.send_summed()
    zsum[z] = rowsum[...]
    z_sums = [links.copy(zsum.at[z], zsum.at[z], links.to_z(s)) for s in (1, 3, 2)]
    for transfer in z_sums:
        transfer.start()
    gather_mlp.x_core.arrived()
    gather_mlp.y_core.arrived()
    gather_mlp.d_core.arrived()
    sum_attn.merge(3)
    sum_attn.four.send_summed()
    for transfer in z_sums:
        transfer.arrived()
    index = lax.broadcasted_iota(jnp.int32, rowsum.shape, 0)
    value = zsum[0] + zsum[1] + zsum[2] + zsum[3]
    value = jnp.where(index < 6, value, zsum[z])
    ssum[0] = value
    steps = [
        links.copy(ssum.at[k], bsum.at[k], device)
        for k, device in enumerate((links.to_core, links.to_x, links.to_y))
    ]
    steps[0].start()

    grad_norm1 = ring_gn1.total()
    _, normed, inv_std = layer_norm(x_all[z].astype(F32), one, zero_shift)
    input_grad[...] = gm_own[...] + norm_backward(grad_norm1, gain_one, normed, inv_std)

    steps[0].arrived()
    ssum[1] = ssum[0] + bsum[0]
    steps[1].start()
    total = sum_attn.four.total().astype(B16)
    h_attn[links.core, links.chip, span:, :] = total[span:]
    qkv_piece[...] = total[:span].reshape(members, small, half)
    own = pl.ds(pl.multiple_of(small * z, 16), small)
    h_attn[links.core, links.chip, own, :] = qkv_piece[z]
    for transfer in spread_qkv:
        transfer.start()
    steps[1].arrived()
    ssum[2] = ssum[1] + bsum[1]
    steps[2].start()
    for transfer in spread_qkv:
        transfer.arrived()
    gather_attn.start()
    steps[2].arrived()
    total = ssum[2] + bsum[2]
    mine = total[:, :span]
    for m in range(1, members):
        mine = jnp.where(
            chosen((z == m).astype(jnp.int32), mine.shape), total[:, m * span : (m + 1) * span], mine
        )
    sums[:6, :span] = mine[:6]
    sums[6:8, :] = total[6:8]
    gather_attn.forward()
    gather_attn.own_core.arrived()
    gather_mlp.own_core.arrived()
    gather_attn.hand_near()
    gather_attn.hand_far()
    gather_attn.x_core.arrived()
    gather_attn.y_core.arrived()
    gather_attn.d_core.arrived()


def block_kernel(*refs):
    ids, x, cot, qkvw, fcw, projw = refs[:6]
    vectors = refs[6:14]
    outw, fcb = refs[14:16]
    outs = refs[16:21]
    lse, qm, kv, x_all, w_all, cot_all, fc_all, proj_all, vec_all, norm1, normed1 = refs[21:32]
    front = refs[32:39]
    a_all = refs[39]
    links = Links(*refs[-2:])
    attn_t = a_all.at[links.z]
    shared = (lse, qm, kv, x_all, w_all, cot_all, fc_all, proj_all, vec_all, norm1)
    arriving = forward_phase(
        links, ids, x, cot, qkvw, fcw, projw, *vectors, attn_t, *shared, normed1, *front
    )
    backward_phase(
        links, arriving, ids, attn_t, *shared, projw, outw, fcb, *outs, normed1, *refs[39:-2]
    )
    links.drain()


def block_call(ids, x, cot, qkvw, fcw, projw, *vectors):
    rows, width = x.shape
    members = 4
    span = qkvw.shape[0]
    group = members * rows
    block = group // 2
    heads = span // HEAD
    half = width // 2
    small = span // 4
    mlp_rows, attn_rows = 2 * span, span + small

    def shape(dims, dtype=B16):
        return jax.ShapeDtypeStruct(dims, dtype)

    def summed(rows_of, cols):
        return [
            VMEM((4, rows_of, cols), B16),
            VMEM((rows_of, cols), B16),
            VMEM((2, rows_of, cols), B16),
        ]

    def ring():
        return [
            VMEM((members, rows, width), B16),
            VMEM((rows, width), B16),
            VMEM((2, rows, width), B16),
        ]

    outs = (
        shape((rows, width), F32),
        shape((rows, width), F32),
        shape((2, 4, mlp_rows, half)),
        shape((2, 4, attn_rows, half)),
        shape((8, width), F32),
    )
    scratch = (
        [
            VMEM((8, group), F32),
            VMEM((heads, group, 4 * HEAD), B16),
            VMEM((2, 4, group, 2 * span), B16),
            VMEM((members, rows, width), B16),
            VMEM((members, span, width), B16),
            VMEM((members, rows, width), B16),
            VMEM((members, span, width), B16),
            VMEM((members, span, width), B16),
            VMEM((members, 16, 256), B16),
            VMEM((group, width), B16),
            VMEM((group, width), F32),
            VMEM((members, span, width), B16),
            VMEM((8, block), F32),
            VMEM((8, block), F32),
            VMEM((span, block), F32),
            VMEM((2, 8, block), F32),
            VMEM((2, 8, block), F32),
            VMEM((2, span, block), F32),
            VMEM((members, span, group), B16),
            VMEM((group, width), F32),
            VMEM((group, width), B16),
            VMEM((group, width), B16),
            VMEM((group, width), B16),
        ]
        + ring()
        + ring()
        + ring()
        + [
            VMEM((members, rows, width), B16),
            VMEM((rows, width), F32),
            VMEM((rows, width), F32),
            VMEM((2, 4, group, 2 * span), B16),
        ]
        + summed(group, 2 * span)
        + [VMEM((2, 4, mlp_rows, half), B16)]
        + summed(mlp_rows, half)
        + [VMEM((2, 4, attn_rows, half), B16)]
        + summed(attn_rows, half)
        + [
            VMEM((members, small, half), B16),
            VMEM((members, small, half), B16),
            VMEM((heads, group, 4 * HEAD), B16),
            VMEM((8, group), F32),
            VMEM((2, span, block), F32),
            VMEM((group, 640), B16),
            VMEM((members, 8, width), F32),
            VMEM((3, 8, width), F32),
            VMEM((3, 8, width), F32),
            VMEM((8, width), F32),
            pltpu.SemaphoreType.DMA((160,)),
            pltpu.SemaphoreType.DMA((160,)),
        ]
    )
    args = (ids, x, cot, qkvw, fcw, projw) + vectors
    return pl.pallas_call(
        block_kernel,
        out_shape=outs,
        in_specs=[pl.BlockSpec(memory_space=SMEM)] + [pl.BlockSpec(memory_space=VMEM)] * (len(args) - 1),
        out_specs=(pl.BlockSpec(memory_space=VMEM),) * len(outs),
        scratch_shapes=scratch,
        compiler_params=pltpu.CompilerParams(
            collective_id=0, has_side_effects=True, vmem_limit_bytes=62 << 20
        ),
        name="block",
    )(*args)


def assemble_kernel(
    block_in, grad_in, h_mlp, h_attn, sums,
    block_out, grad_out, gain1, bias1, qkv, qbias, vbias, proj, pbias, gain2, bias2, fc, fbias, out, obias,
):
    span, width = proj.shape
    half = width // 2
    small = span // 4
    block_out[...] = block_in[...]
    grad_out[...] = grad_in[...]
    for ref, index in ((gain1, 0), (bias1, 1), (pbias, 2), (gain2, 3), (bias2, 4), (obias, 5)):
        ref[...] = sums[index : index + 1, :span].reshape(span)
    qbias[...] = sums[6:7, :span].reshape(span)
    vbias[...] = sums[6:7, span : 2 * span].reshape(span)
    fbias[...] = sums[7:8, :].reshape(width)
    for chip in range(4):
        rows = slice(chip * small, (chip + 1) * small)
        for core in range(2):
            cols = slice(core * half, (core + 1) * half)
            out[chip * span : (chip + 1) * span, cols] = h_mlp[core, chip, :span, :].astype(F32)
            proj[rows, cols] = h_attn[core, chip, span:, :].astype(F32)
            for member in range(4):
                at = span + member * small
                fc[rows, member * width + core * half : member * width + (core + 1) * half] = h_mlp[
                    core, chip, at : at + small, :
                ].astype(F32)
        pieces = []
        for member in range(4):
            at = slice(member * small, (member + 1) * small)
            pieces.append(
                jnp.concatenate(
                    [h_attn[0, chip, at, :], h_attn[1, chip, at, 128 : 3 * span - 256]], axis=1
                ).astype(F32)
            )
        qkv[rows, :] = jnp.concatenate(
            [piece[:, t * span : (t + 1) * span] for t in range(3) for piece in pieces], axis=1
        )


def assemble(block_in, grad_in, h_mlp, h_attn, sums):
    width = block_in.shape[1]
    span = width // 4

    def shape(*dims):
        return jax.ShapeDtypeStruct(dims, F32)

    narrow = shape(span)
    outs = (
        shape(*block_in.shape), shape(*block_in.shape), narrow, narrow, shape(span, 3 * width), narrow, narrow,
        shape(span, width), narrow, narrow, narrow, shape(span, 4 * width), shape(width), shape(width, width),
        narrow,
    )
    return pl.pallas_call(
        assemble_kernel,
        out_shape=outs,
        in_specs=[pl.BlockSpec(memory_space=VMEM)] * 5,
        out_specs=(pl.BlockSpec(memory_space=VMEM),) * len(outs),
        compiler_params=pltpu.CompilerParams(vmem_limit_bytes=48 << 20),
        name="assemble",
    )(block_in, grad_in, h_mlp, h_attn, sums)


def head_shards(
    block_input,
    positions,
    norm1_gain,
    norm1_bias,
    qkv_weight,
    query_bias,
    value_bias,
    proj_weight,
    proj_bias,
    norm2_gain,
    norm2_bias,
    fc_weight,
    fc_bias,
    out_weight,
    out_bias,
    cotangent,
):
    rows, width = block_input.shape
    ids = positions.reshape(-1, 2 * rows)[:, 0] // (2 * rows)
    results = block_call(
        ids, block_input, cotangent, qkv_weight, fc_weight, proj_weight, norm1_gain, norm1_bias, proj_bias,
        norm2_gain, norm2_bias, out_bias, query_bias, value_bias, out_weight, fc_bias,
    )
    return assemble(*results)


def solution(mesh):
    sharded = P(("ctx", "fsdp"), None)
    rows, vector = P("fsdp", None), P("fsdp")
    in_specs = (
        sharded, P(), vector, vector, rows, vector, vector, rows, vector, vector, vector, rows, vector, rows,
        vector, sharded,
    )
    out_specs = (
        sharded, sharded, vector, vector, rows, vector, vector, rows, vector, vector, vector, rows, vector, rows,
        vector,
    )
    body = head_shards if dict(mesh.shape) == {"ctx": 8, "fsdp": 4} else shards
    return jax.shard_map(body, mesh=mesh, in_specs=in_specs, out_specs=out_specs, check_vma=False)
```

```python
import functools

import jax
import jax.numpy as jnp
from jax import lax
from jax.experimental import pallas as pl
from jax.experimental.pallas import tpu as pltpu
from jax.sharding import PartitionSpec as P

HEADS = 12
HEAD = 64


EPSILON = 1e-05
NEG_FILL = -1e30
GELU_C = 0.7978845608028654
GELU_K = 0.044715


def passed_along(block, axis, distance):
    devices = range(lax.axis_size(axis))
    route = [((i - distance) % len(devices), i) for i in devices]
    return lax.ppermute(block, axis, route)


def layer_norm(values_in, gain, shift):
    row_mean = jnp.mean(values_in, axis=-1, keepdims=True)
    centered = values_in - row_mean
    variance = jnp.mean(centered * centered, axis=-1, keepdims=True)
    inv_std = lax.rsqrt(variance + EPSILON)
    normed = centered * inv_std
    return (normed * gain.astype(jnp.float32) + shift.astype(jnp.float32), normed, inv_std)


def norm_backward(grad_norm, gain, normed, inv_std):
    scaled = grad_norm * gain.astype(jnp.float32)
    scaled_mean = jnp.mean(scaled, axis=-1, keepdims=True)
    cross_mean = jnp.mean(scaled * normed, axis=-1, keepdims=True)
    return inv_std * (scaled - scaled_mean - normed * cross_mean)


def gelu_forward(pre_act):
    cubed = pre_act * pre_act * pre_act
    return 0.5 * pre_act * (1.0 + jnp.tanh(GELU_C * (pre_act + GELU_K * cubed)))


def gelu_slope(pre_act):
    cubed = pre_act * pre_act * pre_act
    tanh_value = jnp.tanh(GELU_C * (pre_act + GELU_K * cubed))
    return 0.5 * (1.0 + tanh_value) + 0.5 * pre_act * (1.0 - tanh_value * tanh_value) * GELU_C * (
        1.0 + 3.0 * GELU_K * pre_act * pre_act
    )


def rows_product(left, right):
    return lax.dot_general(
        left, right, (((0,), (0,)), ((), ())), preferred_element_type=jnp.float32
    )


def transposed_product(left, right):
    return lax.dot_general(
        left, right, (((1,), (1,)), ((), ())), preferred_element_type=jnp.float32
    )


def split_heads(matrix):
    return matrix.reshape(matrix.shape[0], HEADS, HEAD)


def masked_scores(query, query_pos, keys, key_pos):
    scores = jnp.einsum(
        "rhd,khd->hrk", split_heads(query), split_heads(keys), preferred_element_type=jnp.float32
    ) * HEAD ** (-0.5)
    allowed = (key_pos[None, :] <= query_pos[:, None])[None]
    return (jnp.where(allowed, scores, NEG_FILL), allowed)


def attend_block(carried, query, query_pos, keys, values, key_pos):
    weighted, run_max, row_total = carried
    scores, allowed = masked_scores(query, query_pos, keys, key_pos)
    new_max = jnp.maximum(run_max, jnp.max(scores, axis=-1))
    weights = jnp.where(allowed, jnp.exp(scores - new_max[..., None]), 0.0)
    factor = jnp.exp(run_max - new_max)
    row_total = row_total * factor + jnp.sum(weights, axis=-1)
    update = jnp.einsum(
        "hrk,khd->rhd",
        weights,
        split_heads(values).astype(jnp.float32),
        precision=lax.Precision.HIGHEST,
        preferred_element_type=jnp.float32,
    )
    weighted = weighted * factor.T[:, :, None] + update
    return (weighted, new_max, row_total)


def attend_tile(carried, query, query_pos, keys, values, key_pos):
    half_rows = keys.shape[0] // 2
    latest = jnp.max(query_pos)
    for half_index in range(2):
        first_row = half_index * half_rows
        part_keys = keys[first_row : first_row + half_rows]
        part_values = values[first_row : first_row + half_rows]
        part_pos = key_pos[first_row : first_row + half_rows]

        def keep_state(state_in, block_keys, block_values, block_pos):
            return state_in

        def update_state(state_in, block_keys, block_values, block_pos):
            return attend_block(state_in, query, query_pos, block_keys, block_values, block_pos)

        carried = lax.cond(
            jnp.min(part_pos) > latest,
            keep_state,
            update_state,
            carried,
            part_keys,
            part_values,
            part_pos,
        )
    return carried


def block_grads(query, grad_attn, row_lse, row_delta, query_pos, keys, values, key_pos):
    scores, allowed = masked_scores(query, query_pos, keys, key_pos)
    probs = jnp.where(allowed, jnp.exp(scores - row_lse[..., None]), 0.0)
    grad_heads = split_heads(grad_attn)
    grad_values = jnp.einsum(
        "hrk,rhd->khd", probs.astype(jnp.bfloat16), grad_heads, preferred_element_type=jnp.float32
    )
    grad_probs = jnp.einsum(
        "rhd,khd->hrk", grad_heads, split_heads(values), preferred_element_type=jnp.float32
    )
    grad_scores = (probs * (grad_probs - row_delta[..., None])).astype(jnp.bfloat16)
    scale = HEAD ** (-0.5)
    grad_query = (
        jnp.einsum(
            "hrk,khd->rhd", grad_scores, split_heads(keys), preferred_element_type=jnp.float32
        )
        * scale
    )
    grad_keys = (
        jnp.einsum(
            "hrk,rhd->khd", grad_scores, split_heads(query), preferred_element_type=jnp.float32
        )
        * scale
    )
    key_rows = keys.shape[0]
    return (grad_query, grad_keys.reshape(key_rows, -1), grad_values.reshape(key_rows, -1))


def tile_grads(query, grad_attn, row_lse, row_delta, query_pos, keys, values, key_pos):
    half_rows = keys.shape[0] // 2
    key_width = keys.shape[1]
    latest = jnp.max(query_pos)
    query_total = jnp.zeros((query.shape[0], HEADS, HEAD), jnp.float32)
    key_parts = []
    value_parts = []
    for half_index in range(2):
        first_row = half_index * half_rows
        part_keys = keys[first_row : first_row + half_rows]
        part_values = values[first_row : first_row + half_rows]
        part_pos = key_pos[first_row : first_row + half_rows]

        def skipped(block_keys, block_values, block_pos):
            return (
                jnp.zeros((query.shape[0], HEADS, HEAD), jnp.float32),
                jnp.zeros((half_rows, key_width), jnp.float32),
                jnp.zeros((half_rows, key_width), jnp.float32),
            )

        def computed(block_keys, block_values, block_pos):
            return block_grads(
                query, grad_attn, row_lse, row_delta, query_pos, block_keys, block_values, block_pos
            )

        step_query, step_keys, step_values = lax.cond(
            jnp.min(part_pos) > latest, skipped, computed, part_keys, part_values, part_pos
        )
        query_total = query_total + step_query
        key_parts.append(step_keys)
        value_parts.append(step_values)
    return (query_total, jnp.concatenate(key_parts, axis=0), jnp.concatenate(value_parts, axis=0))


def shards(
    block_input,
    positions,
    norm1_gain,
    norm1_bias,
    qkv_weight,
    query_bias,
    value_bias,
    proj_weight,
    proj_bias,
    norm2_gain,
    norm2_bias,
    fc_weight,
    fc_bias,
    out_weight,
    out_bias,
    cotangent,
):
    rows = block_input.shape[0]
    width = block_input.shape[1]
    ctx_size = lax.axis_size("ctx")
    shard_count = lax.axis_size("fsdp")
    ctx_index = lax.axis_index("ctx")
    shard_index = lax.axis_index("fsdp")
    group_rows = rows * shard_count

    def key_positions(source):
        return lax.dynamic_slice_in_dim(positions, source * group_rows, group_rows)

    gain_one, shift_one, qkv_full, qbias_full, vbias_full, proj_full, pbias_full = (
        lax.all_gather(norm1_gain, "fsdp", axis=0, tiled=True),
        lax.all_gather(norm1_bias, "fsdp", axis=0, tiled=True),
        lax.all_gather(qkv_weight, "fsdp", axis=0, tiled=True),
        lax.all_gather(query_bias, "fsdp", axis=0, tiled=True),
        lax.all_gather(value_bias, "fsdp", axis=0, tiled=True),
        lax.all_gather(proj_weight, "fsdp", axis=0, tiled=True),
        lax.all_gather(proj_bias, "fsdp", axis=0, tiled=True),
    )
    gain_two, shift_two, fc_full, fbias_full, out_full, obias_full = (
        lax.all_gather(norm2_gain, "fsdp", axis=0, tiled=True),
        lax.all_gather(norm2_bias, "fsdp", axis=0, tiled=True),
        lax.all_gather(fc_weight, "fsdp", axis=0, tiled=True),
        lax.all_gather(fc_bias, "fsdp", axis=0, tiled=True),
        lax.all_gather(out_weight, "fsdp", axis=0, tiled=True),
        lax.all_gather(out_bias, "fsdp", axis=0, tiled=True),
    )
    residual = block_input.astype(jnp.float32)
    normed1_out, normed1, inv_std1 = layer_norm(residual, gain_one, shift_one)
    norm1 = normed1_out.astype(jnp.bfloat16)
    qkv = jnp.dot(norm1, qkv_full, preferred_element_type=jnp.float32)
    query = (qkv[:, :width] + qbias_full.astype(jnp.float32)).astype(jnp.bfloat16)
    keys = qkv[:, width : 2 * width].astype(jnp.bfloat16)
    values = (qkv[:, 2 * width :] + vbias_full.astype(jnp.float32)).astype(jnp.bfloat16)
    group_keys, group_values = (
        lax.all_gather(keys, "fsdp", axis=0, tiled=True),
        lax.all_gather(values, "fsdp", axis=0, tiled=True),
    )
    own_qpos = lax.dynamic_slice_in_dim(
        positions, (ctx_index * shard_count + shard_index) * rows, rows
    )
    own_kpos = key_positions(ctx_index)
    initial = (
        jnp.zeros((rows, HEADS, HEAD), jnp.float32),
        jnp.full((HEADS, rows), NEG_FILL, jnp.float32),
        jnp.zeros((HEADS, rows), jnp.float32),
    )
    carried = attend_tile(initial, query, own_qpos, group_keys, group_values, own_kpos)

    def forward_hop(hop_index, loop_carry):
        state_now, cycle_keys, cycle_values = loop_carry
        cycle_keys, cycle_values = passed_along((cycle_keys, cycle_values), "ctx", 1)
        source = (ctx_index - hop_index) % ctx_size
        state_now = attend_tile(
            state_now, query, own_qpos, cycle_keys, cycle_values, key_positions(source)
        )
        return (state_now, cycle_keys, cycle_values)

    result = lax.fori_loop(1, ctx_size, forward_hop, (carried, group_keys, group_values))
    carried = result[0]
    weighted, run_max, row_total = carried
    attn = (weighted / row_total.T[:, :, None]).reshape(rows, width).astype(jnp.bfloat16)
    row_lse = run_max + jnp.log(row_total)
    middle = (
        residual
        + jnp.dot(attn, proj_full, preferred_element_type=jnp.float32)
        + pbias_full.astype(jnp.float32)
    )
    normed2_out, normed2, inv_std2 = layer_norm(middle, gain_two, shift_two)
    norm2 = normed2_out.astype(jnp.bfloat16)
    pre_act = jnp.dot(norm2, fc_full, preferred_element_type=jnp.float32) + fbias_full.astype(
        jnp.float32
    )
    act = gelu_forward(pre_act).astype(jnp.bfloat16)
    block_output = (
        middle
        + jnp.dot(act, out_full, preferred_element_type=jnp.float32)
        + obias_full.astype(jnp.float32)
    )
    grad_out = cotangent.astype(jnp.float32)
    out_weight_grad = rows_product(act, cotangent)
    out_bias_grad = jnp.sum(grad_out, axis=0)
    grad_act = transposed_product(cotangent, out_full)
    grad_pre = grad_act * gelu_slope(pre_act)
    fc_bias_grad = jnp.sum(grad_pre, axis=0)
    grad_pre_half = grad_pre.astype(jnp.bfloat16)
    fc_weight_grad = rows_product(norm2, grad_pre_half)
    grad_norm2 = transposed_product(grad_pre_half, fc_full)
    norm2_gain_grad = jnp.sum(grad_norm2 * normed2, axis=0)
    norm2_bias_grad = jnp.sum(grad_norm2, axis=0)
    grad_middle = grad_out + norm_backward(grad_norm2, gain_two, normed2, inv_std2)
    mlp_shares = (
        lax.psum_scatter(norm2_gain_grad, "fsdp", scatter_dimension=0, tiled=True),
        lax.psum_scatter(norm2_bias_grad, "fsdp", scatter_dimension=0, tiled=True),
        lax.psum_scatter(fc_weight_grad, "fsdp", scatter_dimension=0, tiled=True),
        lax.psum_scatter(fc_bias_grad, "fsdp", scatter_dimension=0, tiled=True),
        lax.psum_scatter(out_weight_grad, "fsdp", scatter_dimension=0, tiled=True),
        lax.psum_scatter(out_bias_grad, "fsdp", scatter_dimension=0, tiled=True),
    )
    proj_bias_grad = jnp.sum(grad_middle, axis=0)
    grad_middle_half = grad_middle.astype(jnp.bfloat16)
    proj_weight_grad = rows_product(attn, grad_middle_half)
    grad_attn = transposed_product(grad_middle_half, proj_full).astype(jnp.bfloat16)
    row_delta = jnp.sum(
        split_heads(grad_attn).astype(jnp.float32) * split_heads(attn).astype(jnp.float32), axis=-1
    ).T
    grad_query, grad_keys, grad_values = tile_grads(
        query, grad_attn, row_lse, row_delta, own_qpos, group_keys, group_values, own_kpos
    )

    def pass_key_grads(key_grads):
        return passed_along((key_grads[0], key_grads[1]), "ctx", 1)

    def backward_hop(hop_index, loop_carry):
        query_sum, key_grads, cycle_keys, cycle_values = loop_carry
        cycle_keys, cycle_values = passed_along((cycle_keys, cycle_values), "ctx", 1)
        key_grads = pass_key_grads(key_grads)
        source = (ctx_index - hop_index) % ctx_size
        step_query, step_keys, step_values = tile_grads(
            query,
            grad_attn,
            row_lse,
            row_delta,
            own_qpos,
            cycle_keys,
            cycle_values,
            key_positions(source),
        )
        return (
            query_sum + step_query,
            (key_grads[0] + step_keys, key_grads[1] + step_values),
            cycle_keys,
            cycle_values,
        )

    result = lax.fori_loop(
        1, ctx_size, backward_hop, (grad_query, (grad_keys, grad_values), group_keys, group_values)
    )
    grad_query = result[0]
    key_grads = pass_key_grads(result[1])
    own_key_grad, own_value_grad = (
        lax.psum_scatter(key_grads[0], "fsdp", scatter_dimension=0, tiled=True),
        lax.psum_scatter(key_grads[1], "fsdp", scatter_dimension=0, tiled=True),
    )
    grad_query_rows = grad_query.reshape(rows, width)
    query_bias_grad = jnp.sum(grad_query_rows, axis=0)
    value_bias_grad = jnp.sum(own_value_grad, axis=0)
    grad_qkv = jnp.concatenate([grad_query_rows, own_key_grad, own_value_grad], axis=1).astype(
        jnp.bfloat16
    )
    qkv_weight_grad = rows_product(norm1, grad_qkv)
    grad_norm1 = transposed_product(grad_qkv, qkv_full)
    norm1_gain_grad = jnp.sum(grad_norm1 * normed1, axis=0)
    norm1_bias_grad = jnp.sum(grad_norm1, axis=0)
    input_grad = grad_middle + norm_backward(grad_norm1, gain_one, normed1, inv_std1)
    attn_shares = (
        lax.psum_scatter(norm1_gain_grad, "fsdp", scatter_dimension=0, tiled=True),
        lax.psum_scatter(norm1_bias_grad, "fsdp", scatter_dimension=0, tiled=True),
        lax.psum_scatter(qkv_weight_grad, "fsdp", scatter_dimension=0, tiled=True),
        lax.psum_scatter(query_bias_grad, "fsdp", scatter_dimension=0, tiled=True),
        lax.psum_scatter(value_bias_grad, "fsdp", scatter_dimension=0, tiled=True),
        lax.psum_scatter(proj_weight_grad, "fsdp", scatter_dimension=0, tiled=True),
        lax.psum_scatter(proj_bias_grad, "fsdp", scatter_dimension=0, tiled=True),
    )
    totals = lax.psum(
        (
            attn_shares[0],
            attn_shares[1],
            attn_shares[2],
            attn_shares[3],
            attn_shares[4],
            attn_shares[5],
            attn_shares[6],
            mlp_shares[0],
            mlp_shares[1],
            mlp_shares[2],
            mlp_shares[3],
            mlp_shares[4],
            mlp_shares[5],
        ),
        "ctx",
    )
    return (
        block_output,
        input_grad,
        totals[0],
        totals[1],
        totals[2],
        totals[3],
        totals[4],
        totals[5],
        totals[6],
        totals[7],
        totals[8],
        totals[9],
        totals[10],
        totals[11],
        totals[12],
    )


MESH = pl.DeviceIdType.MESH
SMEM = pltpu.SMEM
VMEM = pltpu.VMEM
F32 = jnp.float32
B16 = jnp.bfloat16


class Transfer:
    def __init__(self, links, src, dst, device):
        self.args = dict(
            src_ref=src,
            dst_ref=dst,
            send_sem=links.send_sem.at[links.count],
            recv_sem=links.recv_sem.at[links.count],
            device_id=device,
            device_id_type=MESH,
        )
        links.count += 1
        links.sent.append(self)

    def start(self):
        pltpu.make_async_remote_copy(**self.args).start()
        return self

    def arrived(self):
        pltpu.make_async_remote_copy(**self.args).wait_recv()

    def left(self):
        pltpu.make_async_remote_copy(**self.args).wait_send()


class Links:
    def __init__(self, send_sem, recv_sem):
        self.send_sem, self.recv_sem = send_sem, recv_sem
        self.count = 0
        self.sent = []
        ctx = lax.axis_index("ctx")
        self.ctx = ctx
        self.z = lax.axis_index("fsdp")
        self.core = lax.rem(ctx, 2)
        self.chip = lax.div(ctx, 2)
        x, y = lax.rem(self.chip, 2), lax.div(self.chip, 2)
        self.chip_x = self.chip + 1 - 2 * x
        self.chip_y = self.chip + 2 - 4 * y
        self.chip_d = 3 - self.chip
        self.other = 1 - self.core
        self.to_core = {"ctx": self.chip * 2 + self.other}
        self.to_x = {"ctx": self.chip_x * 2 + self.core}
        self.to_y = {"ctx": self.chip_y * 2 + self.core}
        self.to_d = {"ctx": self.chip_d * 2 + self.core}

    def zed(self, step):
        return lax.rem(self.z + step, 4)

    def to_z(self, step):
        return {"fsdp": self.zed(step)}

    def peers(self):
        near = [self.to_core, self.to_x, self.to_y, self.to_d]
        return near + [self.to_z(step) for step in (1, 2, 3)]

    def copy(self, src, dst, device):
        return Transfer(self, src, dst, device)

    def greet(self):
        barrier = pltpu.get_barrier_semaphore()
        for device in self.peers():
            pl.semaphore_signal(barrier, inc=1, device_id=device, device_id_type=MESH)

    def greeted(self):
        pl.semaphore_wait(pltpu.get_barrier_semaphore(), len(self.peers()))

    def drain(self):
        for transfer in self.sent:
            transfer.left()


class RingGather:
    def __init__(self, links, buf):
        half = buf.shape[1] // 2
        own, left, right = links.z, links.zed(3), links.zed(1)

        def piece(member, part):
            return buf.at[member, part * half : (part + 1) * half]

        def move(member, part, step):
            return links.copy(piece(member, part), piece(member, part), links.to_z(step))

        self.first = [move(own, 0, 1), move(own, 1, 3), move(own, 1, 1), move(own, 0, 3)]
        self.second = [move(left, 0, 1), move(right, 1, 3)]

    def start(self):
        for transfer in self.first:
            transfer.start()

    def forward(self):
        for transfer, onward in zip(self.first[:2], self.second):
            transfer.arrived()
            onward.start()

    def near(self):
        for transfer in self.first[2:]:
            transfer.arrived()

    def far(self):
        for transfer in self.second:
            transfer.arrived()


class Shared:
    def __init__(self, links, source, target):
        small, half = target.shape[1] // 4, target.shape[2] // 2
        cols = pl.ds(pl.multiple_of(links.core * half, 128), half)

        def rows(chip):
            return pl.ds(pl.multiple_of(chip * small, 16), small)

        def move(chip, part, device):
            ref = target.at[2 * part : 2 * part + 2, rows(chip), cols]
            return links.copy(ref, ref, device)

        own = rows(links.chip)
        place = target.at[links.z, own, cols]
        place[...] = source(links.z, own)[...]
        self.cross = [
            links.copy(source(links.zed(step), own), place, links.to_z(step)) for step in (2, 1, 3)
        ]
        own, x, y = links.chip, links.chip_x, links.chip_y
        self.near = [
            move(own, 0, links.to_x),
            move(own, 1, links.to_y),
            move(own, 1, links.to_x),
            move(own, 0, links.to_y),
        ]
        self.onward = [move(x, 0, links.to_y), move(y, 1, links.to_x)]
        ref = target.at[:, :, cols]
        self.hand = links.copy(ref, ref, links.to_core)

    def start(self):
        for transfer in self.cross:
            transfer.start()

    def gather(self):
        for transfer in self.cross:
            transfer.arrived()
        for transfer in self.near:
            transfer.start()

    def forward(self):
        for transfer, onward in zip(self.near[:2], self.onward):
            transfer.arrived()
            onward.start()

    def give(self):
        for transfer in self.near[2:] + self.onward:
            transfer.arrived()
        self.hand.start()

    def finish(self):
        self.hand.arrived()


class ContextGather:
    def __init__(self, links, buf):
        half = buf.shape[2] // 2

        def move(chip, part, device):
            rows = slice(None) if part is None else slice(part * half, (part + 1) * half)
            ref = buf.at[links.core, chip, rows]
            return links.copy(ref, ref, device)

        own, x, y, d = links.chip, links.chip_x, links.chip_y, links.chip_d
        self.own_core = move(own, None, links.to_core)
        self.x_parts = [move(own, 0, links.to_x), move(own, 1, links.to_x)]
        self.y_parts = [move(own, 1, links.to_y), move(own, 0, links.to_y)]
        self.onward = [move(x, 0, links.to_y), move(y, 1, links.to_x)]
        self.x_core = move(x, None, links.to_core)
        self.y_core = move(y, None, links.to_core)
        self.d_core = move(d, None, links.to_core)

    def start(self):
        for transfer in (
            self.x_parts[0],
            self.y_parts[0],
            self.own_core,
            self.x_parts[1],
            self.y_parts[1],
        ):
            transfer.start()

    def forward(self):
        self.x_parts[0].arrived()
        self.onward[0].start()
        self.y_parts[0].arrived()
        self.onward[1].start()

    def hand_near(self):
        self.x_parts[1].arrived()
        self.x_core.start()
        self.y_parts[1].arrived()
        self.y_core.start()

    def hand_far(self):
        self.onward[0].arrived()
        self.onward[1].arrived()
        self.d_core.start()


class DirectGather:
    def __init__(self, links, buf):
        def move(chip, device):
            ref = buf.at[links.core, chip]
            return links.copy(ref, ref, device)

        self.first = [move(links.chip, device) for device in (links.to_d, links.to_x, links.to_y)]
        self.own_core = move(links.chip, links.to_core)
        self.hands = [
            move(chip, links.to_core) for chip in (links.chip_d, links.chip_x, links.chip_y)
        ]

    def start(self):
        for transfer in self.first + [self.own_core]:
            transfer.start()

    def finish(self):
        for k in (1, 2, 0):
            self.first[k].arrived()
            self.hands[k].start()
        for transfer in [self.own_core] + self.hands:
            transfer.arrived()


def chosen(flag, shape):
    return jnp.full(shape, flag, jnp.int32) == 1


def masked_heads(value, first, width):
    rows, span = value.shape
    pieces = []
    if first > 0:
        pieces.append(jnp.zeros((rows, first), value.dtype))
    pieces.append(value)
    if first + span < width:
        pieces.append(jnp.zeros((rows, width - first - span), value.dtype))
    wide = jnp.concatenate(pieces, axis=1) if len(pieces) > 1 else value
    head = (lax.broadcasted_iota(jnp.int32, (rows, width), 1) - first + HEAD) // HEAD - 1
    return [
        jnp.where(head == index, wide.astype(F32), 0.0).astype(value.dtype)
        for index in range(span // HEAD)
    ]


def soft_step(scores, old_max, old_sum):
    new_max = jnp.maximum(old_max, jnp.max(scores, axis=0, keepdims=True))
    weights = jnp.exp(scores - new_max)
    factor = jnp.exp(old_max - new_max)
    new_sum = old_sum * factor + jnp.sum(weights, axis=0, keepdims=True)
    return weights.astype(B16), factor, new_max, new_sum


def forward_phase(
    links, ids, x, cot, qkvw, fcw, projw, v0, v1, v2, v3, v4, v5, qbias, vbias,
    attn_t, lse, qm, kv, x_all, w_all, cot_all, fc_all, proj_all, vec_all, norm1, normed1,
    stage, max_h, sum_h, acc_h, max_x, sum_x, acc_x,
):
    rows = x.shape[0]
    span = qkvw.shape[0]
    block = 2 * rows
    heads = span // HEAD
    z = links.z
    links.greet()
    x_all[z] = x[...]
    cot_all[z] = cot[...]
    own_vectors = jnp.concatenate(
        [v[...].astype(F32).reshape(1, span) for v in (v0, v1, v2, v3, v4, v5)]
        + [jnp.zeros((10, span), F32)],
        axis=0,
    )
    vec_all[z, :, :span] = own_vectors.astype(B16)
    for member in range(4):
        stage[member, :, : 3 * span] = jnp.concatenate(
            [qkvw[:, t * 4 * span + member * span : t * 4 * span + (member + 1) * span] for t in range(3)],
            axis=1,
        )

    vectors = [
        links.copy(vec_all.at[z], vec_all.at[z], links.to_z(step)) for step in (1, 3, 2)
    ]
    inputs = RingGather(links, x_all)
    half = cot.shape[1] // 2

    def own_cols(first):
        return pl.ds(pl.multiple_of(first + links.core * half, 128), half)

    weights = Shared(links, lambda member, at: stage.at[member, at, own_cols(0)], w_all)
    cots = RingGather(links, cot_all)
    fcs_in = Shared(links, lambda member, at: fcw.at[at, own_cols(member * 2 * half)], fc_all)
    projs = Shared(links, lambda member, at: projw.at[at, own_cols(0)], proj_all)
    context = ContextGather(links, kv)

    links.greeted()
    for transfer in vectors:
        transfer.start()
    weights.start()
    inputs.start()
    for transfer in vectors:
        transfer.arrived()

    gain = jnp.concatenate([vec_all[m, 0:1, :span] for m in range(4)], axis=1).astype(F32)
    shift = jnp.concatenate([vec_all[m, 1:2, :span] for m in range(4)], axis=1).astype(F32)

    def normalise(member):
        shifted, normed, _ = layer_norm(x_all[member].astype(F32), gain, shift)
        at = pl.ds(pl.multiple_of(member * rows, rows), rows)
        norm1[at, :] = shifted.astype(B16)
        normed1[at, :] = normed

    normalise(z)
    inputs.forward()
    weights.gather()
    fcs_in.start()
    projs.start()
    inputs.near()
    normalise(links.zed(1))
    normalise(links.zed(3))
    weights.forward()
    inputs.far()
    cots.start()
    normalise(links.zed(2))
    weights.give()
    fcs_in.gather()
    weights.finish()

    matrix = w_all[...].reshape(4 * span, w_all.shape[2])[:, : 3 * span]
    for part in range(2):
        at = slice(part * block, (part + 1) * block)
        product = jnp.dot(norm1[at, :], matrix, preferred_element_type=F32)
        query = (product[:, :span] + qbias[...].astype(F32).reshape(1, span)).astype(B16)
        query = query * jnp.asarray(HEAD**-0.5, B16)
        for head, lone in enumerate(masked_heads(query, 0, 4 * HEAD)):
            qm[head, at, :] = lone
        values = product[:, 2 * span :] + vbias[...].astype(F32).reshape(1, span)
        kv[links.core, links.chip, at, :] = jnp.concatenate(
            [product[:, span : 2 * span], values], axis=1
        ).astype(B16)
    context.start()

    own_block = ids[2 * links.ctx]
    keep = lax.broadcasted_iota(jnp.int32, (block, block), 0) <= lax.broadcasted_iota(
        jnp.int32, (block, block), 1
    )
    none = jnp.full((1, block), NEG_FILL, F32)
    zero = jnp.zeros((1, block), F32)

    def halves(core, chip, part):
        at = slice(part * block, (part + 1) * block)
        return kv[core, chip, at, : 4 * HEAD], kv[core, chip, at, 2 * HEAD :].T

    def value_rows(head):
        return slice((1 + head) * HEAD, (2 + head) * HEAD)

    def head_rows(head):
        return slice(head * HEAD, (head + 1) * HEAD)

    k_low, vt_low = halves(links.core, links.chip, 0)
    k_high, vt_high = halves(links.core, links.chip, 1)
    for head in range(heads):
        q_low, q_high = qm[head, :block, :], qm[head, block:, :]
        scores = jnp.where(keep, transposed_product(k_low, q_low), NEG_FILL)
        w, _, top, total = soft_step(scores, none, zero)
        max_x[0, head : head + 1, :] = top
        sum_x[0, head : head + 1, :] = total
        acc_x[0, head_rows(head), :] = jnp.dot(
            vt_low[value_rows(head)], w, preferred_element_type=F32
        )
        scores = transposed_product(k_low, q_high)
        w, _, top, total = soft_step(scores, none, zero)
        acc = jnp.dot(vt_low[value_rows(head)], w, preferred_element_type=F32)
        scores = jnp.where(keep, transposed_product(k_high, q_high), NEG_FILL)
        w, factor, top, total = soft_step(scores, top, total)
        max_h[head : head + 1, :] = top
        sum_h[head : head + 1, :] = total
        acc_h[head_rows(head), :] = acc * factor + jnp.dot(
            vt_high[value_rows(head)], w, preferred_element_type=F32
        )
    max_x[1] = jnp.full_like(max_h, NEG_FILL)
    sum_x[1] = jnp.zeros_like(sum_h)
    acc_x[1] = jnp.zeros_like(acc_h)

    def hop(index, carry):
        near = index < 3
        far = index >= 5
        core = jnp.where((index == 1) | (index == 2) | (index == 5), links.core, links.other)
        chip = jnp.where(
            index == 0,
            links.chip,
            jnp.where(far, links.chip_d, jnp.where(lax.rem(index, 2) == 1, links.chip_x, links.chip_y)),
        )

        @pl.when(index == 0)
        def _():
            context.own_core.arrived()
            fcs_in.forward()
            context.forward()

        @pl.when(index == 1)
        def _():
            context.hand_near()
            cots.forward()

        @pl.when(index == 2)
        def _():
            projs.gather()

        @pl.when(index == 3)
        def _():
            context.x_core.arrived()
            context.hand_far()

        @pl.when(index == 4)
        def _():
            context.y_core.arrived()
            cots.near()
            fcs_in.give()

        @pl.when(index == 5)
        def _():
            projs.forward()

        @pl.when(index == 6)
        def _():
            context.d_core.arrived()

        block_id = ids[2 * (2 * chip + core)]
        low = (block_id < own_block).astype(jnp.int32)
        in_low = chosen(low, (1, block))
        kv_low = kv[core, chip, :block, :]
        kv_high = kv[core, chip, block:, :]
        kv_pick = jnp.where(chosen(low, kv_low.shape), kv_low, kv_high)
        q_mask = chosen(low, (block, 4 * HEAD))
        work = []
        for head in range(heads):
            scores = transposed_product(kv_low[:, : 4 * HEAD], qm[head, block:, :])
            work.append((scores, max_h[head : head + 1, :], sum_h[head : head + 1, :]))
        for head in range(heads):
            q_pick = jnp.where(q_mask, qm[head, :block, :], qm[head, block:, :])
            scores = transposed_product(kv_pick[:, : 4 * HEAD], q_pick)
            at = slice(head, head + 1)
            work.append(
                (
                    scores,
                    jnp.where(in_low, max_x[0, at, :], max_x[1, at, :]),
                    jnp.where(in_low, sum_x[0, at, :], sum_x[1, at, :]),
                )
            )
        done = [soft_step(*entry) for entry in work]
        vt = kv_low[:, 2 * HEAD :].T
        for head in range(heads):
            w, factor, top, total = done[head]
            max_h[head : head + 1, :] = top
            sum_h[head : head + 1, :] = total
            acc_h[head_rows(head), :] = acc_h[head_rows(head), :] * factor + jnp.dot(
                vt[value_rows(head)], w, preferred_element_type=F32
            )
        vt = kv_pick[:, 2 * HEAD :].T
        for head in range(heads):
            w, factor, top, total = done[heads + head]
            acc = jnp.where(in_low, acc_x[0, head_rows(head), :], acc_x[1, head_rows(head), :])
            acc = acc * factor + jnp.dot(
                vt[value_rows(head)], w, preferred_element_type=F32
            )
            for part in range(2):
                own = in_low if part == 0 else ~in_low
                max_x[part, head : head + 1, :] = jnp.where(own, top, max_x[part, head : head + 1, :])
                sum_x[part, head : head + 1, :] = jnp.where(
                    own, total, sum_x[part, head : head + 1, :]
                )
                acc_x[part, head_rows(head), :] = jnp.where(own, acc, acc_x[part, head_rows(head), :])
        return carry

    lax.fori_loop(0, 7, hop, 0)
    for head in range(heads):
        at = slice(head, head + 1)
        total = sum_x[0, at, :]
        attn_t[head_rows(head), :block] = (acc_x[0, head_rows(head), :] / total).astype(B16)
        lse[at, :block] = max_x[0, at, :] + jnp.log(total)
        top = jnp.maximum(max_h[at, :], max_x[1, at, :])
        left, right = jnp.exp(max_h[at, :] - top), jnp.exp(max_x[1, at, :] - top)
        total = sum_h[at, :] * left + sum_x[1, at, :] * right
        acc = acc_h[head_rows(head), :] * left + acc_x[1, head_rows(head), :] * right
        attn_t[head_rows(head), block:] = (acc / total).astype(B16)
        lse[at, block:] = top + jnp.log(total)
    return cots, fcs_in, projs


def parts_of(rows):
    first = (rows // 2 + 15) // 16 * 16
    return [slice(0, first), slice(first, rows)]


class FourSum:
    def __init__(self, links, parts, early, late, far, own, near):
        self.parts, self.early, self.late, self.own, self.near = parts, early, late, own, near
        self.cuts = parts_of(early.shape[0])
        self.far = [
            links.copy(parts.at[far, self.cuts[k]], early.at[self.cuts[k]], near[k][0]) for k in range(2)
        ]
        self.ready, self.summed = [], []
        for k, (device, part, added) in enumerate(near):
            for half, group in ((1 - added, self.ready), (added, self.summed)):
                cut = self.cuts[half]
                group.append(links.copy(parts.at[part, cut], late.at[k, cut], device))

    def send_far(self):
        for transfer in self.far:
            transfer.start()

    def send_ready(self):
        for transfer in self.ready:
            transfer.start()

    def send_summed(self):
        for k, (_, part, added) in enumerate(self.near):
            cut = self.cuts[added]
            self.far[added].arrived()
            both = self.parts[part, cut].astype(F32) + self.early[cut].astype(F32)
            self.parts[part, cut] = both.astype(B16)
            self.summed[k].start()

    def total(self):
        for transfer in self.ready + self.summed:
            transfer.arrived()
        return (
            self.parts[self.own].astype(F32)
            + self.late[0].astype(F32)
            + self.late[1].astype(F32)
        )


class ThreeSum:
    def __init__(self, links, parts, late, own, targets):
        self.parts, self.late, self.own = parts, late, own
        self.sends = [
            links.copy(parts.at[part], late.at[k], device) for k, (device, part) in enumerate(targets)
        ]

    def total(self):
        value = self.parts[self.own].astype(F32)
        for k in (1, 2, 0):
            self.sends[k].arrived()
            value = value + self.late[k].astype(F32)
        return value


def ring_sum(links, parts, early, late):
    right, left = links.zed(1), links.zed(3)
    near = [(links.to_z(1), right, 0), (links.to_z(3), left, 1)]
    return FourSum(links, parts, early, late, links.zed(2), links.z, near)


class ContextSum:
    def __init__(self, links, grads, handed, early, late):
        self.links, self.grads, self.handed = links, grads, handed
        order = (links.chip_d, links.chip_x, links.chip_y, links.chip)
        self.order = order
        self.hands = [
            links.copy(grads.at[links.other, chip], handed.at[k], links.to_core)
            for k, chip in enumerate(order)
        ]
        if early is None:
            targets = [(links.to_d, order[0]), (links.to_x, order[1]), (links.to_y, order[2])]
            self.four = ThreeSum(links, grads.at[links.core], late, links.chip, targets)
            return
        near = [(links.to_x, links.chip_x, 1), (links.to_y, links.chip_y, 0)]
        self.four = FourSum(
            links, grads.at[links.core], early, late, links.chip_d, links.chip, near
        )

    def hand(self, k):
        self.hands[k].start()

    def merge(self, k):
        self.hands[k].arrived()
        core, chip = self.links.core, self.order[k]
        both = self.grads[core, chip].astype(F32) + self.handed[k].astype(F32)
        self.grads[core, chip] = both.astype(B16)


def backward_phase(
    links, arriving, ids, attn_t, lse, qm, kv, x_all, w_all, cot_all, fc_all, proj_all, vec_all, norm1, projw, outw, fcb,
    block_out, input_grad, h_mlp, h_attn, sums, normed1,
    a_all, grad_act, norm2, act, grad_pre, gn2, gn2_e, gn2_l, mlp, mlp_e, mlp_l, gn1, gn1_e, gn1_l,
    gm_all, gm_own, mid_own, dkv, dkv_h, dkv_e, dkv_l, g_mlp, gmlp_h, gmlp_e, gmlp_l,
    g_attn, gattn_h, gattn_l, fc_piece, qkv_piece, dom, delta, dq, gqkv, zsum, bsum, ssum, rowsum,
):
    members, rows, width = x_all.shape
    span = attn_t.shape[0]
    group = members * rows
    block = group // 2
    heads = span // HEAD
    half = width // 2
    small = span // 4
    z = links.z
    right, left, opposite = links.zed(1), links.zed(3), links.zed(2)

    def row(index):
        return jnp.concatenate(
            [vec_all[m, index : index + 1, :span] for m in range(members)], axis=1
        ).astype(F32)

    def head_rows(head):
        return slice(head * HEAD, (head + 1) * HEAD)

    def member_rows(member):
        return pl.ds(pl.multiple_of(member * rows, rows), rows)

    def pair(index):
        first = index == 0
        return jnp.where(first, opposite, left), jnp.where(first, right, z)

    def both_rows(ref, ats):
        return jnp.concatenate([ref[at, :] for at in ats], axis=0)

    attns = RingGather(links, a_all)
    gms = RingGather(links, gm_all)
    ring_gn2 = ring_sum(links, gn2, gn2_e, gn2_l)
    ring_mlp = ring_sum(links, mlp, mlp_e, mlp_l)
    ring_gn1 = ring_sum(links, gn1, gn1_e, gn1_l)
    sum_mlp = ContextSum(links, g_mlp, gmlp_h, gmlp_e, gmlp_l)
    sum_attn = ContextSum(links, g_attn, gattn_h, None, gattn_l)
    sum_kv = ContextSum(links, dkv, dkv_h, dkv_e, dkv_l)
    gather_mlp = ContextGather(links, h_mlp)
    gather_attn = DirectGather(links, h_attn)

    def spread(piece, gathered, first):
        at = pl.ds(pl.multiple_of(first + small * z, 16), small)
        place = gathered.at[links.core, links.chip, at]
        return [links.copy(piece.at[links.zed(s)], place, links.to_z(s)) for s in (1, 3, 2)]

    spread_fc = spread(fc_piece, h_mlp, span)
    spread_qkv = spread(qkv_piece, h_attn, 0)

    cots, fcs_in, projs = arriving
    gain_one = row(0)
    gain_two, shift_two = row(3), row(4)
    proj_bias, out_bias = row(2), row(5)
    fc_bias = fcb[...].astype(F32).reshape(1, fcb.shape[0])
    attns.start()
    projs.give()
    cots.far()
    one, zero_shift = jnp.ones((1, width), F32), jnp.zeros((1, width), F32)

    def before(index, carry):
        cots_of = cot_all[pl.ds(2 * index, 2)].reshape(block, width)
        at = pl.ds(pl.multiple_of(index * block, block), block)
        grad_act[at, :] = transposed_product(cots_of, outw[...])
        return carry

    lax.fori_loop(0, 1, before, 0)
    attns.forward()
    lax.fori_loop(1, 2, before, 0)
    attns.near()
    attns.far()
    fcs_in.finish()
    projs.finish()
    rowsum[...] = jnp.zeros_like(rowsum)
    fc_matrix = fc_all.shape

    def mlp_block(index, carry):
        members_of = pair(index)
        ats = [member_rows(member) for member in members_of]
        attn_cols = jnp.concatenate([a_all[:, :, at].reshape(width, rows) for at in ats], axis=1)
        inputs_of = jnp.concatenate([x_all[member] for member in members_of], axis=0)
        middle = (
            inputs_of.astype(F32)
            + rows_product(attn_cols, proj_all[...].reshape(width, width))
            + proj_bias
        )
        shifted, normed, _ = layer_norm(middle, gain_two, shift_two)
        half_norm = shifted.astype(B16)
        fc = fc_all[...].reshape(width, fc_matrix[2])
        pre_act = jnp.dot(half_norm, fc, preferred_element_type=F32) + fc_bias
        squared = pre_act * pre_act
        tanh_value = jnp.tanh(GELU_C * pre_act * (1.0 + GELU_K * squared))
        act_half = (0.5 * pre_act * (1.0 + tanh_value)).astype(B16)
        slope = 0.5 * (1.0 + tanh_value) + (0.5 * GELU_C) * pre_act * (
            1.0 - tanh_value * tanh_value
        ) * (1.0 + 3.0 * GELU_K * squared)
        grad = both_rows(grad_act, ats) * slope
        rowsum[7:8, :] += jnp.sum(grad, axis=0, keepdims=True)
        grad_half = grad.astype(B16)
        back = transposed_product(grad_half, fc)
        rowsum[3:4, :] += jnp.sum(back * normed, axis=0, keepdims=True)
        rowsum[4:5, :] += jnp.sum(back, axis=0, keepdims=True)
        back_half = back.astype(B16)
        for k in range(2):
            part = slice(k * rows, (k + 1) * rows)
            gn2[members_of[k]] = back_half[part]
            norm2[ats[k], :] = half_norm[part]
            act[ats[k], :] = act_half[part]
            grad_pre[ats[k], :] = grad_half[part]

        @pl.when(index == 0)
        def _():
            ring_gn2.send_far()
            ring_gn2.ready[0].start()

        @pl.when(index == 1)
        def _():
            ring_gn2.ready[1].start()
            ring_gn2.send_summed()
            mid_own[...] = middle[rows:]

        return carry

    lax.fori_loop(0, 2, mlp_block, 0)

    def mlp_weights(core):
        cols = pl.ds(pl.multiple_of(core * half, half), half)
        cots = cot_all[:, :, cols].reshape(group, half)
        product = rows_product(act[...], cots).astype(B16)
        g_mlp[core, :, :span, :] = product.reshape(4, span, half)
        product = rows_product(norm2[...], grad_pre[:, cols]).astype(B16)
        product = product.reshape(members, 4, small, half)
        for member in range(members):
            at = span + member * small
            g_mlp[core, :, at : at + small, :] = product[member]

    mlp_weights(links.other)
    for k in range(4):
        sum_mlp.hand(k)
    mlp_weights(links.core)
    sum_mlp.merge(0)
    sum_mlp.four.send_far()
    sum_mlp.merge(1)
    sum_mlp.merge(2)
    sum_mlp.four.send_ready()

    grad_norm2 = ring_gn2.total()
    _, normed, inv_std = layer_norm(mid_own[...], gain_two, shift_two)
    cot_own = cot_all[z].astype(F32)
    grad_middle = cot_own + norm_backward(grad_norm2, gain_two, normed, inv_std)
    gm_own[...] = grad_middle
    gm_all[z] = grad_middle.astype(B16)
    gms.start()
    rowsum[2:3, :] = jnp.sum(grad_middle, axis=0, keepdims=True)
    rowsum[5:6, :] = jnp.sum(cot_own, axis=0, keepdims=True)

    sum_mlp.four.send_summed()
    sum_mlp.merge(3)
    gms.forward()

    def mlp_product(index, carry):
        at = pl.ds(pl.multiple_of(index * block, block), block)
        product = jnp.dot(act[at, :], outw[...], preferred_element_type=F32).astype(B16)
        mlp[pl.ds(2 * index, 2)] = product.reshape(2, rows, width)
        return carry

    lax.fori_loop(0, 2, mlp_product, 0)
    gms.near()
    gms.far()
    ring_mlp.send_far()
    ring_mlp.send_ready()
    grad_mid = gm_all[...].reshape(group, width)
    grad_attn_t = transposed_product(projw[...], grad_mid).astype(B16).astype(F32)
    delta_rows = grad_attn_t * attn_t[...].astype(F32)
    for head in range(heads):
        delta[head : head + 1, :] = jnp.sum(delta_rows[head_rows(head), :], axis=0, keepdims=True)
    grad_attn = transposed_product(grad_mid, projw[...]).astype(B16)
    for head, lone in enumerate(masked_heads(grad_attn, HEAD, 4 * HEAD)):
        dom[head] = lone
    product = jnp.dot(attn_t[...], grad_mid, preferred_element_type=F32).astype(B16)
    for core in range(2):
        g_attn[core, :, span:, :] = product[:, core * half : (core + 1) * half].reshape(4, small, half)
    dq[...] = jnp.zeros_like(dq)

    own_block = ids[2 * links.ctx]
    keep = lax.broadcasted_iota(jnp.int32, (block, block), 0) <= lax.broadcasted_iota(
        jnp.int32, (block, block), 1
    )
    low_rows, high_rows = slice(0, block), slice(block, group)

    def tile(keys, queries, grads, lse_of, delta_of, masked=False):
        probs, scores_grad = [], []
        for head in range(heads):
            scores = transposed_product(keys[:, : 4 * HEAD], queries[head])
            if masked:
                scores = jnp.where(keep, scores, NEG_FILL)
            weights = jnp.exp(scores - lse_of(head))
            grad_probs = transposed_product(keys[:, 2 * HEAD :], grads[head])
            probs.append(weights.astype(B16))
            scores_grad.append((weights * (grad_probs - delta_of(head))).astype(B16))
        keys_t = keys[:, : 4 * HEAD].T
        query_grad = [
            jnp.dot(keys_t[head_rows(head)], scores_grad[head], preferred_element_type=F32)
            for head in range(heads)
        ]
        value_grad = jnp.dot(
            jnp.concatenate(probs, axis=1),
            jnp.concatenate(grads, axis=0),
            preferred_element_type=F32,
        )
        key_grad = jnp.dot(
            jnp.concatenate(scores_grad, axis=1),
            jnp.concatenate(queries, axis=0),
            preferred_element_type=F32,
        )
        both = jnp.concatenate(
            [
                key_grad[:, : 2 * HEAD],
                key_grad[:, 2 * HEAD :] + value_grad[:, : 2 * HEAD],
                value_grad[:, 2 * HEAD :],
            ],
            axis=1,
        )
        return query_grad, both

    def stacked(ref, at):
        return [ref[head, at, :] for head in range(heads)]

    def rows_at(ref, at):
        return lambda head: ref[head : head + 1, at]

    def hop(index, carry):
        chip = jnp.where(
            index < 2,
            links.chip_d,
            jnp.where(index < 4, links.chip_x, jnp.where(index < 6, links.chip_y, links.chip)),
        )
        core = jnp.where(lax.rem(index, 2) == 0, links.other, links.core)

        @pl.when(index == 1)
        def _():
            sum_kv.hand(0)
            ring_mlp.send_summed()

        @pl.when(index == 2)
        def _():
            sum_kv.merge(0)
            sum_kv.four.send_far()

        @pl.when(index == 3)
        def _():
            sum_kv.hand(1)
            total = sum_mlp.four.total().astype(B16)
            h_mlp[links.core, links.chip, :span, :] = total[:span]
            fc_piece[...] = total[span:].reshape(members, small, half)
            own = pl.ds(pl.multiple_of(span + small * z, 16), small)
            h_mlp[links.core, links.chip, own, :] = fc_piece[z]
            for transfer in spread_fc:
                transfer.start()

        @pl.when(index == 4)
        def _():
            sum_kv.merge(1)
            sum_kv.four.ready[0].start()

        @pl.when(index == 5)
        def _():
            sum_kv.hand(2)

        @pl.when(index == 6)
        def _():
            sum_kv.merge(2)
            sum_kv.four.ready[1].start()
            sum_kv.four.send_summed()
            for transfer in spread_fc:
                transfer.arrived()
            gather_mlp.start()

        block_id = ids[2 * (2 * chip + core)]
        low = (block_id < own_block).astype(jnp.int32)
        in_low = chosen(low, (1, block))
        kv_low = kv[core, chip, low_rows, :]
        kv_pick = jnp.where(chosen(low, kv_low.shape), kv_low, kv[core, chip, high_rows, :])
        q_mask = chosen(low, (block, 4 * HEAD))

        def pick(ref):
            return [
                jnp.where(q_mask, ref[head, low_rows, :], ref[head, high_rows, :])
                for head in range(heads)
            ]

        def pick_row(ref):
            return lambda head: jnp.where(
                in_low, ref[head : head + 1, low_rows], ref[head : head + 1, high_rows]
            )

        query_grad, first = tile(
            kv_low,
            stacked(qm, high_rows),
            stacked(dom, high_rows),
            rows_at(lse, high_rows),
            rows_at(delta, high_rows),
        )
        for head in range(heads):
            dq[1, head_rows(head), :] += query_grad[head]
        query_grad, second = tile(kv_pick, pick(qm), pick(dom), pick_row(lse), pick_row(delta))
        for head in range(heads):
            at = head_rows(head)
            dq[0, at, :] += jnp.where(in_low, query_grad[head], 0.0)
            dq[1, at, :] += jnp.where(in_low, 0.0, query_grad[head])
        mask = chosen(low, second.shape)
        dkv[core, chip, low_rows, :] = (first + jnp.where(mask, second, 0.0)).astype(B16)
        dkv[core, chip, high_rows, :] = jnp.where(mask, 0.0, second).astype(B16)
        return carry

    lax.fori_loop(0, 7, hop, 0)
    sum_kv.hand(3)
    block_out[...] = ring_mlp.total() + mid_own[...] + out_bias
    for keys_at, queries_at, masked in (
        (low_rows, high_rows, False),
        (low_rows, low_rows, True),
        (high_rows, high_rows, True),
    ):
        query_grad, both = tile(
            kv[links.core, links.chip, keys_at, :],
            stacked(qm, queries_at),
            stacked(dom, queries_at),
            rows_at(lse, queries_at),
            rows_at(delta, queries_at),
            masked,
        )
        part = 0 if queries_at is low_rows else 1
        for head in range(heads):
            dq[part, head_rows(head), :] += query_grad[head]
        if keys_at is low_rows and not masked:
            held = both
        elif keys_at is low_rows:
            dkv[links.core, links.chip, keys_at, :] = (held + both).astype(B16)
        else:
            dkv[links.core, links.chip, keys_at, :] = both.astype(B16)

    grad_query = jnp.concatenate([dq[0].T, dq[1].T], axis=0) * HEAD**-0.5
    sum_kv.merge(3)
    own_kv = sum_kv.four.total().astype(B16)
    split = jnp.concatenate(
        [
            jnp.sum(grad_query, axis=0, keepdims=True),
            jnp.sum(own_kv[:, span:].astype(F32), axis=0, keepdims=True),
            jnp.zeros((1, width - 2 * span), F32),
        ],
        axis=1,
    )
    rowsum[6:7, :] = split
    gqkv[...] = jnp.concatenate(
        [grad_query.astype(B16), own_kv, jnp.zeros((group, 640 - 3 * span), B16)], axis=1
    )

    def attn_weights(core):
        cols = pl.ds(pl.multiple_of(core * 256, 256), half)
        product = rows_product(norm1[...], gqkv[:, cols]).astype(B16)
        product = product.reshape(members, 4, small, half)
        for member in range(members):
            g_attn[core, :, member * small : (member + 1) * small, :] = product[member]

    attn_weights(links.other)
    for k in range(4):
        sum_attn.hand(k)
    attn_weights(links.core)
    for k in range(3):
        sum_attn.merge(k)
        sum_attn.four.sends[k].start()
    gather_mlp.forward()

    def norm1_block(index, carry):
        members_of = pair(index)
        ats = [member_rows(member) for member in members_of]
        back = transposed_product(
            both_rows(gqkv, ats)[:, : 3 * span], w_all[...].reshape(width, width)[:, : 3 * span]
        )
        rowsum[0:1, :] += jnp.sum(back * both_rows(normed1, ats), axis=0, keepdims=True)
        rowsum[1:2, :] += jnp.sum(back, axis=0, keepdims=True)
        back_half = back.astype(B16)
        for k in range(2):
            gn1[members_of[k]] = back_half[k * rows : (k + 1) * rows]

        @pl.when(index == 0)
        def _():
            ring_gn1.send_far()
            ring_gn1.ready[0].start()

        @pl.when(index == 1)
        def _():
            ring_gn1.ready[1].start()

        return carry

    lax.fori_loop(0, 2, norm1_block, 0)
    ring_gn1.send_summed()
    zsum[z] = rowsum[...]
    z_sums = [links.copy(zsum.at[z], zsum.at[z], links.to_z(s)) for s in (1, 3, 2)]
    for transfer in z_sums:
        transfer.start()
    sum_attn.merge(3)
    gather_mlp.hand_near()
    for transfer in z_sums:
        transfer.arrived()
    index = lax.broadcasted_iota(jnp.int32, rowsum.shape, 0)
    value = zsum[0] + zsum[1] + zsum[2] + zsum[3]
    value = jnp.where(index < 6, value, zsum[z])
    ssum[0] = value
    steps = [
        links.copy(ssum.at[k], bsum.at[k], device)
        for k, device in enumerate((links.to_core, links.to_x, links.to_y))
    ]
    steps[0].start()

    grad_norm1 = ring_gn1.total()
    _, normed, inv_std = layer_norm(x_all[z].astype(F32), one, zero_shift)
    input_grad[...] = gm_own[...] + norm_backward(grad_norm1, gain_one, normed, inv_std)

    steps[0].arrived()
    ssum[1] = ssum[0] + bsum[0]
    steps[1].start()
    total = sum_attn.four.total().astype(B16)
    h_attn[links.core, links.chip, span:, :] = total[span:]
    qkv_piece[...] = total[:span].reshape(members, small, half)
    own = pl.ds(pl.multiple_of(small * z, 16), small)
    h_attn[links.core, links.chip, own, :] = qkv_piece[z]
    for transfer in spread_qkv:
        transfer.start()
    steps[1].arrived()
    ssum[2] = ssum[1] + bsum[1]
    steps[2].start()
    for transfer in spread_qkv:
        transfer.arrived()
    gather_attn.start()
    steps[2].arrived()
    total = ssum[2] + bsum[2]
    mine = total[:, :span]
    for m in range(1, members):
        mine = jnp.where(
            chosen((z == m).astype(jnp.int32), mine.shape), total[:, m * span : (m + 1) * span], mine
        )
    sums[:6, :span] = mine[:6]
    sums[6:8, :] = total[6:8]
    gather_mlp.hand_far()
    gather_attn.finish()
    gather_mlp.own_core.arrived()
    gather_mlp.x_core.arrived()
    gather_mlp.y_core.arrived()
    gather_mlp.d_core.arrived()


def block_kernel(*refs):
    ids, x, cot, qkvw, fcw, projw = refs[:6]
    vectors = refs[6:14]
    outw, fcb = refs[14:16]
    outs = refs[16:21]
    lse, qm, kv, x_all, w_all, cot_all, fc_all, proj_all, vec_all, norm1, normed1 = refs[21:32]
    front = refs[32:39]
    a_all = refs[39]
    links = Links(*refs[-2:])
    attn_t = a_all.at[links.z]
    shared = (lse, qm, kv, x_all, w_all, cot_all, fc_all, proj_all, vec_all, norm1)
    arriving = forward_phase(
        links, ids, x, cot, qkvw, fcw, projw, *vectors, attn_t, *shared, normed1, *front
    )
    backward_phase(
        links, arriving, ids, attn_t, *shared, projw, outw, fcb, *outs, normed1, *refs[39:-2]
    )
    links.drain()


def block_call(ids, x, cot, qkvw, fcw, projw, *vectors):
    rows, width = x.shape
    members = 4
    span = qkvw.shape[0]
    group = members * rows
    block = group // 2
    heads = span // HEAD
    half = width // 2
    small = span // 4
    mlp_rows, attn_rows = 2 * span, span + small

    def shape(dims, dtype=B16):
        return jax.ShapeDtypeStruct(dims, dtype)

    def summed(rows_of, cols):
        return [
            VMEM((4, rows_of, cols), B16),
            VMEM((rows_of, cols), B16),
            VMEM((2, rows_of, cols), B16),
        ]

    def ring():
        return [
            VMEM((members, rows, width), B16),
            VMEM((rows, width), B16),
            VMEM((2, rows, width), B16),
        ]

    outs = (
        shape((rows, width), F32),
        shape((rows, width), F32),
        shape((2, 4, mlp_rows, half)),
        shape((2, 4, attn_rows, half)),
        shape((8, width), F32),
    )
    scratch = (
        [
            VMEM((8, group), F32),
            VMEM((heads, group, 4 * HEAD), B16),
            VMEM((2, 4, group, 2 * span), B16),
            VMEM((members, rows, width), B16),
            VMEM((members, span, width), B16),
            VMEM((members, rows, width), B16),
            VMEM((members, span, width), B16),
            VMEM((members, span, width), B16),
            VMEM((members, 16, 256), B16),
            VMEM((group, width), B16),
            VMEM((group, width), F32),
            VMEM((members, span, width), B16),
            VMEM((8, block), F32),
            VMEM((8, block), F32),
            VMEM((span, block), F32),
            VMEM((2, 8, block), F32),
            VMEM((2, 8, block), F32),
            VMEM((2, span, block), F32),
            VMEM((members, span, group), B16),
            VMEM((group, width), F32),
            VMEM((group, width), B16),
            VMEM((group, width), B16),
            VMEM((group, width), B16),
        ]
        + ring()
        + ring()
        + ring()
        + [
            VMEM((members, rows, width), B16),
            VMEM((rows, width), F32),
            VMEM((rows, width), F32),
            VMEM((2, 4, group, 2 * span), B16),
        ]
        + summed(group, 2 * span)
        + [VMEM((2, 4, mlp_rows, half), B16)]
        + summed(mlp_rows, half)
        + [VMEM((2, 4, attn_rows, half), B16)]
        + [VMEM((4, attn_rows, half), B16), VMEM((3, attn_rows, half), B16)]
        + [
            VMEM((members, small, half), B16),
            VMEM((members, small, half), B16),
            VMEM((heads, group, 4 * HEAD), B16),
            VMEM((8, group), F32),
            VMEM((2, span, block), F32),
            VMEM((group, 640), B16),
            VMEM((members, 8, width), F32),
            VMEM((3, 8, width), F32),
            VMEM((3, 8, width), F32),
            VMEM((8, width), F32),
            pltpu.SemaphoreType.DMA((160,)),
            pltpu.SemaphoreType.DMA((160,)),
        ]
    )
    args = (ids, x, cot, qkvw, fcw, projw) + vectors
    return pl.pallas_call(
        block_kernel,
        out_shape=outs,
        in_specs=[pl.BlockSpec(memory_space=SMEM)] + [pl.BlockSpec(memory_space=VMEM)] * (len(args) - 1),
        out_specs=(pl.BlockSpec(memory_space=VMEM),) * len(outs),
        scratch_shapes=scratch,
        compiler_params=pltpu.CompilerParams(
            collective_id=0, has_side_effects=True, vmem_limit_bytes=62 << 20
        ),
        name="block",
    )(*args)


def assemble_kernel(
    block_in, grad_in, h_mlp, h_attn, sums,
    block_out, grad_out, gain1, bias1, qkv, qbias, vbias, proj, pbias, gain2, bias2, fc, fbias, out, obias,
):
    small, width = proj.shape
    span = 4 * small
    half = width // 2
    block_out[...] = block_in[...]
    grad_out[...] = grad_in[...]
    for ref, index in ((gain1, 0), (bias1, 1), (pbias, 2), (gain2, 3), (bias2, 4), (obias, 5)):
        ref[...] = sums[index : index + 1, :span].reshape(span)
    qbias[...] = sums[6:7, :span].reshape(span)
    vbias[...] = sums[6:7, span : 2 * span].reshape(span)
    fbias[...] = sums[7:8, :].reshape(width)
    for core in range(2):
        cols = slice(core * half, (core + 1) * half)
        out[:, cols] = h_mlp[core, 0, :span, :].astype(F32)
        proj[:, cols] = h_attn[core, 0, span:, :].astype(F32)
        for member in range(4):
            at = span + member * small
            first = member * width + core * half
            fc[:, first : first + half] = h_mlp[core, 0, at : at + small, :].astype(F32)
    pieces = []
    for member in range(4):
        at = slice(member * small, (member + 1) * small)
        pieces.append(
            jnp.concatenate(
                [h_attn[0, 0, at, :], h_attn[1, 0, at, 128 : 3 * span - 256]], axis=1
            ).astype(F32)
        )
    qkv[...] = jnp.concatenate(
        [piece[:, t * span : (t + 1) * span] for t in range(3) for piece in pieces], axis=1
    )


def assemble(block_in, grad_in, h_mlp, h_attn, sums):
    width = block_in.shape[1]
    span = width // 4

    def shape(*dims):
        return jax.ShapeDtypeStruct(dims, F32)

    narrow = shape(span)
    outs = (
        shape(*block_in.shape), shape(*block_in.shape), narrow, narrow, shape(span, 3 * width), narrow, narrow,
        shape(span, width), narrow, narrow, narrow, shape(span, 4 * width), shape(width), shape(width, width),
        narrow,
    )
    def in_rows(array):
        if len(array.shape) == 1:
            return pl.BlockSpec(array.shape, lambda chip: (0,))
        return pl.BlockSpec((array.shape[0] // 4, array.shape[1]), lambda chip: (chip, 0))

    def of_chip(array):
        return pl.BlockSpec((2, 1) + array.shape[2:], lambda chip: (0, chip, 0, 0))

    return pl.pallas_call(
        assemble_kernel,
        out_shape=outs,
        grid=(4,),
        in_specs=[
            in_rows(block_in),
            in_rows(grad_in),
            of_chip(h_mlp),
            of_chip(h_attn),
            pl.BlockSpec(sums.shape, lambda chip: (0, 0)),
        ],
        out_specs=tuple(in_rows(array) for array in outs),
        compiler_params=pltpu.CompilerParams(vmem_limit_bytes=62 << 20),
        name="assemble",
    )(block_in, grad_in, h_mlp, h_attn, sums)


def head_shards(
    block_input,
    positions,
    norm1_gain,
    norm1_bias,
    qkv_weight,
    query_bias,
    value_bias,
    proj_weight,
    proj_bias,
    norm2_gain,
    norm2_bias,
    fc_weight,
    fc_bias,
    out_weight,
    out_bias,
    cotangent,
):
    rows, width = block_input.shape
    ids = positions.reshape(-1, 2 * rows)[:, 0] // (2 * rows)
    results = block_call(
        ids, block_input, cotangent, qkv_weight, fc_weight, proj_weight, norm1_gain, norm1_bias, proj_bias,
        norm2_gain, norm2_bias, out_bias, query_bias, value_bias, out_weight, fc_bias,
    )
    return assemble(*results)


def solution(mesh):
    sharded = P(("ctx", "fsdp"), None)
    rows, vector = P("fsdp", None), P("fsdp")
    in_specs = (
        sharded, P(), vector, vector, rows, vector, vector, rows, vector, vector, vector, rows, vector, rows,
        vector, sharded,
    )
    out_specs = (
        sharded, sharded, vector, vector, rows, vector, vector, rows, vector, vector, vector, rows, vector, rows,
        vector,
    )
    body = head_shards if dict(mesh.shape) == {"ctx": 8, "fsdp": 4} else shards
    return jax.shard_map(body, mesh=mesh, in_specs=in_specs, out_specs=out_specs, check_vma=False)
```

```python
import functools

import jax
import jax.numpy as jnp
from jax import lax
from jax.experimental import pallas as pl
from jax.experimental.pallas import tpu as pltpu
from jax.sharding import PartitionSpec as P

HEADS = 12
HEAD = 64


EPSILON = 1e-05
NEG_FILL = -1e30
GELU_C = 0.7978845608028654
GELU_K = 0.044715


def passed_along(block, axis, distance):
    devices = range(lax.axis_size(axis))
    route = [((i - distance) % len(devices), i) for i in devices]
    return lax.ppermute(block, axis, route)


def layer_norm(values_in, gain, shift):
    row_mean = jnp.mean(values_in, axis=-1, keepdims=True)
    centered = values_in - row_mean
    variance = jnp.mean(centered * centered, axis=-1, keepdims=True)
    inv_std = lax.rsqrt(variance + EPSILON)
    normed = centered * inv_std
    return (normed * gain.astype(jnp.float32) + shift.astype(jnp.float32), normed, inv_std)


def norm_backward(grad_norm, gain, normed, inv_std):
    scaled = grad_norm * gain.astype(jnp.float32)
    scaled_mean = jnp.mean(scaled, axis=-1, keepdims=True)
    cross_mean = jnp.mean(scaled * normed, axis=-1, keepdims=True)
    return inv_std * (scaled - scaled_mean - normed * cross_mean)


def gelu_forward(pre_act):
    cubed = pre_act * pre_act * pre_act
    return 0.5 * pre_act * (1.0 + jnp.tanh(GELU_C * (pre_act + GELU_K * cubed)))


def gelu_slope(pre_act):
    cubed = pre_act * pre_act * pre_act
    tanh_value = jnp.tanh(GELU_C * (pre_act + GELU_K * cubed))
    return 0.5 * (1.0 + tanh_value) + 0.5 * pre_act * (1.0 - tanh_value * tanh_value) * GELU_C * (
        1.0 + 3.0 * GELU_K * pre_act * pre_act
    )


def rows_product(left, right):
    return lax.dot_general(
        left, right, (((0,), (0,)), ((), ())), preferred_element_type=jnp.float32
    )


def transposed_product(left, right):
    return lax.dot_general(
        left, right, (((1,), (1,)), ((), ())), preferred_element_type=jnp.float32
    )


def split_heads(matrix):
    return matrix.reshape(matrix.shape[0], HEADS, HEAD)


def masked_scores(query, query_pos, keys, key_pos):
    scores = jnp.einsum(
        "rhd,khd->hrk", split_heads(query), split_heads(keys), preferred_element_type=jnp.float32
    ) * HEAD ** (-0.5)
    allowed = (key_pos[None, :] <= query_pos[:, None])[None]
    return (jnp.where(allowed, scores, NEG_FILL), allowed)


def attend_block(carried, query, query_pos, keys, values, key_pos):
    weighted, run_max, row_total = carried
    scores, allowed = masked_scores(query, query_pos, keys, key_pos)
    new_max = jnp.maximum(run_max, jnp.max(scores, axis=-1))
    weights = jnp.where(allowed, jnp.exp(scores - new_max[..., None]), 0.0)
    factor = jnp.exp(run_max - new_max)
    row_total = row_total * factor + jnp.sum(weights, axis=-1)
    update = jnp.einsum(
        "hrk,khd->rhd",
        weights,
        split_heads(values).astype(jnp.float32),
        precision=lax.Precision.HIGHEST,
        preferred_element_type=jnp.float32,
    )
    weighted = weighted * factor.T[:, :, None] + update
    return (weighted, new_max, row_total)


def attend_tile(carried, query, query_pos, keys, values, key_pos):
    half_rows = keys.shape[0] // 2
    latest = jnp.max(query_pos)
    for half_index in range(2):
        first_row = half_index * half_rows
        part_keys = keys[first_row : first_row + half_rows]
        part_values = values[first_row : first_row + half_rows]
        part_pos = key_pos[first_row : first_row + half_rows]

        def keep_state(state_in, block_keys, block_values, block_pos):
            return state_in

        def update_state(state_in, block_keys, block_values, block_pos):
            return attend_block(state_in, query, query_pos, block_keys, block_values, block_pos)

        carried = lax.cond(
            jnp.min(part_pos) > latest,
            keep_state,
            update_state,
            carried,
            part_keys,
            part_values,
            part_pos,
        )
    return carried


def block_grads(query, grad_attn, row_lse, row_delta, query_pos, keys, values, key_pos):
    scores, allowed = masked_scores(query, query_pos, keys, key_pos)
    probs = jnp.where(allowed, jnp.exp(scores - row_lse[..., None]), 0.0)
    grad_heads = split_heads(grad_attn)
    grad_values = jnp.einsum(
        "hrk,rhd->khd", probs.astype(jnp.bfloat16), grad_heads, preferred_element_type=jnp.float32
    )
    grad_probs = jnp.einsum(
        "rhd,khd->hrk", grad_heads, split_heads(values), preferred_element_type=jnp.float32
    )
    grad_scores = (probs * (grad_probs - row_delta[..., None])).astype(jnp.bfloat16)
    scale = HEAD ** (-0.5)
    grad_query = (
        jnp.einsum(
            "hrk,khd->rhd", grad_scores, split_heads(keys), preferred_element_type=jnp.float32
        )
        * scale
    )
    grad_keys = (
        jnp.einsum(
            "hrk,rhd->khd", grad_scores, split_heads(query), preferred_element_type=jnp.float32
        )
        * scale
    )
    key_rows = keys.shape[0]
    return (grad_query, grad_keys.reshape(key_rows, -1), grad_values.reshape(key_rows, -1))


def tile_grads(query, grad_attn, row_lse, row_delta, query_pos, keys, values, key_pos):
    half_rows = keys.shape[0] // 2
    key_width = keys.shape[1]
    latest = jnp.max(query_pos)
    query_total = jnp.zeros((query.shape[0], HEADS, HEAD), jnp.float32)
    key_parts = []
    value_parts = []
    for half_index in range(2):
        first_row = half_index * half_rows
        part_keys = keys[first_row : first_row + half_rows]
        part_values = values[first_row : first_row + half_rows]
        part_pos = key_pos[first_row : first_row + half_rows]

        def skipped(block_keys, block_values, block_pos):
            return (
                jnp.zeros((query.shape[0], HEADS, HEAD), jnp.float32),
                jnp.zeros((half_rows, key_width), jnp.float32),
                jnp.zeros((half_rows, key_width), jnp.float32),
            )

        def computed(block_keys, block_values, block_pos):
            return block_grads(
                query, grad_attn, row_lse, row_delta, query_pos, block_keys, block_values, block_pos
            )

        step_query, step_keys, step_values = lax.cond(
            jnp.min(part_pos) > latest, skipped, computed, part_keys, part_values, part_pos
        )
        query_total = query_total + step_query
        key_parts.append(step_keys)
        value_parts.append(step_values)
    return (query_total, jnp.concatenate(key_parts, axis=0), jnp.concatenate(value_parts, axis=0))


def shards(
    block_input,
    positions,
    norm1_gain,
    norm1_bias,
    qkv_weight,
    query_bias,
    value_bias,
    proj_weight,
    proj_bias,
    norm2_gain,
    norm2_bias,
    fc_weight,
    fc_bias,
    out_weight,
    out_bias,
    cotangent,
):
    rows = block_input.shape[0]
    width = block_input.shape[1]
    ctx_size = lax.axis_size("ctx")
    shard_count = lax.axis_size("fsdp")
    ctx_index = lax.axis_index("ctx")
    shard_index = lax.axis_index("fsdp")
    group_rows = rows * shard_count

    def key_positions(source):
        return lax.dynamic_slice_in_dim(positions, source * group_rows, group_rows)

    gain_one, shift_one, qkv_full, qbias_full, vbias_full, proj_full, pbias_full = (
        lax.all_gather(norm1_gain, "fsdp", axis=0, tiled=True),
        lax.all_gather(norm1_bias, "fsdp", axis=0, tiled=True),
        lax.all_gather(qkv_weight, "fsdp", axis=0, tiled=True),
        lax.all_gather(query_bias, "fsdp", axis=0, tiled=True),
        lax.all_gather(value_bias, "fsdp", axis=0, tiled=True),
        lax.all_gather(proj_weight, "fsdp", axis=0, tiled=True),
        lax.all_gather(proj_bias, "fsdp", axis=0, tiled=True),
    )
    gain_two, shift_two, fc_full, fbias_full, out_full, obias_full = (
        lax.all_gather(norm2_gain, "fsdp", axis=0, tiled=True),
        lax.all_gather(norm2_bias, "fsdp", axis=0, tiled=True),
        lax.all_gather(fc_weight, "fsdp", axis=0, tiled=True),
        lax.all_gather(fc_bias, "fsdp", axis=0, tiled=True),
        lax.all_gather(out_weight, "fsdp", axis=0, tiled=True),
        lax.all_gather(out_bias, "fsdp", axis=0, tiled=True),
    )
    residual = block_input.astype(jnp.float32)
    normed1_out, normed1, inv_std1 = layer_norm(residual, gain_one, shift_one)
    norm1 = normed1_out.astype(jnp.bfloat16)
    qkv = jnp.dot(norm1, qkv_full, preferred_element_type=jnp.float32)
    query = (qkv[:, :width] + qbias_full.astype(jnp.float32)).astype(jnp.bfloat16)
    keys = qkv[:, width : 2 * width].astype(jnp.bfloat16)
    values = (qkv[:, 2 * width :] + vbias_full.astype(jnp.float32)).astype(jnp.bfloat16)
    group_keys, group_values = (
        lax.all_gather(keys, "fsdp", axis=0, tiled=True),
        lax.all_gather(values, "fsdp", axis=0, tiled=True),
    )
    own_qpos = lax.dynamic_slice_in_dim(
        positions, (ctx_index * shard_count + shard_index) * rows, rows
    )
    own_kpos = key_positions(ctx_index)
    initial = (
        jnp.zeros((rows, HEADS, HEAD), jnp.float32),
        jnp.full((HEADS, rows), NEG_FILL, jnp.float32),
        jnp.zeros((HEADS, rows), jnp.float32),
    )
    carried = attend_tile(initial, query, own_qpos, group_keys, group_values, own_kpos)

    def forward_hop(hop_index, loop_carry):
        state_now, cycle_keys, cycle_values = loop_carry
        cycle_keys, cycle_values = passed_along((cycle_keys, cycle_values), "ctx", 1)
        source = (ctx_index - hop_index) % ctx_size
        state_now = attend_tile(
            state_now, query, own_qpos, cycle_keys, cycle_values, key_positions(source)
        )
        return (state_now, cycle_keys, cycle_values)

    result = lax.fori_loop(1, ctx_size, forward_hop, (carried, group_keys, group_values))
    carried = result[0]
    weighted, run_max, row_total = carried
    attn = (weighted / row_total.T[:, :, None]).reshape(rows, width).astype(jnp.bfloat16)
    row_lse = run_max + jnp.log(row_total)
    middle = (
        residual
        + jnp.dot(attn, proj_full, preferred_element_type=jnp.float32)
        + pbias_full.astype(jnp.float32)
    )
    normed2_out, normed2, inv_std2 = layer_norm(middle, gain_two, shift_two)
    norm2 = normed2_out.astype(jnp.bfloat16)
    pre_act = jnp.dot(norm2, fc_full, preferred_element_type=jnp.float32) + fbias_full.astype(
        jnp.float32
    )
    act = gelu_forward(pre_act).astype(jnp.bfloat16)
    block_output = (
        middle
        + jnp.dot(act, out_full, preferred_element_type=jnp.float32)
        + obias_full.astype(jnp.float32)
    )
    grad_out = cotangent.astype(jnp.float32)
    out_weight_grad = rows_product(act, cotangent)
    out_bias_grad = jnp.sum(grad_out, axis=0)
    grad_act = transposed_product(cotangent, out_full)
    grad_pre = grad_act * gelu_slope(pre_act)
    fc_bias_grad = jnp.sum(grad_pre, axis=0)
    grad_pre_half = grad_pre.astype(jnp.bfloat16)
    fc_weight_grad = rows_product(norm2, grad_pre_half)
    grad_norm2 = transposed_product(grad_pre_half, fc_full)
    norm2_gain_grad = jnp.sum(grad_norm2 * normed2, axis=0)
    norm2_bias_grad = jnp.sum(grad_norm2, axis=0)
    grad_middle = grad_out + norm_backward(grad_norm2, gain_two, normed2, inv_std2)
    mlp_shares = (
        lax.psum_scatter(norm2_gain_grad, "fsdp", scatter_dimension=0, tiled=True),
        lax.psum_scatter(norm2_bias_grad, "fsdp", scatter_dimension=0, tiled=True),
        lax.psum_scatter(fc_weight_grad, "fsdp", scatter_dimension=0, tiled=True),
        lax.psum_scatter(fc_bias_grad, "fsdp", scatter_dimension=0, tiled=True),
        lax.psum_scatter(out_weight_grad, "fsdp", scatter_dimension=0, tiled=True),
        lax.psum_scatter(out_bias_grad, "fsdp", scatter_dimension=0, tiled=True),
    )
    proj_bias_grad = jnp.sum(grad_middle, axis=0)
    grad_middle_half = grad_middle.astype(jnp.bfloat16)
    proj_weight_grad = rows_product(attn, grad_middle_half)
    grad_attn = transposed_product(grad_middle_half, proj_full).astype(jnp.bfloat16)
    row_delta = jnp.sum(
        split_heads(grad_attn).astype(jnp.float32) * split_heads(attn).astype(jnp.float32), axis=-1
    ).T
    grad_query, grad_keys, grad_values = tile_grads(
        query, grad_attn, row_lse, row_delta, own_qpos, group_keys, group_values, own_kpos
    )

    def pass_key_grads(key_grads):
        return passed_along((key_grads[0], key_grads[1]), "ctx", 1)

    def backward_hop(hop_index, loop_carry):
        query_sum, key_grads, cycle_keys, cycle_values = loop_carry
        cycle_keys, cycle_values = passed_along((cycle_keys, cycle_values), "ctx", 1)
        key_grads = pass_key_grads(key_grads)
        source = (ctx_index - hop_index) % ctx_size
        step_query, step_keys, step_values = tile_grads(
            query,
            grad_attn,
            row_lse,
            row_delta,
            own_qpos,
            cycle_keys,
            cycle_values,
            key_positions(source),
        )
        return (
            query_sum + step_query,
            (key_grads[0] + step_keys, key_grads[1] + step_values),
            cycle_keys,
            cycle_values,
        )

    result = lax.fori_loop(
        1, ctx_size, backward_hop, (grad_query, (grad_keys, grad_values), group_keys, group_values)
    )
    grad_query = result[0]
    key_grads = pass_key_grads(result[1])
    own_key_grad, own_value_grad = (
        lax.psum_scatter(key_grads[0], "fsdp", scatter_dimension=0, tiled=True),
        lax.psum_scatter(key_grads[1], "fsdp", scatter_dimension=0, tiled=True),
    )
    grad_query_rows = grad_query.reshape(rows, width)
    query_bias_grad = jnp.sum(grad_query_rows, axis=0)
    value_bias_grad = jnp.sum(own_value_grad, axis=0)
    grad_qkv = jnp.concatenate([grad_query_rows, own_key_grad, own_value_grad], axis=1).astype(
        jnp.bfloat16
    )
    qkv_weight_grad = rows_product(norm1, grad_qkv)
    grad_norm1 = transposed_product(grad_qkv, qkv_full)
    norm1_gain_grad = jnp.sum(grad_norm1 * normed1, axis=0)
    norm1_bias_grad = jnp.sum(grad_norm1, axis=0)
    input_grad = grad_middle + norm_backward(grad_norm1, gain_one, normed1, inv_std1)
    attn_shares = (
        lax.psum_scatter(norm1_gain_grad, "fsdp", scatter_dimension=0, tiled=True),
        lax.psum_scatter(norm1_bias_grad, "fsdp", scatter_dimension=0, tiled=True),
        lax.psum_scatter(qkv_weight_grad, "fsdp", scatter_dimension=0, tiled=True),
        lax.psum_scatter(query_bias_grad, "fsdp", scatter_dimension=0, tiled=True),
        lax.psum_scatter(value_bias_grad, "fsdp", scatter_dimension=0, tiled=True),
        lax.psum_scatter(proj_weight_grad, "fsdp", scatter_dimension=0, tiled=True),
        lax.psum_scatter(proj_bias_grad, "fsdp", scatter_dimension=0, tiled=True),
    )
    totals = lax.psum(
        (
            attn_shares[0],
            attn_shares[1],
            attn_shares[2],
            attn_shares[3],
            attn_shares[4],
            attn_shares[5],
            attn_shares[6],
            mlp_shares[0],
            mlp_shares[1],
            mlp_shares[2],
            mlp_shares[3],
            mlp_shares[4],
            mlp_shares[5],
        ),
        "ctx",
    )
    return (
        block_output,
        input_grad,
        totals[0],
        totals[1],
        totals[2],
        totals[3],
        totals[4],
        totals[5],
        totals[6],
        totals[7],
        totals[8],
        totals[9],
        totals[10],
        totals[11],
        totals[12],
    )


MESH = pl.DeviceIdType.MESH
SMEM = pltpu.SMEM
VMEM = pltpu.VMEM
F32 = jnp.float32
B16 = jnp.bfloat16


class Transfer:
    def __init__(self, links, src, dst, device):
        self.args = dict(
            src_ref=src,
            dst_ref=dst,
            send_sem=links.send_sem.at[links.count],
            recv_sem=links.recv_sem.at[links.count],
            device_id=device,
            device_id_type=MESH,
        )
        links.count += 1
        links.sent.append(self)

    def start(self):
        pltpu.make_async_remote_copy(**self.args).start()
        return self

    def arrived(self):
        pltpu.make_async_remote_copy(**self.args).wait_recv()

    def left(self):
        pltpu.make_async_remote_copy(**self.args).wait_send()


class Links:
    def __init__(self, send_sem, recv_sem):
        self.send_sem, self.recv_sem = send_sem, recv_sem
        self.count = 0
        self.sent = []
        ctx = lax.axis_index("ctx")
        self.ctx = ctx
        self.z = lax.axis_index("fsdp")
        self.core = lax.rem(ctx, 2)
        self.chip = lax.div(ctx, 2)
        x, y = lax.rem(self.chip, 2), lax.div(self.chip, 2)
        self.chip_x = self.chip + 1 - 2 * x
        self.chip_y = self.chip + 2 - 4 * y
        self.chip_d = 3 - self.chip
        self.other = 1 - self.core
        self.to_core = {"ctx": self.chip * 2 + self.other}
        self.to_x = {"ctx": self.chip_x * 2 + self.core}
        self.to_y = {"ctx": self.chip_y * 2 + self.core}
        self.to_d = {"ctx": self.chip_d * 2 + self.core}

    def zed(self, step):
        return lax.rem(self.z + step, 4)

    def to_z(self, step):
        return {"fsdp": self.zed(step)}

    def peers(self):
        near = [self.to_core, self.to_x, self.to_y, self.to_d]
        return near + [self.to_z(step) for step in (1, 2, 3)]

    def copy(self, src, dst, device):
        return Transfer(self, src, dst, device)

    def greet(self):
        barrier = pltpu.get_barrier_semaphore()
        for device in self.peers():
            pl.semaphore_signal(barrier, inc=1, device_id=device, device_id_type=MESH)

    def greeted(self):
        pl.semaphore_wait(pltpu.get_barrier_semaphore(), len(self.peers()))

    def drain(self):
        for transfer in self.sent:
            transfer.left()


class RingGather:
    def __init__(self, links, buf):
        half = buf.shape[1] // 2
        own, left, right = links.z, links.zed(3), links.zed(1)

        def piece(member, part):
            return buf.at[member, part * half : (part + 1) * half]

        def move(member, part, step):
            return links.copy(piece(member, part), piece(member, part), links.to_z(step))

        self.first = [move(own, 0, 1), move(own, 1, 3), move(own, 1, 1), move(own, 0, 3)]
        self.second = [move(left, 0, 1), move(right, 1, 3)]

    def start(self):
        for transfer in self.first:
            transfer.start()

    def forward(self):
        for transfer, onward in zip(self.first[:2], self.second):
            transfer.arrived()
            onward.start()

    def near(self):
        for transfer in self.first[2:]:
            transfer.arrived()

    def far(self):
        for transfer in self.second:
            transfer.arrived()


class Shared:
    def __init__(self, links, source, target):
        small, half = target.shape[1] // 4, target.shape[2] // 2
        cols = pl.ds(pl.multiple_of(links.core * half, 128), half)

        def rows(chip):
            return pl.ds(pl.multiple_of(chip * small, 16), small)

        def move(chip, part, device):
            ref = target.at[2 * part : 2 * part + 2, rows(chip), cols]
            return links.copy(ref, ref, device)

        own = rows(links.chip)
        place = target.at[links.z, own, cols]
        place[...] = source(links.z, own)[...]
        self.cross = [
            links.copy(source(links.zed(step), own), place, links.to_z(step)) for step in (2, 1, 3)
        ]
        own, x, y = links.chip, links.chip_x, links.chip_y
        self.near = [
            move(own, 0, links.to_x),
            move(own, 1, links.to_y),
            move(own, 1, links.to_x),
            move(own, 0, links.to_y),
        ]
        self.onward = [move(x, 0, links.to_y), move(y, 1, links.to_x)]
        ref = target.at[:, :, cols]
        self.hand = links.copy(ref, ref, links.to_core)

    def start(self):
        for transfer in self.cross:
            transfer.start()

    def gather(self):
        for transfer in self.cross:
            transfer.arrived()
        for transfer in self.near:
            transfer.start()

    def forward(self):
        for transfer, onward in zip(self.near[:2], self.onward):
            transfer.arrived()
            onward.start()

    def give(self):
        for transfer in self.near[2:] + self.onward:
            transfer.arrived()
        self.hand.start()

    def finish(self):
        self.hand.arrived()


class ContextGather:
    def __init__(self, links, buf):
        half = buf.shape[2] // 2

        def move(chip, part, device):
            rows = slice(None) if part is None else slice(part * half, (part + 1) * half)
            ref = buf.at[links.core, chip, rows]
            return links.copy(ref, ref, device)

        own, x, y, d = links.chip, links.chip_x, links.chip_y, links.chip_d
        self.own_core = move(own, None, links.to_core)
        self.x_parts = [move(own, 0, links.to_x), move(own, 1, links.to_x)]
        self.y_parts = [move(own, 1, links.to_y), move(own, 0, links.to_y)]
        self.onward = [move(x, 0, links.to_y), move(y, 1, links.to_x)]
        self.x_core = move(x, None, links.to_core)
        self.y_core = move(y, None, links.to_core)
        self.d_core = move(d, None, links.to_core)

    def start(self):
        for transfer in (
            self.x_parts[0],
            self.y_parts[0],
            self.own_core,
            self.x_parts[1],
            self.y_parts[1],
        ):
            transfer.start()

    def forward(self):
        self.x_parts[0].arrived()
        self.onward[0].start()
        self.y_parts[0].arrived()
        self.onward[1].start()

    def hand_near(self):
        self.x_parts[1].arrived()
        self.x_core.start()
        self.y_parts[1].arrived()
        self.y_core.start()

    def hand_far(self):
        self.onward[0].arrived()
        self.onward[1].arrived()
        self.d_core.start()


class DirectGather:
    def __init__(self, links, buf):
        def move(chip, device):
            ref = buf.at[links.core, chip]
            return links.copy(ref, ref, device)

        self.first = [move(links.chip, device) for device in (links.to_d, links.to_x, links.to_y)]
        self.own_core = move(links.chip, links.to_core)
        self.hands = [
            move(chip, links.to_core) for chip in (links.chip_d, links.chip_x, links.chip_y)
        ]

    def start(self):
        for transfer in self.first + [self.own_core]:
            transfer.start()

    def finish(self):
        for k in (1, 2, 0):
            self.first[k].arrived()
            self.hands[k].start()
        for transfer in [self.own_core] + self.hands:
            transfer.arrived()


def chosen(flag, shape):
    return jnp.full(shape, flag, jnp.int32) == 1


def masked_heads(value, first, width):
    rows, span = value.shape
    pieces = []
    if first > 0:
        pieces.append(jnp.zeros((rows, first), value.dtype))
    pieces.append(value)
    if first + span < width:
        pieces.append(jnp.zeros((rows, width - first - span), value.dtype))
    wide = jnp.concatenate(pieces, axis=1) if len(pieces) > 1 else value
    head = (lax.broadcasted_iota(jnp.int32, (rows, width), 1) - first + HEAD) // HEAD - 1
    return [
        jnp.where(head == index, wide.astype(F32), 0.0).astype(value.dtype)
        for index in range(span // HEAD)
    ]


def soft_step(scores, old_max, old_sum):
    new_max = jnp.maximum(old_max, jnp.max(scores, axis=0, keepdims=True))
    weights = jnp.exp(scores - new_max)
    factor = jnp.exp(old_max - new_max)
    new_sum = old_sum * factor + jnp.sum(weights, axis=0, keepdims=True)
    return weights.astype(B16), factor, new_max, new_sum


def forward_phase(
    links, ids, x, cot, qkvw, fcw, projw, v0, v1, v2, v3, v4, v5, qbias, vbias,
    attn_t, lse, qm, kv, x_all, w_all, cot_all, fc_all, proj_all, vec_all, norm1, normed1,
    stage, max_h, sum_h, acc_h, max_x, sum_x, acc_x,
):
    rows = x.shape[0]
    span = qkvw.shape[0]
    block = 2 * rows
    heads = span // HEAD
    z = links.z
    links.greet()
    x_all[z] = x[...]
    cot_all[z] = cot[...]
    own_vectors = jnp.concatenate(
        [v[...].astype(F32).reshape(1, span) for v in (v0, v1, v2, v3, v4, v5)]
        + [jnp.zeros((10, span), F32)],
        axis=0,
    )
    vec_all[z, :, :span] = own_vectors.astype(B16)
    for member in range(4):
        stage[member, :, : 3 * span] = jnp.concatenate(
            [qkvw[:, t * 4 * span + member * span : t * 4 * span + (member + 1) * span] for t in range(3)],
            axis=1,
        )

    vectors = [
        links.copy(vec_all.at[z], vec_all.at[z], links.to_z(step)) for step in (1, 3, 2)
    ]
    inputs = RingGather(links, x_all)
    half = cot.shape[1] // 2

    def own_cols(first):
        return pl.ds(pl.multiple_of(first + links.core * half, 128), half)

    weights = Shared(links, lambda member, at: stage.at[member, at, own_cols(0)], w_all)
    cots = RingGather(links, cot_all)
    fcs_in = Shared(links, lambda member, at: fcw.at[at, own_cols(member * 2 * half)], fc_all)
    projs = Shared(links, lambda member, at: projw.at[at, own_cols(0)], proj_all)
    context = ContextGather(links, kv)

    links.greeted()
    for transfer in vectors:
        transfer.start()
    weights.start()
    inputs.start()
    for transfer in vectors:
        transfer.arrived()

    gain = jnp.concatenate([vec_all[m, 0:1, :span] for m in range(4)], axis=1).astype(F32)
    shift = jnp.concatenate([vec_all[m, 1:2, :span] for m in range(4)], axis=1).astype(F32)

    def normalise(member):
        shifted, normed, _ = layer_norm(x_all[member].astype(F32), gain, shift)
        at = pl.ds(pl.multiple_of(member * rows, rows), rows)
        norm1[at, :] = shifted.astype(B16)
        normed1[at, :] = normed

    normalise(z)
    inputs.forward()
    weights.gather()
    fcs_in.start()
    projs.start()
    inputs.near()
    normalise(links.zed(1))
    normalise(links.zed(3))
    weights.forward()
    inputs.far()
    cots.start()
    normalise(links.zed(2))
    weights.give()
    fcs_in.gather()
    weights.finish()

    matrix = w_all[...].reshape(4 * span, w_all.shape[2])[:, : 3 * span]
    for part in range(2):
        at = slice(part * block, (part + 1) * block)
        product = jnp.dot(norm1[at, :], matrix, preferred_element_type=F32)
        query = (product[:, :span] + qbias[...].astype(F32).reshape(1, span)).astype(B16)
        query = query * jnp.asarray(HEAD**-0.5, B16)
        for head, lone in enumerate(masked_heads(query, 0, 4 * HEAD)):
            qm[head, at, :] = lone
        values = product[:, 2 * span :] + vbias[...].astype(F32).reshape(1, span)
        kv[links.core, links.chip, at, :] = jnp.concatenate(
            [product[:, span : 2 * span], values], axis=1
        ).astype(B16)
    context.start()

    own_block = ids[2 * links.ctx]
    keep = lax.broadcasted_iota(jnp.int32, (block, block), 0) <= lax.broadcasted_iota(
        jnp.int32, (block, block), 1
    )
    none = jnp.full((1, block), NEG_FILL, F32)
    zero = jnp.zeros((1, block), F32)

    def halves(core, chip, part):
        at = slice(part * block, (part + 1) * block)
        return kv[core, chip, at, : 4 * HEAD], kv[core, chip, at, 2 * HEAD :].T

    def value_rows(head):
        return slice((1 + head) * HEAD, (2 + head) * HEAD)

    def head_rows(head):
        return slice(head * HEAD, (head + 1) * HEAD)

    k_low, vt_low = halves(links.core, links.chip, 0)
    k_high, vt_high = halves(links.core, links.chip, 1)
    for head in range(heads):
        q_low, q_high = qm[head, :block, :], qm[head, block:, :]
        scores = jnp.where(keep, transposed_product(k_low, q_low), NEG_FILL)
        w, _, top, total = soft_step(scores, none, zero)
        max_x[0, head : head + 1, :] = top
        sum_x[0, head : head + 1, :] = total
        acc_x[0, head_rows(head), :] = jnp.dot(
            vt_low[value_rows(head)], w, preferred_element_type=F32
        )
        scores = transposed_product(k_low, q_high)
        w, _, top, total = soft_step(scores, none, zero)
        acc = jnp.dot(vt_low[value_rows(head)], w, preferred_element_type=F32)
        scores = jnp.where(keep, transposed_product(k_high, q_high), NEG_FILL)
        w, factor, top, total = soft_step(scores, top, total)
        max_h[head : head + 1, :] = top
        sum_h[head : head + 1, :] = total
        acc_h[head_rows(head), :] = acc * factor + jnp.dot(
            vt_high[value_rows(head)], w, preferred_element_type=F32
        )
    max_x[1] = jnp.full_like(max_h, NEG_FILL)
    sum_x[1] = jnp.zeros_like(sum_h)
    acc_x[1] = jnp.zeros_like(acc_h)

    def hop(index, carry):
        near = index < 3
        far = index >= 5
        core = jnp.where((index == 1) | (index == 2) | (index == 5), links.core, links.other)
        chip = jnp.where(
            index == 0,
            links.chip,
            jnp.where(far, links.chip_d, jnp.where(lax.rem(index, 2) == 1, links.chip_x, links.chip_y)),
        )

        @pl.when(index == 0)
        def _():
            context.own_core.arrived()
            fcs_in.forward()
            context.forward()

        @pl.when(index == 1)
        def _():
            context.hand_near()
            cots.forward()

        @pl.when(index == 2)
        def _():
            projs.gather()

        @pl.when(index == 3)
        def _():
            context.x_core.arrived()
            context.hand_far()

        @pl.when(index == 4)
        def _():
            context.y_core.arrived()
            cots.near()
            fcs_in.give()

        @pl.when(index == 5)
        def _():
            projs.forward()

        @pl.when(index == 6)
        def _():
            context.d_core.arrived()

        block_id = ids[2 * (2 * chip + core)]
        low = (block_id < own_block).astype(jnp.int32)
        in_low = chosen(low, (1, block))
        kv_low = kv[core, chip, :block, :]
        kv_high = kv[core, chip, block:, :]
        kv_pick = jnp.where(chosen(low, kv_low.shape), kv_low, kv_high)
        q_mask = chosen(low, (block, 4 * HEAD))
        work = []
        for head in range(heads):
            scores = transposed_product(kv_low[:, : 4 * HEAD], qm[head, block:, :])
            work.append((scores, max_h[head : head + 1, :], sum_h[head : head + 1, :]))
        for head in range(heads):
            q_pick = jnp.where(q_mask, qm[head, :block, :], qm[head, block:, :])
            scores = transposed_product(kv_pick[:, : 4 * HEAD], q_pick)
            at = slice(head, head + 1)
            work.append(
                (
                    scores,
                    jnp.where(in_low, max_x[0, at, :], max_x[1, at, :]),
                    jnp.where(in_low, sum_x[0, at, :], sum_x[1, at, :]),
                )
            )
        done = [soft_step(*entry) for entry in work]
        vt = kv_low[:, 2 * HEAD :].T
        for head in range(heads):
            w, factor, top, total = done[head]
            max_h[head : head + 1, :] = top
            sum_h[head : head + 1, :] = total
            acc_h[head_rows(head), :] = acc_h[head_rows(head), :] * factor + jnp.dot(
                vt[value_rows(head)], w, preferred_element_type=F32
            )
        vt = kv_pick[:, 2 * HEAD :].T
        for head in range(heads):
            w, factor, top, total = done[heads + head]
            acc = jnp.where(in_low, acc_x[0, head_rows(head), :], acc_x[1, head_rows(head), :])
            acc = acc * factor + jnp.dot(
                vt[value_rows(head)], w, preferred_element_type=F32
            )
            for part in range(2):
                own = in_low if part == 0 else ~in_low
                max_x[part, head : head + 1, :] = jnp.where(own, top, max_x[part, head : head + 1, :])
                sum_x[part, head : head + 1, :] = jnp.where(
                    own, total, sum_x[part, head : head + 1, :]
                )
                acc_x[part, head_rows(head), :] = jnp.where(own, acc, acc_x[part, head_rows(head), :])
        return carry

    lax.fori_loop(0, 7, hop, 0)
    for head in range(heads):
        at = slice(head, head + 1)
        total = sum_x[0, at, :]
        attn_t[head_rows(head), :block] = (acc_x[0, head_rows(head), :] / total).astype(B16)
        lse[at, :block] = max_x[0, at, :] + jnp.log(total)
        top = jnp.maximum(max_h[at, :], max_x[1, at, :])
        left, right = jnp.exp(max_h[at, :] - top), jnp.exp(max_x[1, at, :] - top)
        total = sum_h[at, :] * left + sum_x[1, at, :] * right
        acc = acc_h[head_rows(head), :] * left + acc_x[1, head_rows(head), :] * right
        attn_t[head_rows(head), block:] = (acc / total).astype(B16)
        lse[at, block:] = top + jnp.log(total)
    return cots, fcs_in, projs


def parts_of(rows):
    first = (rows // 2 + 15) // 16 * 16
    return [slice(0, first), slice(first, rows)]


class FourSum:
    def __init__(self, links, parts, early, late, far, own, near):
        self.parts, self.early, self.late, self.own, self.near = parts, early, late, own, near
        self.cuts = parts_of(early.shape[0])
        self.far = [
            links.copy(parts.at[far, self.cuts[k]], early.at[self.cuts[k]], near[k][0]) for k in range(2)
        ]
        self.ready, self.summed = [], []
        for k, (device, part, added) in enumerate(near):
            for half, group in ((1 - added, self.ready), (added, self.summed)):
                cut = self.cuts[half]
                group.append(links.copy(parts.at[part, cut], late.at[k, cut], device))

    def send_far(self):
        for transfer in self.far:
            transfer.start()

    def send_ready(self):
        for transfer in self.ready:
            transfer.start()

    def send_summed(self):
        for k, (_, part, added) in enumerate(self.near):
            cut = self.cuts[added]
            self.far[added].arrived()
            both = self.parts[part, cut].astype(F32) + self.early[cut].astype(F32)
            self.parts[part, cut] = both.astype(B16)
            self.summed[k].start()

    def total(self):
        for transfer in self.ready + self.summed:
            transfer.arrived()
        return (
            self.parts[self.own].astype(F32)
            + self.late[0].astype(F32)
            + self.late[1].astype(F32)
        )


class ThreeSum:
    def __init__(self, links, parts, late, own, targets):
        self.parts, self.late, self.own = parts, late, own
        self.sends = [
            links.copy(parts.at[part], late.at[k], device) for k, (device, part) in enumerate(targets)
        ]

    def total(self):
        value = self.parts[self.own].astype(F32)
        for k in (1, 2, 0):
            self.sends[k].arrived()
            value = value + self.late[k].astype(F32)
        return value


def ring_sum(links, parts, early, late):
    right, left = links.zed(1), links.zed(3)
    near = [(links.to_z(1), right, 0), (links.to_z(3), left, 1)]
    return FourSum(links, parts, early, late, links.zed(2), links.z, near)


class ContextSum:
    def __init__(self, links, grads, handed, early, late):
        self.links, self.grads, self.handed = links, grads, handed
        order = (links.chip_d, links.chip_x, links.chip_y, links.chip)
        self.order = order
        self.hands = [
            links.copy(grads.at[links.other, chip], handed.at[k], links.to_core)
            for k, chip in enumerate(order)
        ]
        if early is None:
            targets = [(links.to_d, order[0]), (links.to_x, order[1]), (links.to_y, order[2])]
            self.four = ThreeSum(links, grads.at[links.core], late, links.chip, targets)
            return
        near = [(links.to_x, links.chip_x, 1), (links.to_y, links.chip_y, 0)]
        self.four = FourSum(
            links, grads.at[links.core], early, late, links.chip_d, links.chip, near
        )

    def hand(self, k):
        self.hands[k].start()

    def merge(self, k):
        self.hands[k].arrived()
        core, chip = self.links.core, self.order[k]
        both = self.grads[core, chip].astype(F32) + self.handed[k].astype(F32)
        self.grads[core, chip] = both.astype(B16)


def backward_phase(
    links, arriving, ids, attn_t, lse, qm, kv, x_all, w_all, cot_all, fc_all, proj_all, vec_all, norm1, projw, outw, fcb,
    block_out, input_grad, h_mlp, h_attn, sums, normed1,
    a_all, grad_act, norm2, act, grad_pre, gn2, gn2_e, gn2_l, mlp, mlp_e, mlp_l, gn1, gn1_e, gn1_l,
    gm_all, gm_own, mid_own, dkv, dkv_h, dkv_e, dkv_l, g_mlp, gmlp_h, gmlp_e, gmlp_l,
    g_attn, gattn_h, gattn_l, fc_piece, qkv_piece, dom, delta, dq, gqkv, zsum, bsum, ssum, rowsum, ga_out, ga_in,
):
    members, rows, width = x_all.shape
    span = attn_t.shape[0]
    group = members * rows
    block = group // 2
    heads = span // HEAD
    half = width // 2
    small = span // 4
    z = links.z
    right, left, opposite = links.zed(1), links.zed(3), links.zed(2)

    def row(index):
        return jnp.concatenate(
            [vec_all[m, index : index + 1, :span] for m in range(members)], axis=1
        ).astype(F32)

    def head_rows(head):
        return slice(head * HEAD, (head + 1) * HEAD)

    def member_rows(member):
        return pl.ds(pl.multiple_of(member * rows, rows), rows)

    def pair(index):
        first = index == 0
        return jnp.where(first, opposite, left), jnp.where(first, right, z)

    def both_rows(ref, ats):
        return jnp.concatenate([ref[at, :] for at in ats], axis=0)

    attns = RingGather(links, a_all)
    gms = RingGather(links, gm_all)
    swaps = [
        links.copy(ga_out.at[links.zed(step)], ga_in.at[z], links.to_z(step)) for step in (2, 1, 3)
    ]
    ring_gn2 = ring_sum(links, gn2, gn2_e, gn2_l)
    ring_mlp = ring_sum(links, mlp, mlp_e, mlp_l)
    ring_gn1 = ring_sum(links, gn1, gn1_e, gn1_l)
    sum_mlp = ContextSum(links, g_mlp, gmlp_h, gmlp_e, gmlp_l)
    sum_attn = ContextSum(links, g_attn, gattn_h, None, gattn_l)
    sum_kv = ContextSum(links, dkv, dkv_h, dkv_e, dkv_l)
    gather_mlp = ContextGather(links, h_mlp)
    gather_attn = DirectGather(links, h_attn)

    def spread(piece, gathered, first):
        at = pl.ds(pl.multiple_of(first + small * z, 16), small)
        place = gathered.at[links.core, links.chip, at]
        return [links.copy(piece.at[links.zed(s)], place, links.to_z(s)) for s in (1, 3, 2)]

    spread_fc = spread(fc_piece, h_mlp, span)
    spread_qkv = spread(qkv_piece, h_attn, 0)

    cots, fcs_in, projs = arriving
    gain_one = row(0)
    gain_two, shift_two = row(3), row(4)
    proj_bias, out_bias = row(2), row(5)
    fc_bias = fcb[...].astype(F32).reshape(1, fcb.shape[0])
    attns.start()
    projs.give()
    cots.far()
    one, zero_shift = jnp.ones((1, width), F32), jnp.zeros((1, width), F32)

    def before(index, carry):
        cots_of = cot_all[pl.ds(2 * index, 2)].reshape(block, width)
        at = pl.ds(pl.multiple_of(index * block, block), block)
        grad_act[at, :] = transposed_product(cots_of, outw[...])
        return carry

    lax.fori_loop(0, 1, before, 0)
    attns.forward()
    lax.fori_loop(1, 2, before, 0)
    attns.near()
    attns.far()
    fcs_in.finish()
    projs.finish()
    rowsum[...] = jnp.zeros_like(rowsum)
    fc_matrix = fc_all.shape

    def mlp_block(index, carry):
        members_of = pair(index)
        ats = [member_rows(member) for member in members_of]
        attn_cols = jnp.concatenate([a_all[:, :, at].reshape(width, rows) for at in ats], axis=1)
        inputs_of = jnp.concatenate([x_all[member] for member in members_of], axis=0)
        middle = (
            inputs_of.astype(F32)
            + rows_product(attn_cols, proj_all[...].reshape(width, width))
            + proj_bias
        )
        shifted, normed, _ = layer_norm(middle, gain_two, shift_two)
        half_norm = shifted.astype(B16)
        fc = fc_all[...].reshape(width, fc_matrix[2])
        pre_act = jnp.dot(half_norm, fc, preferred_element_type=F32) + fc_bias
        squared = pre_act * pre_act
        tanh_value = jnp.tanh(GELU_C * pre_act * (1.0 + GELU_K * squared))
        act_half = (0.5 * pre_act * (1.0 + tanh_value)).astype(B16)
        slope = 0.5 * (1.0 + tanh_value) + (0.5 * GELU_C) * pre_act * (
            1.0 - tanh_value * tanh_value
        ) * (1.0 + 3.0 * GELU_K * squared)
        grad = both_rows(grad_act, ats) * slope
        rowsum[7:8, :] += jnp.sum(grad, axis=0, keepdims=True)
        grad_half = grad.astype(B16)
        back = transposed_product(grad_half, fc)
        rowsum[3:4, :] += jnp.sum(back * normed, axis=0, keepdims=True)
        rowsum[4:5, :] += jnp.sum(back, axis=0, keepdims=True)
        back_half = back.astype(B16)
        for k in range(2):
            part = slice(k * rows, (k + 1) * rows)
            gn2[members_of[k]] = back_half[part]
            norm2[ats[k], :] = half_norm[part]
            act[ats[k], :] = act_half[part]
            grad_pre[ats[k], :] = grad_half[part]

        @pl.when(index == 0)
        def _():
            ring_gn2.send_far()
            ring_gn2.ready[0].start()

        @pl.when(index == 1)
        def _():
            ring_gn2.ready[1].start()
            ring_gn2.send_summed()
            mid_own[...] = middle[rows:]

        return carry

    lax.fori_loop(0, 2, mlp_block, 0)

    def mlp_weights(core):
        cols = pl.ds(pl.multiple_of(core * half, half), half)
        cots = cot_all[:, :, cols].reshape(group, half)
        product = rows_product(act[...], cots).astype(B16)
        g_mlp[core, :, :span, :] = product.reshape(4, span, half)
        product = rows_product(norm2[...], grad_pre[:, cols]).astype(B16)
        product = product.reshape(members, 4, small, half)
        for member in range(members):
            at = span + member * small
            g_mlp[core, :, at : at + small, :] = product[member]

    mlp_weights(links.other)
    for k in range(4):
        sum_mlp.hand(k)
    mlp_weights(links.core)
    sum_mlp.merge(0)
    sum_mlp.four.send_far()
    sum_mlp.merge(1)
    sum_mlp.merge(2)
    sum_mlp.four.send_ready()

    grad_norm2 = ring_gn2.total()
    _, normed, inv_std = layer_norm(mid_own[...], gain_two, shift_two)
    cot_own = cot_all[z].astype(F32)
    grad_middle = cot_own + norm_backward(grad_norm2, gain_two, normed, inv_std)
    gm_own[...] = grad_middle
    grad_half = grad_middle.astype(B16)
    gm_all[z] = grad_half
    for transfer, step in zip(swaps, (2, 1, 3)):
        member = links.zed(step)
        ga_out[member, :, :span] = transposed_product(grad_half, proj_all[member]).astype(B16)
        transfer.start()
    ga_in[z, :, :span] = transposed_product(grad_half, proj_all[z]).astype(B16)
    gms.start()
    rowsum[2:3, :] = jnp.sum(grad_middle, axis=0, keepdims=True)
    rowsum[5:6, :] = jnp.sum(cot_own, axis=0, keepdims=True)

    sum_mlp.four.send_summed()
    sum_mlp.merge(3)

    def mlp_product(index, carry):
        at = pl.ds(pl.multiple_of(index * block, block), block)
        product = jnp.dot(act[at, :], outw[...], preferred_element_type=F32).astype(B16)
        mlp[pl.ds(2 * index, 2)] = product.reshape(2, rows, width)
        return carry

    lax.fori_loop(0, 2, mlp_product, 0)
    for transfer in swaps:
        transfer.arrived()
    gms.forward()
    ring_mlp.send_far()
    ring_mlp.send_ready()

    grad_attn = ga_in[...].reshape(group, ga_in.shape[2])[:, :span]
    grad_attn_t = grad_attn.astype(F32).T
    delta_rows = grad_attn_t * attn_t[...].astype(F32)
    for head in range(heads):
        delta[head : head + 1, :] = jnp.sum(delta_rows[head_rows(head), :], axis=0, keepdims=True)
    for head, lone in enumerate(masked_heads(grad_attn, HEAD, 4 * HEAD)):
        dom[head] = lone
    dq[...] = jnp.zeros_like(dq)

    own_block = ids[2 * links.ctx]
    keep = lax.broadcasted_iota(jnp.int32, (block, block), 0) <= lax.broadcasted_iota(
        jnp.int32, (block, block), 1
    )
    low_rows, high_rows = slice(0, block), slice(block, group)

    def tile(keys, queries, grads, lse_of, delta_of, masked=False):
        probs, scores_grad = [], []
        for head in range(heads):
            scores = transposed_product(keys[:, : 4 * HEAD], queries[head])
            if masked:
                scores = jnp.where(keep, scores, NEG_FILL)
            weights = jnp.exp(scores - lse_of(head))
            grad_probs = transposed_product(keys[:, 2 * HEAD :], grads[head])
            probs.append(weights.astype(B16))
            scores_grad.append((weights * (grad_probs - delta_of(head))).astype(B16))
        keys_t = keys[:, : 4 * HEAD].T
        query_grad = [
            jnp.dot(keys_t[head_rows(head)], scores_grad[head], preferred_element_type=F32)
            for head in range(heads)
        ]
        value_grad = jnp.dot(
            jnp.concatenate(probs, axis=1),
            jnp.concatenate(grads, axis=0),
            preferred_element_type=F32,
        )
        key_grad = jnp.dot(
            jnp.concatenate(scores_grad, axis=1),
            jnp.concatenate(queries, axis=0),
            preferred_element_type=F32,
        )
        both = jnp.concatenate(
            [
                key_grad[:, : 2 * HEAD],
                key_grad[:, 2 * HEAD :] + value_grad[:, : 2 * HEAD],
                value_grad[:, 2 * HEAD :],
            ],
            axis=1,
        )
        return query_grad, both

    def stacked(ref, at):
        return [ref[head, at, :] for head in range(heads)]

    def rows_at(ref, at):
        return lambda head: ref[head : head + 1, at]

    def hop(index, carry):
        chip = jnp.where(
            index < 2,
            links.chip_d,
            jnp.where(index < 4, links.chip_x, jnp.where(index < 6, links.chip_y, links.chip)),
        )
        core = jnp.where(lax.rem(index, 2) == 0, links.other, links.core)

        @pl.when(index == 1)
        def _():
            sum_kv.hand(0)

        @pl.when(index == 2)
        def _():
            sum_kv.merge(0)
            sum_kv.four.send_far()

        @pl.when(index == 3)
        def _():
            sum_kv.hand(1)

        @pl.when(index == 4)
        def _():
            sum_kv.merge(1)
            sum_kv.four.ready[0].start()
            gms.near()
            gms.far()

        @pl.when(index == 5)
        def _():
            sum_kv.hand(2)
            ring_mlp.send_summed()
            total = sum_mlp.four.total().astype(B16)
            h_mlp[links.core, links.chip, :span, :] = total[:span]
            fc_piece[...] = total[span:].reshape(members, small, half)
            own = pl.ds(pl.multiple_of(span + small * z, 16), small)
            h_mlp[links.core, links.chip, own, :] = fc_piece[z]
            for transfer in spread_fc:
                transfer.start()

        @pl.when(index == 6)
        def _():
            sum_kv.merge(2)
            sum_kv.four.ready[1].start()
            sum_kv.four.send_summed()

        block_id = ids[2 * (2 * chip + core)]
        low = (block_id < own_block).astype(jnp.int32)
        in_low = chosen(low, (1, block))
        kv_low = kv[core, chip, low_rows, :]
        kv_pick = jnp.where(chosen(low, kv_low.shape), kv_low, kv[core, chip, high_rows, :])
        q_mask = chosen(low, (block, 4 * HEAD))

        def pick(ref):
            return [
                jnp.where(q_mask, ref[head, low_rows, :], ref[head, high_rows, :])
                for head in range(heads)
            ]

        def pick_row(ref):
            return lambda head: jnp.where(
                in_low, ref[head : head + 1, low_rows], ref[head : head + 1, high_rows]
            )

        query_grad, first = tile(
            kv_low,
            stacked(qm, high_rows),
            stacked(dom, high_rows),
            rows_at(lse, high_rows),
            rows_at(delta, high_rows),
        )
        for head in range(heads):
            dq[1, head_rows(head), :] += query_grad[head]
        query_grad, second = tile(kv_pick, pick(qm), pick(dom), pick_row(lse), pick_row(delta))
        for head in range(heads):
            at = head_rows(head)
            dq[0, at, :] += jnp.where(in_low, query_grad[head], 0.0)
            dq[1, at, :] += jnp.where(in_low, 0.0, query_grad[head])
        mask = chosen(low, second.shape)
        dkv[core, chip, low_rows, :] = (first + jnp.where(mask, second, 0.0)).astype(B16)
        dkv[core, chip, high_rows, :] = jnp.where(mask, 0.0, second).astype(B16)
        return carry

    lax.fori_loop(0, 7, hop, 0)
    sum_kv.hand(3)
    grad_mid = gm_all[...].reshape(group, width)
    product = jnp.dot(attn_t[...], grad_mid, preferred_element_type=F32).astype(B16)
    for core in range(2):
        g_attn[core, :, span:, :] = product[:, core * half : (core + 1) * half].reshape(4, small, half)
    block_out[...] = ring_mlp.total() + mid_own[...] + out_bias
    for keys_at, queries_at, masked in (
        (low_rows, high_rows, False),
        (low_rows, low_rows, True),
        (high_rows, high_rows, True),
    ):
        query_grad, both = tile(
            kv[links.core, links.chip, keys_at, :],
            stacked(qm, queries_at),
            stacked(dom, queries_at),
            rows_at(lse, queries_at),
            rows_at(delta, queries_at),
            masked,
        )
        part = 0 if queries_at is low_rows else 1
        for head in range(heads):
            dq[part, head_rows(head), :] += query_grad[head]
        if keys_at is low_rows and not masked:
            held = both
        elif keys_at is low_rows:
            dkv[links.core, links.chip, keys_at, :] = (held + both).astype(B16)
        else:
            dkv[links.core, links.chip, keys_at, :] = both.astype(B16)

    grad_query = jnp.concatenate([dq[0].T, dq[1].T], axis=0) * HEAD**-0.5
    sum_kv.merge(3)
    for transfer in spread_fc:
        transfer.arrived()
    own_kv = sum_kv.four.total().astype(B16)
    gather_mlp.start()
    split = jnp.concatenate(
        [
            jnp.sum(grad_query, axis=0, keepdims=True),
            jnp.sum(own_kv[:, span:].astype(F32), axis=0, keepdims=True),
            jnp.zeros((1, width - 2 * span), F32),
        ],
        axis=1,
    )
    rowsum[6:7, :] = split
    gqkv[...] = jnp.concatenate(
        [grad_query.astype(B16), own_kv, jnp.zeros((group, 640 - 3 * span), B16)], axis=1
    )

    def attn_weights(core):
        cols = pl.ds(pl.multiple_of(core * 256, 256), half)
        product = rows_product(norm1[...], gqkv[:, cols]).astype(B16)
        product = product.reshape(members, 4, small, half)
        for member in range(members):
            g_attn[core, :, member * small : (member + 1) * small, :] = product[member]

    attn_weights(links.other)
    for k in range(4):
        sum_attn.hand(k)
    attn_weights(links.core)
    for k in range(3):
        sum_attn.merge(k)
        sum_attn.four.sends[k].start()
    gather_mlp.forward()

    def norm1_block(index, carry):
        members_of = pair(index)
        ats = [member_rows(member) for member in members_of]
        back = transposed_product(
            both_rows(gqkv, ats)[:, : 3 * span], w_all[...].reshape(width, width)[:, : 3 * span]
        )
        rowsum[0:1, :] += jnp.sum(back * both_rows(normed1, ats), axis=0, keepdims=True)
        rowsum[1:2, :] += jnp.sum(back, axis=0, keepdims=True)
        back_half = back.astype(B16)
        for k in range(2):
            gn1[members_of[k]] = back_half[k * rows : (k + 1) * rows]

        @pl.when(index == 0)
        def _():
            ring_gn1.send_far()
            ring_gn1.ready[0].start()

        @pl.when(index == 1)
        def _():
            ring_gn1.ready[1].start()

        return carry

    lax.fori_loop(0, 2, norm1_block, 0)
    ring_gn1.send_summed()
    zsum[z] = rowsum[...]
    z_sums = [links.copy(zsum.at[z], zsum.at[z], links.to_z(s)) for s in (1, 3, 2)]
    for transfer in z_sums:
        transfer.start()
    sum_attn.merge(3)
    gather_mlp.hand_near()
    for transfer in z_sums:
        transfer.arrived()
    index = lax.broadcasted_iota(jnp.int32, rowsum.shape, 0)
    value = zsum[0] + zsum[1] + zsum[2] + zsum[3]
    value = jnp.where(index < 6, value, zsum[z])
    ssum[0] = value
    steps = [
        links.copy(ssum.at[k], bsum.at[k], device)
        for k, device in enumerate((links.to_core, links.to_x, links.to_y))
    ]
    steps[0].start()

    grad_norm1 = ring_gn1.total()
    _, normed, inv_std = layer_norm(x_all[z].astype(F32), one, zero_shift)
    input_grad[...] = gm_own[...] + norm_backward(grad_norm1, gain_one, normed, inv_std)

    steps[0].arrived()
    ssum[1] = ssum[0] + bsum[0]
    steps[1].start()
    total = sum_attn.four.total().astype(B16)
    h_attn[links.core, links.chip, span:, :] = total[span:]
    qkv_piece[...] = total[:span].reshape(members, small, half)
    own = pl.ds(pl.multiple_of(small * z, 16), small)
    h_attn[links.core, links.chip, own, :] = qkv_piece[z]
    for transfer in spread_qkv:
        transfer.start()
    steps[1].arrived()
    ssum[2] = ssum[1] + bsum[1]
    steps[2].start()
    for transfer in spread_qkv:
        transfer.arrived()
    gather_attn.start()
    steps[2].arrived()
    total = ssum[2] + bsum[2]
    mine = total[:, :span]
    for m in range(1, members):
        mine = jnp.where(
            chosen((z == m).astype(jnp.int32), mine.shape), total[:, m * span : (m + 1) * span], mine
        )
    sums[:6, :span] = mine[:6]
    sums[6:8, :] = total[6:8]
    gather_mlp.hand_far()
    gather_attn.finish()
    gather_mlp.own_core.arrived()
    gather_mlp.x_core.arrived()
    gather_mlp.y_core.arrived()
    gather_mlp.d_core.arrived()


def block_kernel(*refs):
    ids, x, cot, qkvw, fcw, projw = refs[:6]
    vectors = refs[6:14]
    outw, fcb = refs[14:16]
    outs = refs[16:21]
    lse, qm, kv, x_all, w_all, cot_all, fc_all, proj_all, vec_all, norm1, normed1 = refs[21:32]
    front = refs[32:39]
    a_all = refs[39]
    links = Links(*refs[-2:])
    attn_t = a_all.at[links.z]
    shared = (lse, qm, kv, x_all, w_all, cot_all, fc_all, proj_all, vec_all, norm1)
    arriving = forward_phase(
        links, ids, x, cot, qkvw, fcw, projw, *vectors, attn_t, *shared, normed1, *front
    )
    backward_phase(
        links, arriving, ids, attn_t, *shared, projw, outw, fcb, *outs, normed1, *refs[39:-2]
    )
    links.drain()


def block_call(ids, x, cot, qkvw, fcw, projw, *vectors):
    rows, width = x.shape
    members = 4
    span = qkvw.shape[0]
    group = members * rows
    block = group // 2
    heads = span // HEAD
    half = width // 2
    small = span // 4
    mlp_rows, attn_rows = 2 * span, span + small

    def shape(dims, dtype=B16):
        return jax.ShapeDtypeStruct(dims, dtype)

    def summed(rows_of, cols):
        return [
            VMEM((4, rows_of, cols), B16),
            VMEM((rows_of, cols), B16),
            VMEM((2, rows_of, cols), B16),
        ]

    def ring():
        return [
            VMEM((members, rows, width), B16),
            VMEM((rows, width), B16),
            VMEM((2, rows, width), B16),
        ]

    outs = (
        shape((rows, width), F32),
        shape((rows, width), F32),
        shape((2, 4, mlp_rows, half)),
        shape((2, 4, attn_rows, half)),
        shape((8, width), F32),
    )
    scratch = (
        [
            VMEM((8, group), F32),
            VMEM((heads, group, 4 * HEAD), B16),
            VMEM((2, 4, group, 2 * span), B16),
            VMEM((members, rows, width), B16),
            VMEM((members, span, width), B16),
            VMEM((members, rows, width), B16),
            VMEM((members, span, width), B16),
            VMEM((members, span, width), B16),
            VMEM((members, 16, 256), B16),
            VMEM((group, width), B16),
            VMEM((group, width), F32),
            VMEM((members, span, width), B16),
            VMEM((8, block), F32),
            VMEM((8, block), F32),
            VMEM((span, block), F32),
            VMEM((2, 8, block), F32),
            VMEM((2, 8, block), F32),
            VMEM((2, span, block), F32),
            VMEM((members, span, group), B16),
            VMEM((group, width), F32),
            VMEM((group, width), B16),
            VMEM((group, width), B16),
            VMEM((group, width), B16),
        ]
        + ring()
        + ring()
        + ring()
        + [
            VMEM((members, rows, width), B16),
            VMEM((rows, width), F32),
            VMEM((rows, width), F32),
            VMEM((2, 4, group, 2 * span), B16),
        ]
        + summed(group, 2 * span)
        + [VMEM((2, 4, mlp_rows, half), B16)]
        + summed(mlp_rows, half)
        + [VMEM((2, 4, attn_rows, half), B16)]
        + [VMEM((4, attn_rows, half), B16), VMEM((3, attn_rows, half), B16)]
        + [
            VMEM((members, small, half), B16),
            VMEM((members, small, half), B16),
            VMEM((heads, group, 4 * HEAD), B16),
            VMEM((8, group), F32),
            VMEM((2, span, block), F32),
            VMEM((group, 640), B16),
            VMEM((members, 8, width), F32),
            VMEM((3, 8, width), F32),
            VMEM((3, 8, width), F32),
            VMEM((8, width), F32),
            VMEM((members, rows, 4 * HEAD), B16),
            VMEM((members, rows, 4 * HEAD), B16),
            pltpu.SemaphoreType.DMA((176,)),
            pltpu.SemaphoreType.DMA((176,)),
        ]
    )
    args = (ids, x, cot, qkvw, fcw, projw) + vectors
    return pl.pallas_call(
        block_kernel,
        out_shape=outs,
        in_specs=[pl.BlockSpec(memory_space=SMEM)] + [pl.BlockSpec(memory_space=VMEM)] * (len(args) - 1),
        out_specs=(pl.BlockSpec(memory_space=VMEM),) * len(outs),
        scratch_shapes=scratch,
        compiler_params=pltpu.CompilerParams(
            collective_id=0, has_side_effects=True, vmem_limit_bytes=62 << 20
        ),
        name="block",
    )(*args)


def assemble_kernel(
    block_in, grad_in, h_mlp, h_attn, sums,
    block_out, grad_out, gain1, bias1, qkv, qbias, vbias, proj, pbias, gain2, bias2, fc, fbias, out, obias,
):
    small, width = proj.shape
    span = 4 * small
    half = width // 2
    block_out[...] = block_in[...]
    grad_out[...] = grad_in[...]
    for ref, index in ((gain1, 0), (bias1, 1), (pbias, 2), (gain2, 3), (bias2, 4), (obias, 5)):
        ref[...] = sums[index : index + 1, :span].reshape(span)
    qbias[...] = sums[6:7, :span].reshape(span)
    vbias[...] = sums[6:7, span : 2 * span].reshape(span)
    fbias[...] = sums[7:8, :].reshape(width)
    for core in range(2):
        cols = slice(core * half, (core + 1) * half)
        out[:, cols] = h_mlp[core, 0, :span, :].astype(F32)
        proj[:, cols] = h_attn[core, 0, span:, :].astype(F32)
        for member in range(4):
            at = span + member * small
            first = member * width + core * half
            fc[:, first : first + half] = h_mlp[core, 0, at : at + small, :].astype(F32)
    pieces = []
    for member in range(4):
        at = slice(member * small, (member + 1) * small)
        pieces.append(
            jnp.concatenate(
                [h_attn[0, 0, at, :], h_attn[1, 0, at, 128 : 3 * span - 256]], axis=1
            ).astype(F32)
        )
    qkv[...] = jnp.concatenate(
        [piece[:, t * span : (t + 1) * span] for t in range(3) for piece in pieces], axis=1
    )


def assemble(block_in, grad_in, h_mlp, h_attn, sums):
    width = block_in.shape[1]
    span = width // 4

    def shape(*dims):
        return jax.ShapeDtypeStruct(dims, F32)

    narrow = shape(span)
    outs = (
        shape(*block_in.shape), shape(*block_in.shape), narrow, narrow, shape(span, 3 * width), narrow, narrow,
        shape(span, width), narrow, narrow, narrow, shape(span, 4 * width), shape(width), shape(width, width),
        narrow,
    )
    def in_rows(array):
        if len(array.shape) == 1:
            return pl.BlockSpec(array.shape, lambda chip: (0,))
        return pl.BlockSpec((array.shape[0] // 4, array.shape[1]), lambda chip: (chip, 0))

    def of_chip(array):
        return pl.BlockSpec((2, 1) + array.shape[2:], lambda chip: (0, chip, 0, 0))

    return pl.pallas_call(
        assemble_kernel,
        out_shape=outs,
        grid=(4,),
        in_specs=[
            in_rows(block_in),
            in_rows(grad_in),
            of_chip(h_mlp),
            of_chip(h_attn),
            pl.BlockSpec(sums.shape, lambda chip: (0, 0)),
        ],
        out_specs=tuple(in_rows(array) for array in outs),
        compiler_params=pltpu.CompilerParams(vmem_limit_bytes=62 << 20),
        name="assemble",
    )(block_in, grad_in, h_mlp, h_attn, sums)


def head_shards(
    block_input,
    positions,
    norm1_gain,
    norm1_bias,
    qkv_weight,
    query_bias,
    value_bias,
    proj_weight,
    proj_bias,
    norm2_gain,
    norm2_bias,
    fc_weight,
    fc_bias,
    out_weight,
    out_bias,
    cotangent,
):
    rows, width = block_input.shape
    ids = positions.reshape(-1, 2 * rows)[:, 0] // (2 * rows)
    results = block_call(
        ids, block_input, cotangent, qkv_weight, fc_weight, proj_weight, norm1_gain, norm1_bias, proj_bias,
        norm2_gain, norm2_bias, out_bias, query_bias, value_bias, out_weight, fc_bias,
    )
    return assemble(*results)


def solution(mesh):
    sharded = P(("ctx", "fsdp"), None)
    rows, vector = P("fsdp", None), P("fsdp")
    in_specs = (
        sharded, P(), vector, vector, rows, vector, vector, rows, vector, vector, vector, rows, vector, rows,
        vector, sharded,
    )
    out_specs = (
        sharded, sharded, vector, vector, rows, vector, vector, rows, vector, vector, vector, rows, vector, rows,
        vector,
    )
    body = head_shards if dict(mesh.shape) == {"ctx": 8, "fsdp": 4} else shards
    return jax.shard_map(body, mesh=mesh, in_specs=in_specs, out_specs=out_specs, check_vma=False)
```

```python
import functools

import jax
import jax.numpy as jnp
from jax import lax
from jax.experimental import pallas as pl
from jax.experimental.pallas import tpu as pltpu
from jax.sharding import PartitionSpec as P

HEADS = 12
HEAD = 64


EPSILON = 1e-05
NEG_FILL = -1e30
GELU_C = 0.7978845608028654
GELU_K = 0.044715


def passed_along(block, axis, distance):
    devices = range(lax.axis_size(axis))
    route = [((i - distance) % len(devices), i) for i in devices]
    return lax.ppermute(block, axis, route)


def layer_norm(values_in, gain, shift):
    row_mean = jnp.mean(values_in, axis=-1, keepdims=True)
    centered = values_in - row_mean
    variance = jnp.mean(centered * centered, axis=-1, keepdims=True)
    inv_std = lax.rsqrt(variance + EPSILON)
    normed = centered * inv_std
    return (normed * gain.astype(jnp.float32) + shift.astype(jnp.float32), normed, inv_std)


def norm_backward(grad_norm, gain, normed, inv_std):
    scaled = grad_norm * gain.astype(jnp.float32)
    scaled_mean = jnp.mean(scaled, axis=-1, keepdims=True)
    cross_mean = jnp.mean(scaled * normed, axis=-1, keepdims=True)
    return inv_std * (scaled - scaled_mean - normed * cross_mean)


def gelu_forward(pre_act):
    cubed = pre_act * pre_act * pre_act
    return 0.5 * pre_act * (1.0 + jnp.tanh(GELU_C * (pre_act + GELU_K * cubed)))


def gelu_slope(pre_act):
    cubed = pre_act * pre_act * pre_act
    tanh_value = jnp.tanh(GELU_C * (pre_act + GELU_K * cubed))
    return 0.5 * (1.0 + tanh_value) + 0.5 * pre_act * (1.0 - tanh_value * tanh_value) * GELU_C * (
        1.0 + 3.0 * GELU_K * pre_act * pre_act
    )


def rows_product(left, right):
    return lax.dot_general(
        left, right, (((0,), (0,)), ((), ())), preferred_element_type=jnp.float32
    )


def transposed_product(left, right):
    return lax.dot_general(
        left, right, (((1,), (1,)), ((), ())), preferred_element_type=jnp.float32
    )


def split_heads(matrix):
    return matrix.reshape(matrix.shape[0], HEADS, HEAD)


def masked_scores(query, query_pos, keys, key_pos):
    scores = jnp.einsum(
        "rhd,khd->hrk", split_heads(query), split_heads(keys), preferred_element_type=jnp.float32
    ) * HEAD ** (-0.5)
    allowed = (key_pos[None, :] <= query_pos[:, None])[None]
    return (jnp.where(allowed, scores, NEG_FILL), allowed)


def attend_block(carried, query, query_pos, keys, values, key_pos):
    weighted, run_max, row_total = carried
    scores, allowed = masked_scores(query, query_pos, keys, key_pos)
    new_max = jnp.maximum(run_max, jnp.max(scores, axis=-1))
    weights = jnp.where(allowed, jnp.exp(scores - new_max[..., None]), 0.0)
    factor = jnp.exp(run_max - new_max)
    row_total = row_total * factor + jnp.sum(weights, axis=-1)
    update = jnp.einsum(
        "hrk,khd->rhd",
        weights,
        split_heads(values).astype(jnp.float32),
        precision=lax.Precision.HIGHEST,
        preferred_element_type=jnp.float32,
    )
    weighted = weighted * factor.T[:, :, None] + update
    return (weighted, new_max, row_total)


def attend_tile(carried, query, query_pos, keys, values, key_pos):
    half_rows = keys.shape[0] // 2
    latest = jnp.max(query_pos)
    for half_index in range(2):
        first_row = half_index * half_rows
        part_keys = keys[first_row : first_row + half_rows]
        part_values = values[first_row : first_row + half_rows]
        part_pos = key_pos[first_row : first_row + half_rows]

        def keep_state(state_in, block_keys, block_values, block_pos):
            return state_in

        def update_state(state_in, block_keys, block_values, block_pos):
            return attend_block(state_in, query, query_pos, block_keys, block_values, block_pos)

        carried = lax.cond(
            jnp.min(part_pos) > latest,
            keep_state,
            update_state,
            carried,
            part_keys,
            part_values,
            part_pos,
        )
    return carried


def block_grads(query, grad_attn, row_lse, row_delta, query_pos, keys, values, key_pos):
    scores, allowed = masked_scores(query, query_pos, keys, key_pos)
    probs = jnp.where(allowed, jnp.exp(scores - row_lse[..., None]), 0.0)
    grad_heads = split_heads(grad_attn)
    grad_values = jnp.einsum(
        "hrk,rhd->khd", probs.astype(jnp.bfloat16), grad_heads, preferred_element_type=jnp.float32
    )
    grad_probs = jnp.einsum(
        "rhd,khd->hrk", grad_heads, split_heads(values), preferred_element_type=jnp.float32
    )
    grad_scores = (probs * (grad_probs - row_delta[..., None])).astype(jnp.bfloat16)
    scale = HEAD ** (-0.5)
    grad_query = (
        jnp.einsum(
            "hrk,khd->rhd", grad_scores, split_heads(keys), preferred_element_type=jnp.float32
        )
        * scale
    )
    grad_keys = (
        jnp.einsum(
            "hrk,rhd->khd", grad_scores, split_heads(query), preferred_element_type=jnp.float32
        )
        * scale
    )
    key_rows = keys.shape[0]
    return (grad_query, grad_keys.reshape(key_rows, -1), grad_values.reshape(key_rows, -1))


def tile_grads(query, grad_attn, row_lse, row_delta, query_pos, keys, values, key_pos):
    half_rows = keys.shape[0] // 2
    key_width = keys.shape[1]
    latest = jnp.max(query_pos)
    query_total = jnp.zeros((query.shape[0], HEADS, HEAD), jnp.float32)
    key_parts = []
    value_parts = []
    for half_index in range(2):
        first_row = half_index * half_rows
        part_keys = keys[first_row : first_row + half_rows]
        part_values = values[first_row : first_row + half_rows]
        part_pos = key_pos[first_row : first_row + half_rows]

        def skipped(block_keys, block_values, block_pos):
            return (
                jnp.zeros((query.shape[0], HEADS, HEAD), jnp.float32),
                jnp.zeros((half_rows, key_width), jnp.float32),
                jnp.zeros((half_rows, key_width), jnp.float32),
            )

        def computed(block_keys, block_values, block_pos):
            return block_grads(
                query, grad_attn, row_lse, row_delta, query_pos, block_keys, block_values, block_pos
            )

        step_query, step_keys, step_values = lax.cond(
            jnp.min(part_pos) > latest, skipped, computed, part_keys, part_values, part_pos
        )
        query_total = query_total + step_query
        key_parts.append(step_keys)
        value_parts.append(step_values)
    return (query_total, jnp.concatenate(key_parts, axis=0), jnp.concatenate(value_parts, axis=0))


def shards(
    block_input,
    positions,
    norm1_gain,
    norm1_bias,
    qkv_weight,
    query_bias,
    value_bias,
    proj_weight,
    proj_bias,
    norm2_gain,
    norm2_bias,
    fc_weight,
    fc_bias,
    out_weight,
    out_bias,
    cotangent,
):
    rows = block_input.shape[0]
    width = block_input.shape[1]
    ctx_size = lax.axis_size("ctx")
    shard_count = lax.axis_size("fsdp")
    ctx_index = lax.axis_index("ctx")
    shard_index = lax.axis_index("fsdp")
    group_rows = rows * shard_count

    def key_positions(source):
        return lax.dynamic_slice_in_dim(positions, source * group_rows, group_rows)

    gain_one, shift_one, qkv_full, qbias_full, vbias_full, proj_full, pbias_full = (
        lax.all_gather(norm1_gain, "fsdp", axis=0, tiled=True),
        lax.all_gather(norm1_bias, "fsdp", axis=0, tiled=True),
        lax.all_gather(qkv_weight, "fsdp", axis=0, tiled=True),
        lax.all_gather(query_bias, "fsdp", axis=0, tiled=True),
        lax.all_gather(value_bias, "fsdp", axis=0, tiled=True),
        lax.all_gather(proj_weight, "fsdp", axis=0, tiled=True),
        lax.all_gather(proj_bias, "fsdp", axis=0, tiled=True),
    )
    gain_two, shift_two, fc_full, fbias_full, out_full, obias_full = (
        lax.all_gather(norm2_gain, "fsdp", axis=0, tiled=True),
        lax.all_gather(norm2_bias, "fsdp", axis=0, tiled=True),
        lax.all_gather(fc_weight, "fsdp", axis=0, tiled=True),
        lax.all_gather(fc_bias, "fsdp", axis=0, tiled=True),
        lax.all_gather(out_weight, "fsdp", axis=0, tiled=True),
        lax.all_gather(out_bias, "fsdp", axis=0, tiled=True),
    )
    residual = block_input.astype(jnp.float32)
    normed1_out, normed1, inv_std1 = layer_norm(residual, gain_one, shift_one)
    norm1 = normed1_out.astype(jnp.bfloat16)
    qkv = jnp.dot(norm1, qkv_full, preferred_element_type=jnp.float32)
    query = (qkv[:, :width] + qbias_full.astype(jnp.float32)).astype(jnp.bfloat16)
    keys = qkv[:, width : 2 * width].astype(jnp.bfloat16)
    values = (qkv[:, 2 * width :] + vbias_full.astype(jnp.float32)).astype(jnp.bfloat16)
    group_keys, group_values = (
        lax.all_gather(keys, "fsdp", axis=0, tiled=True),
        lax.all_gather(values, "fsdp", axis=0, tiled=True),
    )
    own_qpos = lax.dynamic_slice_in_dim(
        positions, (ctx_index * shard_count + shard_index) * rows, rows
    )
    own_kpos = key_positions(ctx_index)
    initial = (
        jnp.zeros((rows, HEADS, HEAD), jnp.float32),
        jnp.full((HEADS, rows), NEG_FILL, jnp.float32),
        jnp.zeros((HEADS, rows), jnp.float32),
    )
    carried = attend_tile(initial, query, own_qpos, group_keys, group_values, own_kpos)

    def forward_hop(hop_index, loop_carry):
        state_now, cycle_keys, cycle_values = loop_carry
        cycle_keys, cycle_values = passed_along((cycle_keys, cycle_values), "ctx", 1)
        source = (ctx_index - hop_index) % ctx_size
        state_now = attend_tile(
            state_now, query, own_qpos, cycle_keys, cycle_values, key_positions(source)
        )
        return (state_now, cycle_keys, cycle_values)

    result = lax.fori_loop(1, ctx_size, forward_hop, (carried, group_keys, group_values))
    carried = result[0]
    weighted, run_max, row_total = carried
    attn = (weighted / row_total.T[:, :, None]).reshape(rows, width).astype(jnp.bfloat16)
    row_lse = run_max + jnp.log(row_total)
    middle = (
        residual
        + jnp.dot(attn, proj_full, preferred_element_type=jnp.float32)
        + pbias_full.astype(jnp.float32)
    )
    normed2_out, normed2, inv_std2 = layer_norm(middle, gain_two, shift_two)
    norm2 = normed2_out.astype(jnp.bfloat16)
    pre_act = jnp.dot(norm2, fc_full, preferred_element_type=jnp.float32) + fbias_full.astype(
        jnp.float32
    )
    act = gelu_forward(pre_act).astype(jnp.bfloat16)
    block_output = (
        middle
        + jnp.dot(act, out_full, preferred_element_type=jnp.float32)
        + obias_full.astype(jnp.float32)
    )
    grad_out = cotangent.astype(jnp.float32)
    out_weight_grad = rows_product(act, cotangent)
    out_bias_grad = jnp.sum(grad_out, axis=0)
    grad_act = transposed_product(cotangent, out_full)
    grad_pre = grad_act * gelu_slope(pre_act)
    fc_bias_grad = jnp.sum(grad_pre, axis=0)
    grad_pre_half = grad_pre.astype(jnp.bfloat16)
    fc_weight_grad = rows_product(norm2, grad_pre_half)
    grad_norm2 = transposed_product(grad_pre_half, fc_full)
    norm2_gain_grad = jnp.sum(grad_norm2 * normed2, axis=0)
    norm2_bias_grad = jnp.sum(grad_norm2, axis=0)
    grad_middle = grad_out + norm_backward(grad_norm2, gain_two, normed2, inv_std2)
    mlp_shares = (
        lax.psum_scatter(norm2_gain_grad, "fsdp", scatter_dimension=0, tiled=True),
        lax.psum_scatter(norm2_bias_grad, "fsdp", scatter_dimension=0, tiled=True),
        lax.psum_scatter(fc_weight_grad, "fsdp", scatter_dimension=0, tiled=True),
        lax.psum_scatter(fc_bias_grad, "fsdp", scatter_dimension=0, tiled=True),
        lax.psum_scatter(out_weight_grad, "fsdp", scatter_dimension=0, tiled=True),
        lax.psum_scatter(out_bias_grad, "fsdp", scatter_dimension=0, tiled=True),
    )
    proj_bias_grad = jnp.sum(grad_middle, axis=0)
    grad_middle_half = grad_middle.astype(jnp.bfloat16)
    proj_weight_grad = rows_product(attn, grad_middle_half)
    grad_attn = transposed_product(grad_middle_half, proj_full).astype(jnp.bfloat16)
    row_delta = jnp.sum(
        split_heads(grad_attn).astype(jnp.float32) * split_heads(attn).astype(jnp.float32), axis=-1
    ).T
    grad_query, grad_keys, grad_values = tile_grads(
        query, grad_attn, row_lse, row_delta, own_qpos, group_keys, group_values, own_kpos
    )

    def pass_key_grads(key_grads):
        return passed_along((key_grads[0], key_grads[1]), "ctx", 1)

    def backward_hop(hop_index, loop_carry):
        query_sum, key_grads, cycle_keys, cycle_values = loop_carry
        cycle_keys, cycle_values = passed_along((cycle_keys, cycle_values), "ctx", 1)
        key_grads = pass_key_grads(key_grads)
        source = (ctx_index - hop_index) % ctx_size
        step_query, step_keys, step_values = tile_grads(
            query,
            grad_attn,
            row_lse,
            row_delta,
            own_qpos,
            cycle_keys,
            cycle_values,
            key_positions(source),
        )
        return (
            query_sum + step_query,
            (key_grads[0] + step_keys, key_grads[1] + step_values),
            cycle_keys,
            cycle_values,
        )

    result = lax.fori_loop(
        1, ctx_size, backward_hop, (grad_query, (grad_keys, grad_values), group_keys, group_values)
    )
    grad_query = result[0]
    key_grads = pass_key_grads(result[1])
    own_key_grad, own_value_grad = (
        lax.psum_scatter(key_grads[0], "fsdp", scatter_dimension=0, tiled=True),
        lax.psum_scatter(key_grads[1], "fsdp", scatter_dimension=0, tiled=True),
    )
    grad_query_rows = grad_query.reshape(rows, width)
    query_bias_grad = jnp.sum(grad_query_rows, axis=0)
    value_bias_grad = jnp.sum(own_value_grad, axis=0)
    grad_qkv = jnp.concatenate([grad_query_rows, own_key_grad, own_value_grad], axis=1).astype(
        jnp.bfloat16
    )
    qkv_weight_grad = rows_product(norm1, grad_qkv)
    grad_norm1 = transposed_product(grad_qkv, qkv_full)
    norm1_gain_grad = jnp.sum(grad_norm1 * normed1, axis=0)
    norm1_bias_grad = jnp.sum(grad_norm1, axis=0)
    input_grad = grad_middle + norm_backward(grad_norm1, gain_one, normed1, inv_std1)
    attn_shares = (
        lax.psum_scatter(norm1_gain_grad, "fsdp", scatter_dimension=0, tiled=True),
        lax.psum_scatter(norm1_bias_grad, "fsdp", scatter_dimension=0, tiled=True),
        lax.psum_scatter(qkv_weight_grad, "fsdp", scatter_dimension=0, tiled=True),
        lax.psum_scatter(query_bias_grad, "fsdp", scatter_dimension=0, tiled=True),
        lax.psum_scatter(value_bias_grad, "fsdp", scatter_dimension=0, tiled=True),
        lax.psum_scatter(proj_weight_grad, "fsdp", scatter_dimension=0, tiled=True),
        lax.psum_scatter(proj_bias_grad, "fsdp", scatter_dimension=0, tiled=True),
    )
    totals = lax.psum(
        (
            attn_shares[0],
            attn_shares[1],
            attn_shares[2],
            attn_shares[3],
            attn_shares[4],
            attn_shares[5],
            attn_shares[6],
            mlp_shares[0],
            mlp_shares[1],
            mlp_shares[2],
            mlp_shares[3],
            mlp_shares[4],
            mlp_shares[5],
        ),
        "ctx",
    )
    return (
        block_output,
        input_grad,
        totals[0],
        totals[1],
        totals[2],
        totals[3],
        totals[4],
        totals[5],
        totals[6],
        totals[7],
        totals[8],
        totals[9],
        totals[10],
        totals[11],
        totals[12],
    )


MESH = pl.DeviceIdType.MESH
SMEM = pltpu.SMEM
VMEM = pltpu.VMEM
F32 = jnp.float32
B16 = jnp.bfloat16


class Transfer:
    def __init__(self, links, src, dst, device):
        self.args = dict(
            src_ref=src,
            dst_ref=dst,
            send_sem=links.send_sem.at[links.count],
            recv_sem=links.recv_sem.at[links.count],
            device_id=device,
            device_id_type=MESH,
        )
        links.count += 1
        links.sent.append(self)

    def start(self):
        pltpu.make_async_remote_copy(**self.args).start()
        return self

    def arrived(self):
        pltpu.make_async_remote_copy(**self.args).wait_recv()

    def left(self):
        pltpu.make_async_remote_copy(**self.args).wait_send()


class Links:
    def __init__(self, send_sem, recv_sem):
        self.send_sem, self.recv_sem = send_sem, recv_sem
        self.count = 0
        self.sent = []
        ctx = lax.axis_index("ctx")
        self.ctx = ctx
        self.z = lax.axis_index("fsdp")
        self.core = lax.rem(ctx, 2)
        self.chip = lax.div(ctx, 2)
        x, y = lax.rem(self.chip, 2), lax.div(self.chip, 2)
        self.chip_x = self.chip + 1 - 2 * x
        self.chip_y = self.chip + 2 - 4 * y
        self.chip_d = 3 - self.chip
        self.other = 1 - self.core
        self.to_core = {"ctx": self.chip * 2 + self.other}
        self.to_x = {"ctx": self.chip_x * 2 + self.core}
        self.to_y = {"ctx": self.chip_y * 2 + self.core}
        self.to_d = {"ctx": self.chip_d * 2 + self.core}

    def zed(self, step):
        return lax.rem(self.z + step, 4)

    def to_z(self, step):
        return {"fsdp": self.zed(step)}

    def peers(self):
        near = [self.to_core, self.to_x, self.to_y, self.to_d]
        return near + [self.to_z(step) for step in (1, 2, 3)]

    def copy(self, src, dst, device):
        return Transfer(self, src, dst, device)

    def greet(self):
        barrier = pltpu.get_barrier_semaphore()
        for device in self.peers():
            pl.semaphore_signal(barrier, inc=1, device_id=device, device_id_type=MESH)

    def greeted(self):
        pl.semaphore_wait(pltpu.get_barrier_semaphore(), len(self.peers()))

    def drain(self):
        for transfer in self.sent:
            transfer.left()


class RingGather:
    def __init__(self, links, buf):
        half = buf.shape[1] // 2
        own, left, right = links.z, links.zed(3), links.zed(1)

        def piece(member, part):
            return buf.at[member, part * half : (part + 1) * half]

        def move(member, part, step):
            return links.copy(piece(member, part), piece(member, part), links.to_z(step))

        self.first = [move(own, 0, 1), move(own, 1, 3), move(own, 1, 1), move(own, 0, 3)]
        self.second = [move(left, 0, 1), move(right, 1, 3)]

    def start(self):
        for transfer in self.first:
            transfer.start()

    def forward(self):
        for transfer, onward in zip(self.first[:2], self.second):
            transfer.arrived()
            onward.start()

    def near(self):
        for transfer in self.first[2:]:
            transfer.arrived()

    def far(self):
        for transfer in self.second:
            transfer.arrived()


class Shared:
    def __init__(self, links, source, target):
        small, half = target.shape[1] // 4, target.shape[2] // 2
        cols = pl.ds(pl.multiple_of(links.core * half, 128), half)

        def rows(chip):
            return pl.ds(pl.multiple_of(chip * small, 16), small)

        def move(chip, part, device):
            ref = target.at[2 * part : 2 * part + 2, rows(chip), cols]
            return links.copy(ref, ref, device)

        own = rows(links.chip)
        place = target.at[links.z, own, cols]
        place[...] = source(links.z, own)[...]
        self.cross = [
            links.copy(source(links.zed(step), own), place, links.to_z(step)) for step in (2, 1, 3)
        ]
        own, x, y = links.chip, links.chip_x, links.chip_y
        self.near = [
            move(own, 0, links.to_x),
            move(own, 1, links.to_y),
            move(own, 1, links.to_x),
            move(own, 0, links.to_y),
        ]
        self.onward = [move(x, 0, links.to_y), move(y, 1, links.to_x)]
        ref = target.at[:, :, cols]
        self.hand = links.copy(ref, ref, links.to_core)

    def start(self):
        for transfer in self.cross:
            transfer.start()

    def gather(self):
        for transfer in self.cross:
            transfer.arrived()
        for transfer in self.near:
            transfer.start()

    def forward(self):
        for transfer, onward in zip(self.near[:2], self.onward):
            transfer.arrived()
            onward.start()

    def give(self):
        for transfer in self.near[2:] + self.onward:
            transfer.arrived()
        self.hand.start()

    def finish(self):
        self.hand.arrived()


class ContextGather:
    def __init__(self, links, buf):
        cuts = parts_of(buf.shape[2])

        def move(chip, part, device):
            rows = slice(None) if part is None else cuts[part]
            ref = buf.at[links.core, chip, rows]
            return links.copy(ref, ref, device)

        own, x, y, d = links.chip, links.chip_x, links.chip_y, links.chip_d
        self.own_core = move(own, None, links.to_core)
        self.x_parts = [move(own, 0, links.to_x), move(own, 1, links.to_x)]
        self.y_parts = [move(own, 1, links.to_y), move(own, 0, links.to_y)]
        self.onward = [move(x, 0, links.to_y), move(y, 1, links.to_x)]
        self.x_core = move(x, None, links.to_core)
        self.y_core = move(y, None, links.to_core)
        self.d_core = move(d, None, links.to_core)

    def start(self):
        for transfer in (
            self.x_parts[0],
            self.y_parts[0],
            self.own_core,
            self.x_parts[1],
            self.y_parts[1],
        ):
            transfer.start()

    def forward(self):
        self.x_parts[0].arrived()
        self.onward[0].start()
        self.y_parts[0].arrived()
        self.onward[1].start()

    def hand_near(self):
        self.x_parts[1].arrived()
        self.x_core.start()
        self.y_parts[1].arrived()
        self.y_core.start()

    def hand_far(self):
        self.onward[0].arrived()
        self.onward[1].arrived()
        self.d_core.start()


class DirectGather:
    def __init__(self, links, buf):
        def move(chip, device):
            ref = buf.at[links.core, chip]
            return links.copy(ref, ref, device)

        self.first = [move(links.chip, device) for device in (links.to_d, links.to_x, links.to_y)]
        self.own_core = move(links.chip, links.to_core)
        self.hands = [
            move(chip, links.to_core) for chip in (links.chip_d, links.chip_x, links.chip_y)
        ]

    def start(self):
        for transfer in self.first + [self.own_core]:
            transfer.start()

    def finish(self):
        for k in (1, 2, 0):
            self.first[k].arrived()
            self.hands[k].start()
        for transfer in [self.own_core] + self.hands:
            transfer.arrived()


def chosen(flag, shape):
    return jnp.full(shape, flag, jnp.int32) == 1


def masked_heads(value, first, width):
    rows, span = value.shape
    pieces = []
    if first > 0:
        pieces.append(jnp.zeros((rows, first), value.dtype))
    pieces.append(value)
    if first + span < width:
        pieces.append(jnp.zeros((rows, width - first - span), value.dtype))
    wide = jnp.concatenate(pieces, axis=1) if len(pieces) > 1 else value
    head = (lax.broadcasted_iota(jnp.int32, (rows, width), 1) - first + HEAD) // HEAD - 1
    return [
        jnp.where(head == index, wide.astype(F32), 0.0).astype(value.dtype)
        for index in range(span // HEAD)
    ]


def soft_step(scores, old_max, old_sum):
    new_max = jnp.maximum(old_max, jnp.max(scores, axis=0, keepdims=True))
    weights = jnp.exp(scores - new_max)
    factor = jnp.exp(old_max - new_max)
    new_sum = old_sum * factor + jnp.sum(weights, axis=0, keepdims=True)
    return weights.astype(B16), factor, new_max, new_sum


def forward_phase(
    links, ids, x, cot, qkvw, fcw, projw, v0, v1, v2, v3, v4, v5, qbias, vbias,
    attn_t, lse, qm, kv, x_all, w_all, cot_all, fc_all, proj_all, vec_all, norm1, normed1,
    stage, max_h, sum_h, acc_h, max_x, sum_x, acc_x,
):
    rows = x.shape[0]
    span = qkvw.shape[0]
    block = 2 * rows
    heads = span // HEAD
    z = links.z
    links.greet()
    x_all[z] = x[...]
    cot_all[z] = cot[...]
    own_vectors = jnp.concatenate(
        [v[...].astype(F32).reshape(1, span) for v in (v0, v1, v2, v3, v4, v5)]
        + [jnp.zeros((10, span), F32)],
        axis=0,
    )
    vec_all[z, :, :span] = own_vectors.astype(B16)
    for member in range(4):
        stage[member, :, : 3 * span] = jnp.concatenate(
            [qkvw[:, t * 4 * span + member * span : t * 4 * span + (member + 1) * span] for t in range(3)],
            axis=1,
        )

    vectors = [
        links.copy(vec_all.at[z], vec_all.at[z], links.to_z(step)) for step in (1, 3, 2)
    ]
    inputs = RingGather(links, x_all)
    half = cot.shape[1] // 2

    def own_cols(first):
        return pl.ds(pl.multiple_of(first + links.core * half, 128), half)

    weights = Shared(links, lambda member, at: stage.at[member, at, own_cols(0)], w_all)
    cots = RingGather(links, cot_all)
    fcs_in = Shared(links, lambda member, at: fcw.at[at, own_cols(member * 2 * half)], fc_all)
    projs = Shared(links, lambda member, at: projw.at[at, own_cols(0)], proj_all)
    context = ContextGather(links, kv)

    links.greeted()
    for transfer in vectors:
        transfer.start()
    weights.start()
    inputs.start()
    for transfer in vectors:
        transfer.arrived()

    gain = jnp.concatenate([vec_all[m, 0:1, :span] for m in range(4)], axis=1).astype(F32)
    shift = jnp.concatenate([vec_all[m, 1:2, :span] for m in range(4)], axis=1).astype(F32)

    def normalise(member):
        shifted, normed, _ = layer_norm(x_all[member].astype(F32), gain, shift)
        at = pl.ds(pl.multiple_of(member * rows, rows), rows)
        norm1[at, :] = shifted.astype(B16)
        normed1[at, :] = normed

    normalise(z)
    inputs.forward()
    weights.gather()
    fcs_in.start()
    projs.start()
    inputs.near()
    normalise(links.zed(1))
    normalise(links.zed(3))
    weights.forward()
    inputs.far()
    cots.start()
    normalise(links.zed(2))
    weights.give()
    fcs_in.gather()
    weights.finish()

    matrix = w_all[...].reshape(4 * span, w_all.shape[2])[:, : 3 * span]
    for part in range(2):
        at = slice(part * block, (part + 1) * block)
        product = jnp.dot(norm1[at, :], matrix, preferred_element_type=F32)
        query = (product[:, :span] + qbias[...].astype(F32).reshape(1, span)).astype(B16)
        query = query * jnp.asarray(HEAD**-0.5, B16)
        for head, lone in enumerate(masked_heads(query, 0, 4 * HEAD)):
            qm[head, at, :] = lone
        values = product[:, 2 * span :] + vbias[...].astype(F32).reshape(1, span)
        kv[links.core, links.chip, at, :] = jnp.concatenate(
            [product[:, span : 2 * span], values], axis=1
        ).astype(B16)
    context.start()

    own_block = ids[2 * links.ctx]
    keep = lax.broadcasted_iota(jnp.int32, (block, block), 0) <= lax.broadcasted_iota(
        jnp.int32, (block, block), 1
    )
    none = jnp.full((1, block), NEG_FILL, F32)
    zero = jnp.zeros((1, block), F32)

    def halves(core, chip, part):
        at = slice(part * block, (part + 1) * block)
        return kv[core, chip, at, : 4 * HEAD], kv[core, chip, at, 2 * HEAD :].T

    def value_rows(head):
        return slice((1 + head) * HEAD, (2 + head) * HEAD)

    def head_rows(head):
        return slice(head * HEAD, (head + 1) * HEAD)

    k_low, vt_low = halves(links.core, links.chip, 0)
    k_high, vt_high = halves(links.core, links.chip, 1)
    for head in range(heads):
        q_low, q_high = qm[head, :block, :], qm[head, block:, :]
        scores = jnp.where(keep, transposed_product(k_low, q_low), NEG_FILL)
        w, _, top, total = soft_step(scores, none, zero)
        max_x[0, head : head + 1, :] = top
        sum_x[0, head : head + 1, :] = total
        acc_x[0, head_rows(head), :] = jnp.dot(
            vt_low[value_rows(head)], w, preferred_element_type=F32
        )
        scores = transposed_product(k_low, q_high)
        w, _, top, total = soft_step(scores, none, zero)
        acc = jnp.dot(vt_low[value_rows(head)], w, preferred_element_type=F32)
        scores = jnp.where(keep, transposed_product(k_high, q_high), NEG_FILL)
        w, factor, top, total = soft_step(scores, top, total)
        max_h[head : head + 1, :] = top
        sum_h[head : head + 1, :] = total
        acc_h[head_rows(head), :] = acc * factor + jnp.dot(
            vt_high[value_rows(head)], w, preferred_element_type=F32
        )
    max_x[1] = jnp.full_like(max_h, NEG_FILL)
    sum_x[1] = jnp.zeros_like(sum_h)
    acc_x[1] = jnp.zeros_like(acc_h)

    def hop(index, carry):
        near = index < 3
        far = index >= 5
        core = jnp.where((index == 1) | (index == 2) | (index == 5), links.core, links.other)
        chip = jnp.where(
            index == 0,
            links.chip,
            jnp.where(far, links.chip_d, jnp.where(lax.rem(index, 2) == 1, links.chip_x, links.chip_y)),
        )

        @pl.when(index == 0)
        def _():
            context.own_core.arrived()
            fcs_in.forward()
            context.forward()

        @pl.when(index == 1)
        def _():
            context.hand_near()
            cots.forward()

        @pl.when(index == 2)
        def _():
            projs.gather()

        @pl.when(index == 3)
        def _():
            context.x_core.arrived()
            context.hand_far()

        @pl.when(index == 4)
        def _():
            context.y_core.arrived()
            cots.near()
            fcs_in.give()

        @pl.when(index == 5)
        def _():
            projs.forward()

        @pl.when(index == 6)
        def _():
            context.d_core.arrived()

        block_id = ids[2 * (2 * chip + core)]
        low = (block_id < own_block).astype(jnp.int32)
        in_low = chosen(low, (1, block))
        kv_low = kv[core, chip, :block, :]
        kv_high = kv[core, chip, block:, :]
        kv_pick = jnp.where(chosen(low, kv_low.shape), kv_low, kv_high)
        q_mask = chosen(low, (block, 4 * HEAD))
        work = []
        for head in range(heads):
            scores = transposed_product(kv_low[:, : 4 * HEAD], qm[head, block:, :])
            work.append((scores, max_h[head : head + 1, :], sum_h[head : head + 1, :]))
        for head in range(heads):
            q_pick = jnp.where(q_mask, qm[head, :block, :], qm[head, block:, :])
            scores = transposed_product(kv_pick[:, : 4 * HEAD], q_pick)
            at = slice(head, head + 1)
            work.append(
                (
                    scores,
                    jnp.where(in_low, max_x[0, at, :], max_x[1, at, :]),
                    jnp.where(in_low, sum_x[0, at, :], sum_x[1, at, :]),
                )
            )
        done = [soft_step(*entry) for entry in work]
        vt = kv_low[:, 2 * HEAD :].T
        for head in range(heads):
            w, factor, top, total = done[head]
            max_h[head : head + 1, :] = top
            sum_h[head : head + 1, :] = total
            acc_h[head_rows(head), :] = acc_h[head_rows(head), :] * factor + jnp.dot(
                vt[value_rows(head)], w, preferred_element_type=F32
            )
        vt = kv_pick[:, 2 * HEAD :].T
        for head in range(heads):
            w, factor, top, total = done[heads + head]
            acc = jnp.where(in_low, acc_x[0, head_rows(head), :], acc_x[1, head_rows(head), :])
            acc = acc * factor + jnp.dot(
                vt[value_rows(head)], w, preferred_element_type=F32
            )
            for part in range(2):
                own = in_low if part == 0 else ~in_low
                max_x[part, head : head + 1, :] = jnp.where(own, top, max_x[part, head : head + 1, :])
                sum_x[part, head : head + 1, :] = jnp.where(
                    own, total, sum_x[part, head : head + 1, :]
                )
                acc_x[part, head_rows(head), :] = jnp.where(own, acc, acc_x[part, head_rows(head), :])
        return carry

    lax.fori_loop(0, 7, hop, 0)
    for head in range(heads):
        at = slice(head, head + 1)
        total = sum_x[0, at, :]
        attn_t[head_rows(head), :block] = (acc_x[0, head_rows(head), :] / total).astype(B16)
        lse[at, :block] = max_x[0, at, :] + jnp.log(total)
        top = jnp.maximum(max_h[at, :], max_x[1, at, :])
        left, right = jnp.exp(max_h[at, :] - top), jnp.exp(max_x[1, at, :] - top)
        total = sum_h[at, :] * left + sum_x[1, at, :] * right
        acc = acc_h[head_rows(head), :] * left + acc_x[1, head_rows(head), :] * right
        attn_t[head_rows(head), block:] = (acc / total).astype(B16)
        lse[at, block:] = top + jnp.log(total)
    return cots, fcs_in, projs


def parts_of(rows):
    first = (rows // 2 + 15) // 16 * 16
    return [slice(0, first), slice(first, rows)]


class FourSum:
    def __init__(self, links, parts, early, late, far, own, near):
        self.parts, self.early, self.late, self.own, self.near = parts, early, late, own, near
        self.cuts = parts_of(early.shape[0])
        self.far = [
            links.copy(parts.at[far, self.cuts[k]], early.at[self.cuts[k]], near[k][0]) for k in range(2)
        ]
        self.ready, self.summed = [], []
        for k, (device, part, added) in enumerate(near):
            for half, group in ((1 - added, self.ready), (added, self.summed)):
                cut = self.cuts[half]
                group.append(links.copy(parts.at[part, cut], late.at[k, cut], device))

    def send_far(self):
        for transfer in self.far:
            transfer.start()

    def send_ready(self):
        for transfer in self.ready:
            transfer.start()

    def send_summed(self):
        for k, (_, part, added) in enumerate(self.near):
            cut = self.cuts[added]
            self.far[added].arrived()
            both = self.parts[part, cut].astype(F32) + self.early[cut].astype(F32)
            self.parts[part, cut] = both.astype(B16)
            self.summed[k].start()

    def total(self):
        for transfer in self.ready + self.summed:
            transfer.arrived()
        return (
            self.parts[self.own].astype(F32)
            + self.late[0].astype(F32)
            + self.late[1].astype(F32)
        )


class ThreeSum:
    def __init__(self, links, parts, late, own, targets):
        self.parts, self.late, self.own = parts, late, own
        self.sends = [
            links.copy(parts.at[part], late.at[k], device) for k, (device, part) in enumerate(targets)
        ]

    def total(self):
        value = self.parts[self.own].astype(F32)
        for k in (1, 2, 0):
            self.sends[k].arrived()
            value = value + self.late[k].astype(F32)
        return value


def ring_sum(links, parts, early, late):
    right, left = links.zed(1), links.zed(3)
    near = [(links.to_z(1), right, 0), (links.to_z(3), left, 1)]
    return FourSum(links, parts, early, late, links.zed(2), links.z, near)


class ContextSum:
    def __init__(self, links, grads, handed, early, late):
        self.links, self.grads, self.handed = links, grads, handed
        order = (links.chip_d, links.chip_x, links.chip_y, links.chip)
        self.order = order
        self.hands = [
            links.copy(grads.at[links.other, chip], handed.at[k], links.to_core)
            for k, chip in enumerate(order)
        ]
        if early is None:
            targets = [(links.to_d, order[0]), (links.to_x, order[1]), (links.to_y, order[2])]
            self.four = ThreeSum(links, grads.at[links.core], late, links.chip, targets)
            return
        near = [(links.to_x, links.chip_x, 1), (links.to_y, links.chip_y, 0)]
        self.four = FourSum(
            links, grads.at[links.core], early, late, links.chip_d, links.chip, near
        )

    def hand(self, k):
        self.hands[k].start()

    def merge(self, k):
        self.hands[k].arrived()
        core, chip = self.links.core, self.order[k]
        both = self.grads[core, chip].astype(F32) + self.handed[k].astype(F32)
        self.grads[core, chip] = both.astype(B16)


def backward_phase(
    links, arriving, ids, attn_t, lse, qm, kv, x_all, w_all, cot_all, fc_all, proj_all, vec_all, norm1, projw, outw, fcb,
    block_out, input_grad, h_mlp, h_attn, sums, normed1,
    a_all, grad_act, norm2, act, grad_pre, gn2, gn2_e, gn2_l, mlp, mlp_e, mlp_l, gn1, gn1_e, gn1_l,
    gm_all, gm_own, mid_own, dkv, dkv_h, dkv_e, dkv_l, g_mlp, gmlp_h, gmlp_e, gmlp_l,
    g_attn, gattn_h, gattn_l, fc_piece, qkv_piece, dom, delta, dq, gqkv, zsum, bsum, ssum, rowsum, ga_out, ga_in,
):
    members, rows, width = x_all.shape
    span = attn_t.shape[0]
    group = members * rows
    block = group // 2
    heads = span // HEAD
    half = width // 2
    small = span // 4
    z = links.z
    right, left, opposite = links.zed(1), links.zed(3), links.zed(2)

    def row(index):
        return jnp.concatenate(
            [vec_all[m, index : index + 1, :span] for m in range(members)], axis=1
        ).astype(F32)

    def head_rows(head):
        return slice(head * HEAD, (head + 1) * HEAD)

    def member_rows(member):
        return pl.ds(pl.multiple_of(member * rows, rows), rows)

    def pair(index):
        first = index == 0
        return jnp.where(first, opposite, left), jnp.where(first, right, z)

    def both_rows(ref, ats):
        return jnp.concatenate([ref[at, :] for at in ats], axis=0)

    attns = RingGather(links, a_all)
    gms = RingGather(links, gm_all)
    swaps = [
        links.copy(ga_out.at[links.zed(step)], ga_in.at[z], links.to_z(step)) for step in (2, 1, 3)
    ]
    ring_gn2 = ring_sum(links, gn2, gn2_e, gn2_l)
    ring_mlp = ring_sum(links, mlp, mlp_e, mlp_l)
    ring_gn1 = ring_sum(links, gn1, gn1_e, gn1_l)
    sum_mlp = ContextSum(links, g_mlp, gmlp_h, gmlp_e, gmlp_l)
    sum_attn = ContextSum(links, g_attn, gattn_h, None, gattn_l)
    sum_kv = ContextSum(links, dkv, dkv_h, dkv_e, dkv_l)
    gather_mlp = ContextGather(links, h_mlp)
    gather_attn = ContextGather(links, h_attn)

    def spread(piece, gathered, first):
        at = pl.ds(pl.multiple_of(first + small * z, 16), small)
        place = gathered.at[links.core, links.chip, at]
        return [links.copy(piece.at[links.zed(s)], place, links.to_z(s)) for s in (1, 3, 2)]

    spread_fc = spread(fc_piece, h_mlp, span)
    spread_qkv = spread(qkv_piece, h_attn, 0)

    cots, fcs_in, projs = arriving
    gain_one = row(0)
    gain_two, shift_two = row(3), row(4)
    proj_bias, out_bias = row(2), row(5)
    fc_bias = fcb[...].astype(F32).reshape(1, fcb.shape[0])
    attns.start()
    projs.give()
    cots.far()
    one, zero_shift = jnp.ones((1, width), F32), jnp.zeros((1, width), F32)

    def before(index, carry):
        cots_of = cot_all[pl.ds(2 * index, 2)].reshape(block, width)
        at = pl.ds(pl.multiple_of(index * block, block), block)
        grad_act[at, :] = transposed_product(cots_of, outw[...])
        return carry

    lax.fori_loop(0, 1, before, 0)
    attns.forward()
    lax.fori_loop(1, 2, before, 0)
    attns.near()
    attns.far()
    fcs_in.finish()
    projs.finish()
    rowsum[...] = jnp.zeros_like(rowsum)
    fc_matrix = fc_all.shape

    def mlp_block(index, carry):
        members_of = pair(index)
        ats = [member_rows(member) for member in members_of]
        attn_cols = jnp.concatenate([a_all[:, :, at].reshape(width, rows) for at in ats], axis=1)
        inputs_of = jnp.concatenate([x_all[member] for member in members_of], axis=0)
        middle = (
            inputs_of.astype(F32)
            + rows_product(attn_cols, proj_all[...].reshape(width, width))
            + proj_bias
        )
        shifted, normed, _ = layer_norm(middle, gain_two, shift_two)
        half_norm = shifted.astype(B16)
        fc = fc_all[...].reshape(width, fc_matrix[2])
        pre_act = jnp.dot(half_norm, fc, preferred_element_type=F32) + fc_bias
        squared = pre_act * pre_act
        tanh_value = jnp.tanh(GELU_C * pre_act * (1.0 + GELU_K * squared))
        act_half = (0.5 * pre_act * (1.0 + tanh_value)).astype(B16)
        slope = 0.5 * (1.0 + tanh_value) + (0.5 * GELU_C) * pre_act * (
            1.0 - tanh_value * tanh_value
        ) * (1.0 + 3.0 * GELU_K * squared)
        grad = both_rows(grad_act, ats) * slope
        rowsum[7:8, :] += jnp.sum(grad, axis=0, keepdims=True)
        grad_half = grad.astype(B16)
        back = transposed_product(grad_half, fc)
        rowsum[3:4, :] += jnp.sum(back * normed, axis=0, keepdims=True)
        rowsum[4:5, :] += jnp.sum(back, axis=0, keepdims=True)
        back_half = back.astype(B16)
        for k in range(2):
            part = slice(k * rows, (k + 1) * rows)
            gn2[members_of[k]] = back_half[part]
            norm2[ats[k], :] = half_norm[part]
            act[ats[k], :] = act_half[part]
            grad_pre[ats[k], :] = grad_half[part]

        @pl.when(index == 0)
        def _():
            ring_gn2.send_far()
            ring_gn2.ready[0].start()

        @pl.when(index == 1)
        def _():
            ring_gn2.ready[1].start()
            ring_gn2.send_summed()
            mid_own[...] = middle[rows:]

        return carry

    lax.fori_loop(0, 2, mlp_block, 0)

    def mlp_weights(core):
        cols = pl.ds(pl.multiple_of(core * half, half), half)
        cots = cot_all[:, :, cols].reshape(group, half)
        product = rows_product(act[...], cots).astype(B16)
        g_mlp[core, :, :span, :] = product.reshape(4, span, half)
        product = rows_product(norm2[...], grad_pre[:, cols]).astype(B16)
        product = product.reshape(members, 4, small, half)
        for member in range(members):
            at = span + member * small
            g_mlp[core, :, at : at + small, :] = product[member]

    mlp_weights(links.other)
    for k in range(4):
        sum_mlp.hand(k)
    mlp_weights(links.core)
    sum_mlp.merge(0)
    sum_mlp.four.send_far()
    sum_mlp.merge(1)
    sum_mlp.merge(2)
    sum_mlp.four.send_ready()

    grad_norm2 = ring_gn2.total()
    _, normed, inv_std = layer_norm(mid_own[...], gain_two, shift_two)
    cot_own = cot_all[z].astype(F32)
    grad_middle = cot_own + norm_backward(grad_norm2, gain_two, normed, inv_std)
    gm_own[...] = grad_middle
    grad_half = grad_middle.astype(B16)
    gm_all[z] = grad_half
    for transfer, step in zip(swaps, (2, 1, 3)):
        member = links.zed(step)
        ga_out[member, :, :span] = transposed_product(grad_half, proj_all[member]).astype(B16)
        transfer.start()
    ga_in[z, :, :span] = transposed_product(grad_half, proj_all[z]).astype(B16)
    gms.start()
    rowsum[2:3, :] = jnp.sum(grad_middle, axis=0, keepdims=True)
    rowsum[5:6, :] = jnp.sum(cot_own, axis=0, keepdims=True)

    sum_mlp.four.send_summed()
    sum_mlp.merge(3)

    def mlp_product(index, carry):
        at = pl.ds(pl.multiple_of(index * block, block), block)
        product = jnp.dot(act[at, :], outw[...], preferred_element_type=F32).astype(B16)
        mlp[pl.ds(2 * index, 2)] = product.reshape(2, rows, width)
        return carry

    lax.fori_loop(0, 2, mlp_product, 0)
    for transfer in swaps:
        transfer.arrived()
    gms.forward()
    ring_mlp.send_far()
    ring_mlp.send_ready()

    grad_attn = ga_in[...].reshape(group, ga_in.shape[2])[:, :span]
    grad_attn_t = grad_attn.astype(F32).T
    delta_rows = grad_attn_t * attn_t[...].astype(F32)
    for head in range(heads):
        delta[head : head + 1, :] = jnp.sum(delta_rows[head_rows(head), :], axis=0, keepdims=True)
    for head, lone in enumerate(masked_heads(grad_attn, HEAD, 4 * HEAD)):
        dom[head] = lone
    dq[...] = jnp.zeros_like(dq)

    own_block = ids[2 * links.ctx]
    keep = lax.broadcasted_iota(jnp.int32, (block, block), 0) <= lax.broadcasted_iota(
        jnp.int32, (block, block), 1
    )
    low_rows, high_rows = slice(0, block), slice(block, group)

    def tile(keys, queries, grads, lse_of, delta_of, masked=False):
        probs, scores_grad = [], []
        for head in range(heads):
            scores = transposed_product(keys[:, : 4 * HEAD], queries[head])
            if masked:
                scores = jnp.where(keep, scores, NEG_FILL)
            weights = jnp.exp(scores - lse_of(head))
            grad_probs = transposed_product(keys[:, 2 * HEAD :], grads[head])
            probs.append(weights.astype(B16))
            scores_grad.append((weights * (grad_probs - delta_of(head))).astype(B16))
        keys_t = keys[:, : 4 * HEAD].T
        query_grad = [
            jnp.dot(keys_t[head_rows(head)], scores_grad[head], preferred_element_type=F32)
            for head in range(heads)
        ]
        value_grad = jnp.dot(
            jnp.concatenate(probs, axis=1),
            jnp.concatenate(grads, axis=0),
            preferred_element_type=F32,
        )
        key_grad = jnp.dot(
            jnp.concatenate(scores_grad, axis=1),
            jnp.concatenate(queries, axis=0),
            preferred_element_type=F32,
        )
        both = jnp.concatenate(
            [
                key_grad[:, : 2 * HEAD],
                key_grad[:, 2 * HEAD :] + value_grad[:, : 2 * HEAD],
                value_grad[:, 2 * HEAD :],
            ],
            axis=1,
        )
        return query_grad, both

    def stacked(ref, at):
        return [ref[head, at, :] for head in range(heads)]

    def rows_at(ref, at):
        return lambda head: ref[head : head + 1, at]

    def hop(index, carry):
        chip = jnp.where(
            index < 2,
            links.chip_d,
            jnp.where(index < 4, links.chip_x, jnp.where(index < 6, links.chip_y, links.chip)),
        )
        core = jnp.where(lax.rem(index, 2) == 0, links.other, links.core)

        @pl.when(index == 1)
        def _():
            sum_kv.hand(0)

        @pl.when(index == 2)
        def _():
            sum_kv.merge(0)
            sum_kv.four.send_far()

        @pl.when(index == 3)
        def _():
            sum_kv.hand(1)

        @pl.when(index == 4)
        def _():
            sum_kv.merge(1)
            sum_kv.four.ready[0].start()
            gms.near()
            gms.far()

        @pl.when(index == 5)
        def _():
            sum_kv.hand(2)
            ring_mlp.send_summed()
            total = sum_mlp.four.total().astype(B16)
            h_mlp[links.core, links.chip, :span, :] = total[:span]
            fc_piece[...] = total[span:].reshape(members, small, half)
            own = pl.ds(pl.multiple_of(span + small * z, 16), small)
            h_mlp[links.core, links.chip, own, :] = fc_piece[z]
            for transfer in spread_fc:
                transfer.start()

        @pl.when(index == 6)
        def _():
            sum_kv.merge(2)
            sum_kv.four.ready[1].start()
            sum_kv.four.send_summed()

        block_id = ids[2 * (2 * chip + core)]
        low = (block_id < own_block).astype(jnp.int32)
        in_low = chosen(low, (1, block))
        kv_low = kv[core, chip, low_rows, :]
        kv_pick = jnp.where(chosen(low, kv_low.shape), kv_low, kv[core, chip, high_rows, :])
        q_mask = chosen(low, (block, 4 * HEAD))

        def pick(ref):
            return [
                jnp.where(q_mask, ref[head, low_rows, :], ref[head, high_rows, :])
                for head in range(heads)
            ]

        def pick_row(ref):
            return lambda head: jnp.where(
                in_low, ref[head : head + 1, low_rows], ref[head : head + 1, high_rows]
            )

        query_grad, first = tile(
            kv_low,
            stacked(qm, high_rows),
            stacked(dom, high_rows),
            rows_at(lse, high_rows),
            rows_at(delta, high_rows),
        )
        for head in range(heads):
            dq[1, head_rows(head), :] += query_grad[head]
        query_grad, second = tile(kv_pick, pick(qm), pick(dom), pick_row(lse), pick_row(delta))
        for head in range(heads):
            at = head_rows(head)
            dq[0, at, :] += jnp.where(in_low, query_grad[head], 0.0)
            dq[1, at, :] += jnp.where(in_low, 0.0, query_grad[head])
        mask = chosen(low, second.shape)
        dkv[core, chip, low_rows, :] = (first + jnp.where(mask, second, 0.0)).astype(B16)
        dkv[core, chip, high_rows, :] = jnp.where(mask, 0.0, second).astype(B16)
        return carry

    lax.fori_loop(0, 7, hop, 0)
    sum_kv.hand(3)
    grad_mid = gm_all[...].reshape(group, width)
    product = jnp.dot(attn_t[...], grad_mid, preferred_element_type=F32).astype(B16)
    for core in range(2):
        g_attn[core, :, span:, :] = product[:, core * half : (core + 1) * half].reshape(4, small, half)
    block_out[...] = ring_mlp.total() + mid_own[...] + out_bias
    for keys_at, queries_at, masked in (
        (low_rows, high_rows, False),
        (low_rows, low_rows, True),
        (high_rows, high_rows, True),
    ):
        query_grad, both = tile(
            kv[links.core, links.chip, keys_at, :],
            stacked(qm, queries_at),
            stacked(dom, queries_at),
            rows_at(lse, queries_at),
            rows_at(delta, queries_at),
            masked,
        )
        part = 0 if queries_at is low_rows else 1
        for head in range(heads):
            dq[part, head_rows(head), :] += query_grad[head]
        if keys_at is low_rows and not masked:
            held = both
        elif keys_at is low_rows:
            dkv[links.core, links.chip, keys_at, :] = (held + both).astype(B16)
        else:
            dkv[links.core, links.chip, keys_at, :] = both.astype(B16)

    grad_query = jnp.concatenate([dq[0].T, dq[1].T], axis=0) * HEAD**-0.5
    sum_kv.merge(3)
    for transfer in spread_fc:
        transfer.arrived()
    own_kv = sum_kv.four.total().astype(B16)
    gather_mlp.start()
    split = jnp.concatenate(
        [
            jnp.sum(grad_query, axis=0, keepdims=True),
            jnp.sum(own_kv[:, span:].astype(F32), axis=0, keepdims=True),
            jnp.zeros((1, width - 2 * span), F32),
        ],
        axis=1,
    )
    rowsum[6:7, :] = split
    gqkv[...] = jnp.concatenate(
        [grad_query.astype(B16), own_kv, jnp.zeros((group, 640 - 3 * span), B16)], axis=1
    )

    def attn_weights(core):
        cols = pl.ds(pl.multiple_of(core * 256, 256), half)
        product = rows_product(norm1[...], gqkv[:, cols]).astype(B16)
        product = product.reshape(members, 4, small, half)
        for member in range(members):
            g_attn[core, :, member * small : (member + 1) * small, :] = product[member]

    attn_weights(links.other)
    for k in range(4):
        sum_attn.hand(k)
    attn_weights(links.core)
    for k in range(3):
        sum_attn.merge(k)
        sum_attn.four.sends[k].start()
    gather_mlp.forward()

    def norm1_block(index, carry):
        members_of = pair(index)
        ats = [member_rows(member) for member in members_of]
        back = transposed_product(
            both_rows(gqkv, ats)[:, : 3 * span], w_all[...].reshape(width, width)[:, : 3 * span]
        )
        rowsum[0:1, :] += jnp.sum(back * both_rows(normed1, ats), axis=0, keepdims=True)
        rowsum[1:2, :] += jnp.sum(back, axis=0, keepdims=True)
        back_half = back.astype(B16)
        for k in range(2):
            gn1[members_of[k]] = back_half[k * rows : (k + 1) * rows]

        @pl.when(index == 0)
        def _():
            ring_gn1.send_far()
            ring_gn1.ready[0].start()

        @pl.when(index == 1)
        def _():
            ring_gn1.ready[1].start()

        return carry

    lax.fori_loop(0, 2, norm1_block, 0)
    ring_gn1.send_summed()
    zsum[z] = rowsum[...]
    z_sums = [links.copy(zsum.at[z], zsum.at[z], links.to_z(s)) for s in (1, 3, 2)]
    for transfer in z_sums:
        transfer.start()
    sum_attn.merge(3)
    gather_mlp.hand_near()
    for transfer in z_sums:
        transfer.arrived()
    index = lax.broadcasted_iota(jnp.int32, rowsum.shape, 0)
    value = zsum[0] + zsum[1] + zsum[2] + zsum[3]
    value = jnp.where(index < 6, value, zsum[z])
    ssum[0] = value
    steps = [
        links.copy(ssum.at[k], bsum.at[k], device)
        for k, device in enumerate((links.to_core, links.to_x, links.to_y))
    ]
    steps[0].start()

    grad_norm1 = ring_gn1.total()
    _, normed, inv_std = layer_norm(x_all[z].astype(F32), one, zero_shift)
    input_grad[...] = gm_own[...] + norm_backward(grad_norm1, gain_one, normed, inv_std)

    steps[0].arrived()
    ssum[1] = ssum[0] + bsum[0]
    steps[1].start()
    total = sum_attn.four.total().astype(B16)
    h_attn[links.core, links.chip, span:, :] = total[span:]
    qkv_piece[...] = total[:span].reshape(members, small, half)
    own = pl.ds(pl.multiple_of(small * z, 16), small)
    h_attn[links.core, links.chip, own, :] = qkv_piece[z]
    for transfer in spread_qkv:
        transfer.start()
    steps[1].arrived()
    ssum[2] = ssum[1] + bsum[1]
    steps[2].start()
    for transfer in spread_qkv:
        transfer.arrived()
    gather_attn.start()
    steps[2].arrived()
    total = ssum[2] + bsum[2]
    mine = total[:, :span]
    for m in range(1, members):
        mine = jnp.where(
            chosen((z == m).astype(jnp.int32), mine.shape), total[:, m * span : (m + 1) * span], mine
        )
    sums[:6, :span] = mine[:6]
    sums[6:8, :] = total[6:8]
    gather_mlp.hand_far()
    gather_attn.forward()
    gather_attn.hand_near()
    gather_attn.hand_far()
    for transfer in (gather_attn.own_core, gather_attn.x_core, gather_attn.y_core, gather_attn.d_core):
        transfer.arrived()
    gather_mlp.own_core.arrived()
    gather_mlp.x_core.arrived()
    gather_mlp.y_core.arrived()
    gather_mlp.d_core.arrived()


def block_kernel(*refs):
    ids, x, cot, qkvw, fcw, projw = refs[:6]
    vectors = refs[6:14]
    outw, fcb = refs[14:16]
    outs = refs[16:21]
    lse, qm, kv, x_all, w_all, cot_all, fc_all, proj_all, vec_all, norm1, normed1 = refs[21:32]
    front = refs[32:39]
    a_all = refs[39]
    links = Links(*refs[-2:])
    attn_t = a_all.at[links.z]
    shared = (lse, qm, kv, x_all, w_all, cot_all, fc_all, proj_all, vec_all, norm1)
    arriving = forward_phase(
        links, ids, x, cot, qkvw, fcw, projw, *vectors, attn_t, *shared, normed1, *front
    )
    backward_phase(
        links, arriving, ids, attn_t, *shared, projw, outw, fcb, *outs, normed1, *refs[39:-2]
    )
    links.drain()


def block_call(ids, x, cot, qkvw, fcw, projw, *vectors):
    rows, width = x.shape
    members = 4
    span = qkvw.shape[0]
    group = members * rows
    block = group // 2
    heads = span // HEAD
    half = width // 2
    small = span // 4
    mlp_rows, attn_rows = 2 * span, span + small

    def shape(dims, dtype=B16):
        return jax.ShapeDtypeStruct(dims, dtype)

    def summed(rows_of, cols):
        return [
            VMEM((4, rows_of, cols), B16),
            VMEM((rows_of, cols), B16),
            VMEM((2, rows_of, cols), B16),
        ]

    def ring():
        return [
            VMEM((members, rows, width), B16),
            VMEM((rows, width), B16),
            VMEM((2, rows, width), B16),
        ]

    outs = (
        shape((rows, width), F32),
        shape((rows, width), F32),
        shape((2, 4, mlp_rows, half)),
        shape((2, 4, attn_rows, half)),
        shape((8, width), F32),
    )
    scratch = (
        [
            VMEM((8, group), F32),
            VMEM((heads, group, 4 * HEAD), B16),
            VMEM((2, 4, group, 2 * span), B16),
            VMEM((members, rows, width), B16),
            VMEM((members, span, width), B16),
            VMEM((members, rows, width), B16),
            VMEM((members, span, width), B16),
            VMEM((members, span, width), B16),
            VMEM((members, 16, 256), B16),
            VMEM((group, width), B16),
            VMEM((group, width), F32),
            VMEM((members, span, width), B16),
            VMEM((8, block), F32),
            VMEM((8, block), F32),
            VMEM((span, block), F32),
            VMEM((2, 8, block), F32),
            VMEM((2, 8, block), F32),
            VMEM((2, span, block), F32),
            VMEM((members, span, group), B16),
            VMEM((group, width), F32),
            VMEM((group, width), B16),
            VMEM((group, width), B16),
            VMEM((group, width), B16),
        ]
        + ring()
        + ring()
        + ring()
        + [
            VMEM((members, rows, width), B16),
            VMEM((rows, width), F32),
            VMEM((rows, width), F32),
            VMEM((2, 4, group, 2 * span), B16),
        ]
        + summed(group, 2 * span)
        + [VMEM((2, 4, mlp_rows, half), B16)]
        + summed(mlp_rows, half)
        + [VMEM((2, 4, attn_rows, half), B16)]
        + [VMEM((4, attn_rows, half), B16), VMEM((3, attn_rows, half), B16)]
        + [
            VMEM((members, small, half), B16),
            VMEM((members, small, half), B16),
            VMEM((heads, group, 4 * HEAD), B16),
            VMEM((8, group), F32),
            VMEM((2, span, block), F32),
            VMEM((group, 640), B16),
            VMEM((members, 8, width), F32),
            VMEM((3, 8, width), F32),
            VMEM((3, 8, width), F32),
            VMEM((8, width), F32),
            VMEM((members, rows, 4 * HEAD), B16),
            VMEM((members, rows, 4 * HEAD), B16),
            pltpu.SemaphoreType.DMA((176,)),
            pltpu.SemaphoreType.DMA((176,)),
        ]
    )
    args = (ids, x, cot, qkvw, fcw, projw) + vectors
    return pl.pallas_call(
        block_kernel,
        out_shape=outs,
        in_specs=[pl.BlockSpec(memory_space=SMEM)] + [pl.BlockSpec(memory_space=VMEM)] * (len(args) - 1),
        out_specs=(pl.BlockSpec(memory_space=VMEM),) * len(outs),
        scratch_shapes=scratch,
        compiler_params=pltpu.CompilerParams(
            collective_id=0, has_side_effects=True, vmem_limit_bytes=62 << 20
        ),
        name="block",
    )(*args)


def assemble_kernel(
    block_in, grad_in, h_mlp, h_attn, sums,
    block_out, grad_out, gain1, bias1, qkv, qbias, vbias, proj, pbias, gain2, bias2, fc, fbias, out, obias,
):
    small, width = proj.shape
    span = 4 * small
    half = width // 2
    block_out[...] = block_in[...]
    grad_out[...] = grad_in[...]
    for ref, index in ((gain1, 0), (bias1, 1), (pbias, 2), (gain2, 3), (bias2, 4), (obias, 5)):
        ref[...] = sums[index : index + 1, :span].reshape(span)
    qbias[...] = sums[6:7, :span].reshape(span)
    vbias[...] = sums[6:7, span : 2 * span].reshape(span)
    fbias[...] = sums[7:8, :].reshape(width)
    for core in range(2):
        cols = slice(core * half, (core + 1) * half)
        out[:, cols] = h_mlp[core, 0, :span, :].astype(F32)
        proj[:, cols] = h_attn[core, 0, span:, :].astype(F32)
        for member in range(4):
            at = span + member * small
            first = member * width + core * half
            fc[:, first : first + half] = h_mlp[core, 0, at : at + small, :].astype(F32)
    pieces = []
    for member in range(4):
        at = slice(member * small, (member + 1) * small)
        pieces.append(
            jnp.concatenate(
                [h_attn[0, 0, at, :], h_attn[1, 0, at, 128 : 3 * span - 256]], axis=1
            ).astype(F32)
        )
    qkv[...] = jnp.concatenate(
        [piece[:, t * span : (t + 1) * span] for t in range(3) for piece in pieces], axis=1
    )


def assemble(block_in, grad_in, h_mlp, h_attn, sums):
    width = block_in.shape[1]
    span = width // 4

    def shape(*dims):
        return jax.ShapeDtypeStruct(dims, F32)

    narrow = shape(span)
    outs = (
        shape(*block_in.shape), shape(*block_in.shape), narrow, narrow, shape(span, 3 * width), narrow, narrow,
        shape(span, width), narrow, narrow, narrow, shape(span, 4 * width), shape(width), shape(width, width),
        narrow,
    )
    def in_rows(array):
        if len(array.shape) == 1:
            return pl.BlockSpec(array.shape, lambda chip: (0,))
        return pl.BlockSpec((array.shape[0] // 4, array.shape[1]), lambda chip: (chip, 0))

    def of_chip(array):
        return pl.BlockSpec((2, 1) + array.shape[2:], lambda chip: (0, chip, 0, 0))

    return pl.pallas_call(
        assemble_kernel,
        out_shape=outs,
        grid=(4,),
        in_specs=[
            in_rows(block_in),
            in_rows(grad_in),
            of_chip(h_mlp),
            of_chip(h_attn),
            pl.BlockSpec(sums.shape, lambda chip: (0, 0)),
        ],
        out_specs=tuple(in_rows(array) for array in outs),
        compiler_params=pltpu.CompilerParams(vmem_limit_bytes=62 << 20),
        name="assemble",
    )(block_in, grad_in, h_mlp, h_attn, sums)


def head_shards(
    block_input,
    positions,
    norm1_gain,
    norm1_bias,
    qkv_weight,
    query_bias,
    value_bias,
    proj_weight,
    proj_bias,
    norm2_gain,
    norm2_bias,
    fc_weight,
    fc_bias,
    out_weight,
    out_bias,
    cotangent,
):
    rows, width = block_input.shape
    ids = positions.reshape(-1, 2 * rows)[:, 0] // (2 * rows)
    results = block_call(
        ids, block_input, cotangent, qkv_weight, fc_weight, proj_weight, norm1_gain, norm1_bias, proj_bias,
        norm2_gain, norm2_bias, out_bias, query_bias, value_bias, out_weight, fc_bias,
    )
    return assemble(*results)


def solution(mesh):
    sharded = P(("ctx", "fsdp"), None)
    rows, vector = P("fsdp", None), P("fsdp")
    in_specs = (
        sharded, P(), vector, vector, rows, vector, vector, rows, vector, vector, vector, rows, vector, rows,
        vector, sharded,
    )
    out_specs = (
        sharded, sharded, vector, vector, rows, vector, vector, rows, vector, vector, vector, rows, vector, rows,
        vector,
    )
    body = head_shards if dict(mesh.shape) == {"ctx": 8, "fsdp": 4} else shards
    return jax.shard_map(body, mesh=mesh, in_specs=in_specs, out_specs=out_specs, check_vma=False)
```
